32 devices in a mesh: groups: 2 (over y), store: 4 (over z), mp: 4 (over x, core).
Axes of the slice: x: 2, y: 2, z: 4, core: 2. Of those that a mesh axis runs over, the one named last changes fastest.
Arguments:
- hidden: bfloat16 [8, 128, 4096], P(('groups', 'store')), parts along dimension 0, may hold values from -6 to 6
- query_weight: bfloat16 [4096, 8192], P('store', 'mp'), may hold values from -0.09375 to 0.09375
- keyvalue_weight: bfloat16 [4096, 2048], P('store', 'mp'), may hold values from -0.09375 to 0.09375
- block_store: bfloat16 [128, 1024, 2048], P('groups', 'store', 'mp'), parts along dimension 0, may hold values from -256 to 256
- block_ids: int32 [8, 4], P('groups'), parts along dimension 0, may hold values from 0 to 63, as said below
- offsets: int32 [8, 4], P('groups'), parts along dimension 0, may hold values from 0 to 3135, as said below
- served: int32 [8], P('groups'), parts along dimension 0, may hold values from 0 to 3, each once
Outputs:
- attended: bfloat16 [8, 128, 8192], P(('groups', 'store'), None, 'mp'), parts along dimension 0
The draws below stay inside these ranges and needn't reach their ends.
There are 2 independent parts, one for each index of `groups`. The reference program is written for one: setup_inputs(seed, part) draws one part's arguments, and reference() takes and returns one part's arrays. A program takes and returns all parts, laid end to end along the dimension named above; an argument that names none is the same for every part. Nothing has to cross between parts.
Inputs may be any that keep to these rules, and one draw needn't show every extreme that they name: `block_ids`: the 4 block ids of one request differ. `offsets`: block c of a request starts at c * 1024 plus 0 to 63.
All inputs are finite; a program needn't handle non-finite values.
Results may differ from the reference program's by a relative error of at most 0.004.
The reference program's roundings to bfloat16 on the way count: a program that leaves them out, or rounds other values in their place, can miss the bound.
Values may be sent and summed in bfloat16 or wider, within the bound.
A program may use at most 128 MiB of HBM per device.

```python
import math
import jax
import jax.numpy as jnp
from jax import lax

D = 4096
QH = 64
KVH = 8
HD = 128
NCH = 4
L = 1024
GAP = 64
NEW = 128
BLOCKS = 64
REQUESTS = 4


def draw_block_store(key, part):
    base = jax.random.normal(key, (BLOCKS, L, KVH, 2, HD), jnp.float32)
    base = jnp.clip(base, -5.0, 5.0)
    return base.reshape(BLOCKS, L, KVH * 2 * HD).astype(jnp.bfloat16)


def draw_block_ids(key, part):

    def one_request(number):
        return jax.random.permutation(jax.random.fold_in(key, number), BLOCKS)[:NCH]
    return jax.vmap(one_request)(jnp.arange(REQUESTS)).astype(jnp.int32)


def draw_offsets(key, part):
    jitter = jax.random.randint(key, (REQUESTS, NCH), 0, GAP)
    return (jnp.arange(NCH, dtype=jnp.int32)[None, :] * L + jitter).astype(jnp.int32)


def levels(own_key, shape, cuts, smallest, high):
    def one(dim, blocks):
        steps = jax.random.uniform(jax.random.fold_in(jax.random.fold_in(own_key, 6), dim), (blocks,), jnp.float32, smallest / len(cuts), high / len(cuts))
        return jnp.repeat(jnp.exp(steps), shape[dim] // blocks).reshape((-1,) + (1,) * (len(shape) - dim - 1))

    factor_of = one(*cuts[0])
    for cut in cuts[1:]:
        factor_of = factor_of * one(*cut)
    return factor_of


def gaussian(rng, extent, spread, reach, split=(), held_as=jnp.bfloat16):
    factor_of = levels(rng, extent, split, -0.22, 0.18) if split else 1.0
    array = jax.random.normal(rng, extent, jnp.float32) * spread * factor_of
    return jnp.minimum(jnp.maximum(array, -reach), reach).astype(held_as)


def setup_inputs(seed: int = 0, part: int = 0) -> dict:
    seeds = jax.random.split(jax.random.key(seed), 8)
    own_keys = jax.random.split(jax.random.fold_in(seeds[7], part), 8)
    return {
        "hidden": gaussian(own_keys[0], (REQUESTS, NEW, D), 1.0, 6.0, ((0, 4),)),
        "query_weight": gaussian(seeds[1], (D, QH * HD), D ** -0.5, 0.09375, ((0, 4), (1, 4))),
        "keyvalue_weight": gaussian(seeds[2], (D, KVH * 2 * HD), D ** -0.5, 0.09375, ((0, 4), (1, 4))),
        "block_store": draw_block_store(jax.random.fold_in(jax.random.fold_in(seeds[7], part), 71), part),
        "block_ids": draw_block_ids(jax.random.fold_in(jax.random.fold_in(seeds[7], part), 71), part),
        "offsets": draw_offsets(jax.random.fold_in(jax.random.fold_in(seeds[7], part), 71), part),
        "served": jax.random.permutation(own_keys[6], REQUESTS).astype(jnp.int32),
    }


def rotary_tables(positions, head_size):
    half_size = head_size // 2
    freq_index = jnp.arange(half_size, dtype=jnp.float32)
    inverse = jnp.exp(freq_index * (-2.0 * math.log(500000.0) / head_size))
    period = jnp.floor(2.0 * math.pi / inverse + 0.5)
    position_f = positions.astype(jnp.float32)[:, None]
    angles = jnp.mod(position_f, period[None, :]) / period[None, :] * (2.0 * math.pi)
    return (jnp.cos(angles), jnp.sin(angles))

def rotate(values, cosine, sine_values):
    half_size = values.shape[-1] // 2
    first_half = values[..., :half_size]
    second_half = values[..., half_size:]
    cos_b = cosine[:, None, :]
    sin_b = sine_values[:, None, :]
    return jnp.concatenate([first_half * cos_b - second_half * sin_b, second_half * cos_b + first_half * sin_b], axis=-1)

def attend(queries, cached_keys, cached_values, new_keys, new_values):
    row_count = queries.shape[0]
    head_count = queries.shape[1]
    sharing = head_count // cached_keys.shape[1]
    scaling = 1.0 / math.sqrt(queries.shape[2])
    causal = jnp.arange(row_count)[:, None] >= jnp.arange(row_count)[None, :]

    def one_head(head_index):
        kv_index = head_index // sharing
        q_one = lax.dynamic_index_in_dim(queries, head_index, 1, keepdims=False)
        k_old = lax.dynamic_index_in_dim(cached_keys, kv_index, 1, keepdims=False)
        v_old = lax.dynamic_index_in_dim(cached_values, kv_index, 1, keepdims=False)
        k_new = lax.dynamic_index_in_dim(new_keys, kv_index, 1, keepdims=False)
        v_new = lax.dynamic_index_in_dim(new_values, kv_index, 1, keepdims=False)
        past_scores = jnp.dot(q_one, k_old.T, preferred_element_type=jnp.float32) * scaling
        own_scores = jnp.dot(q_one, k_new.T, preferred_element_type=jnp.float32) * scaling
        own_scores = jnp.where(causal, own_scores, -jnp.inf)
        row_top = jnp.maximum(lax.optimization_barrier(jnp.max(past_scores, axis=1)), lax.optimization_barrier(jnp.max(own_scores, axis=1)))[:, None]
        w_old = jnp.exp(past_scores - row_top)
        w_new = jnp.exp(own_scores - row_top)
        denominator = lax.optimization_barrier(jnp.sum(w_old, axis=1)) + lax.optimization_barrier(jnp.sum(w_new, axis=1))
        mixed = jnp.dot(w_old.astype(jnp.bfloat16), v_old, preferred_element_type=jnp.float32)
        mixed = mixed + jnp.dot(w_new.astype(jnp.bfloat16), v_new, preferred_element_type=jnp.float32)
        return (mixed / denominator[:, None]).astype(jnp.bfloat16)
    per_head = lax.map(one_head, jnp.arange(head_count, dtype=jnp.int32))
    return jnp.transpose(per_head, (1, 0, 2)).reshape(row_count, head_count * queries.shape[2])

def reference(hidden, query_weight, keyvalue_weight, block_store, block_ids, offsets, served):

    def one_slot(slot_index):
        tokens = hidden[slot_index]
        request = served[slot_index]
        queries = jnp.dot(tokens, query_weight, preferred_element_type=jnp.float32).reshape(NEW, QH, HD)
        fresh_proj = jnp.dot(tokens, keyvalue_weight, preferred_element_type=jnp.float32).reshape(NEW, KVH, 2, HD)
        query_pos = NCH * L + GAP + jnp.arange(NEW, dtype=jnp.int32)
        cos_query, sin_query = rotary_tables(query_pos, HD)
        queries = rotate(queries, cos_query, sin_query).astype(jnp.bfloat16)
        new_keys = rotate(fresh_proj[:, :, 0, :], cos_query, sin_query).astype(jnp.bfloat16)
        new_values = fresh_proj[:, :, 1, :].astype(jnp.bfloat16)
        wanted = block_ids[request]
        page_data = jnp.take(block_store, wanted, axis=0).reshape(NCH * L, KVH, 2, HD)
        key_pos = (offsets[request][:, None] + jnp.arange(L, dtype=jnp.int32)[None, :]).reshape(NCH * L)
        cos_key, sin_key = rotary_tables(key_pos, HD)
        cached_keys = rotate(page_data[:, :, 0, :].astype(jnp.float32), cos_key, sin_key).astype(jnp.bfloat16)
        cached_values = page_data[:, :, 1, :]
        return attend(queries, cached_keys, cached_values, new_keys, new_values)
    return lax.map(one_slot, jnp.arange(REQUESTS, dtype=jnp.int32))
```

```python
import functools
import math

import jax
import jax.numpy as jnp
import numpy as np
from jax import lax
from jax.experimental import pallas as pl
from jax.experimental.pallas import tpu as pltpu
from jax.sharding import PartitionSpec as P

HD = 128
HALF = HD // 2
NCH = 4
L = 1024
GAP = 64
BASE = 500000.0


def periods():
    inverse = np.exp(
        np.arange(HALF, dtype=np.float32) * np.float32(-2.0 * math.log(BASE) / HD)
    ).astype(np.float32)
    return np.floor(np.float32(2.0 * math.pi) / inverse + np.float32(0.5)).astype(np.float64)


def signed_tables(positions):
    period = periods()[None, :]
    angles = np.mod(np.asarray(positions, np.float64)[:, None], period) / period * (2.0 * math.pi)
    cos, sin = np.cos(angles), np.sin(angles)
    return (
        np.concatenate([cos, cos], axis=1).astype(np.float32),
        np.concatenate([-sin, sin], axis=1).astype(np.float32),
    )


def gather_body(
    slots, ids_ref, served_ref, offsets_ref, store_ref, period_ref, out_ref, oc_ref, os_ref, sems
):
    copies = []
    for s in range(slots):
        request = served_ref[s]
        for c in range(NCH):
            copy = pltpu.make_async_copy(
                store_ref.at[ids_ref[request, c]], out_ref.at[s, c], sems.at[s, c]
            )
            copy.start()
            copies.append(copy)
    request = served_ref[lax.axis_index("store")]
    row = lax.broadcasted_iota(jnp.int32, oc_ref.shape, 0)
    lane = lax.broadcasted_iota(jnp.int32, oc_ref.shape, 1)
    first = jnp.zeros(oc_ref.shape, jnp.float32)
    for c in range(NCH):
        first = jnp.where(row == c, offsets_ref[request, c].astype(jnp.float32), first)
    period = period_ref[...]
    turns = (first - jnp.floor(first / period) * period) / period
    angles = turns * (2.0 * math.pi)
    sin = jnp.sin(angles)
    oc_ref[...] = jnp.cos(angles)
    os_ref[...] = jnp.where(lane < HALF, -sin, sin)
    for copy in copies:
        copy.wait()


def gather_blocks(block_ids, served, offsets, block_store):
    slots = served.shape[0]
    period = np.broadcast_to(np.tile(periods(), 2).astype(np.float32), (8, HD))
    table = jax.ShapeDtypeStruct((8, HD), jnp.float32)
    vmem = pl.BlockSpec(memory_space=pltpu.VMEM)
    return pl.pallas_call(
        functools.partial(gather_body, slots),
        grid_spec=pltpu.PrefetchScalarGridSpec(
            num_scalar_prefetch=3,
            grid=(),
            in_specs=[pl.BlockSpec(memory_space=pl.ANY), vmem],
            out_specs=[vmem, vmem, vmem],
            scratch_shapes=[pltpu.SemaphoreType.DMA((slots, NCH))],
        ),
        out_shape=[
            jax.ShapeDtypeStruct((slots, NCH) + block_store.shape[1:], block_store.dtype), table, table,
        ],
        compiler_params=pltpu.CompilerParams(vmem_limit_bytes=56 << 20),
        name="gather_blocks",
    )(block_ids, served, offsets, block_store, period)


def turn(x, cos, sin):
    return x * cos + pltpu.roll(x, HALF, 1) * sin


MESH = pl.DeviceIdType.MESH


def serve_body(
    slots, peers, heads, kv_heads,
    hidden_ref, wq_hbm, wkv_hbm, sending_ref, qc_ref, qs_ref, tc_ref, ts_ref, oc_ref, os_ref,
    out_ref,
    tokens, wq, wkv, sums, arrived, blocks, keys, fresh, queries, scores, weights, totals, mixed,
    load_sem, own_sem, a_send, a_recv, b_send, b_recv, k_send, k_recv, p_send, p_recv,
):
    me = lax.axis_index("store")
    part = lax.axis_index("mp")
    rows = hidden_ref.shape[1]
    depth = tokens.shape[2]
    chunks, _, _, width = sums.shape
    share = blocks.shape[2]
    sharing = heads // kv_heads
    past = NCH * L
    strip = rows // peers

    loads = [
        pltpu.make_async_copy(wq_hbm, wq, load_sem.at[0]),
        pltpu.make_async_copy(wkv_hbm, wkv, load_sem.at[1]),
    ]
    for load in loads:
        load.start()
    own_copy = pltpu.make_async_copy(sending_ref.at[me], blocks.at[me], own_sem.at[0])
    own_copy.start()

    barrier = pltpu.get_barrier_semaphore()
    for k in range(1, slots):
        pl.semaphore_signal(
            barrier, inc=1, device_id={"store": lax.rem(me + k, slots)}, device_id_type=MESH
        )
    for k in range(1, peers):
        pl.semaphore_signal(
            barrier, inc=1, device_id={"mp": lax.rem(part + k, peers)}, device_id_type=MESH
        )
    pl.semaphore_wait(barrier, slots + peers - 2)

    def strip_copy(k):
        to = lax.rem(me + k, slots)
        mine = pl.ds(pl.multiple_of(part * strip, strip), strip)
        return pltpu.make_async_remote_copy(
            src_ref=hidden_ref.at[0, mine, pl.ds(pl.multiple_of(to * depth, depth), depth)],
            dst_ref=tokens.at[me, mine, :],
            send_sem=a_send.at[k],
            recv_sem=a_recv.at[k],
            device_id={"store": to},
            device_id_type=MESH,
        )

    def spread_copy(k, d):
        source = lax.rem(me - k + slots, slots)
        mine = pl.ds(pl.multiple_of(part * strip, strip), strip)
        return pltpu.make_async_remote_copy(
            src_ref=tokens.at[source, mine, :],
            dst_ref=tokens.at[source, mine, :],
            send_sem=b_send.at[k, d],
            recv_sem=b_recv.at[k, d],
            device_id={"mp": lax.rem(part + d, peers)},
            device_id_type=MESH,
        )

    def block_copy(k, g, v):
        to = lax.rem(me + k, slots)
        cols = pl.ds(pl.multiple_of((2 * g + v) * HD, HD), HD)
        return pltpu.make_async_remote_copy(
            src_ref=sending_ref.at[to, :, :, cols],
            dst_ref=blocks.at[me, :, :, cols],
            send_sem=k_send.at[k, 2 * g + v],
            recv_sem=k_recv.at[k, 2 * g + v],
            device_id={"store": to},
            device_id_type=MESH,
        )

    low = me < slots // 2

    def other(j):
        far_first = jnp.where(low, slots - 1 - me, me)
        near = jnp.where(low, me + 1 + j, me - 1 - j)
        rest = jnp.where(low, slots - 2 - j, j + 1)
        return jnp.where(j < far_first, near, rest)

    def other_shift(j):
        return lax.rem(me - other(j) + slots, slots)

    def send_blocks(v, up):
        def one(j):
            d = slots - 1 - j
            fits = (me + d < slots) if up else (me >= d)

            @pl.when(fits)
            def _():
                for g in range(kv_heads):
                    block_copy(d if up else slots - d, g, v).start()

        each(slots - 1, one)

    def sum_copy(s, q, up):
        index = s + 1 if up else s
        return pltpu.make_async_remote_copy(
            src_ref=sums.at[q, s],
            dst_ref=arrived.at[index, q],
            send_sem=p_send.at[index, q],
            recv_sem=p_recv.at[index, q],
            device_id={"store": lax.rem(me + 1, slots) if up else lax.rem(me + slots - 1, slots)},
            device_id_type=MESH,
        )

    def each(count, body, first=0):
        def step(i, carry):
            body(i)
            return carry

        lax.fori_loop(first, count, step, 0)

    each(slots, lambda k: strip_copy(k).start(), 1)
    send_blocks(0, True)
    send_blocks(0, False)

    @pl.when(low)
    def _():
        send_blocks(1, False)

    @pl.when(jnp.logical_not(low))
    def _():
        send_blocks(1, True)

    tokens[me] = hidden_ref[0, :, pl.ds(pl.multiple_of(me * depth, depth), depth)]

    def spread(k):
        strip_copy(k).wait_recv()
        for d in range(1, peers):
            spread_copy(k, d).start()

    each(slots, spread, 1)

    def spread_wait(k):
        for d in range(1, peers):
            spread_copy(k, d).wait_recv()

    each(slots, spread_wait, 1)
    for load in loads:
        load.wait()

    group = 4 if slots % 4 == 0 else 1

    def project(q, panel):
        def some(i):
            t = tokens[pl.ds(i * group, group)].reshape(group * rows, depth)
            sums[q, pl.ds(i * group, group)] = jnp.dot(
                t, panel, preferred_element_type=jnp.float32
            ).reshape(group, rows, width)

        each(slots // group, some)

    def relay_up(k, q):
        s = slots - 1 - k

        @pl.when(s > me)
        def _():
            @pl.when(me > 0)
            def _():
                sum_copy(s, q, True).wait_recv()
                sums[q, s] = sums[q, s] + arrived[s + 1, q]

            @pl.when((me > 0) | (k > 0))
            def _():
                sum_copy(s, q, True).start()

    def relay_down(k, q):
        @pl.when(k < me)
        def _():
            @pl.when(me < slots - 1)
            def _():
                sum_copy(k, q, False).wait_recv()
                sums[q, k] = sums[q, k] + arrived[k, q]

            @pl.when((me < slots - 1) | (k > 0))
            def _():
                sum_copy(k, q, False).start()

    for q in range(chunks):
        if q < chunks - 1:
            project(q, wq[:, q * width : (q + 1) * width])
        else:
            project(q, wkv[...])

        @pl.when(me == 0)
        def _():
            sum_copy(slots - 1, q, True).start()

        @pl.when(me == slots - 1)
        def _():
            sum_copy(0, q, False).start()

    steps = (slots - 1) * chunks

    def relay(i):
        def at(i, move):
            @pl.when((i >= 0) & (i < steps))
            def _():
                move(i // chunks, i % chunks)

        @pl.when(low)
        def _():
            at(i, relay_up)
            at(i - chunks, relay_down)

        @pl.when(jnp.logical_not(low))
        def _():
            at(i, relay_down)
            at(i - chunks, relay_up)

    each(steps + chunks, relay)

    @pl.when(low)
    def _():
        send_blocks(1, True)

    @pl.when(jnp.logical_not(low))
    def _():
        send_blocks(1, False)

    def drain_sums(i):
        k, q = i // chunks, i % chunks

        @pl.when(slots - 1 - k > me)
        def _():
            sum_copy(slots - 1 - k, q, True).wait_send()

        @pl.when(k < me)
        def _():
            sum_copy(k, q, False).wait_send()

    def rotate_share(source):
        at_t = pl.multiple_of(source * share, share)
        tc, ts = tc_ref[pl.ds(at_t, share), :], ts_ref[pl.ds(at_t, share), :]

        def one(c):
            at_k = pl.multiple_of((source * NCH + c) * share, share)
            oc, os = oc_ref[pl.ds(c, 1), :], os_ref[pl.ds(c, 1), :]
            cos = tc * oc - ts * os
            sin = ts * oc + tc * os
            for g in range(kv_heads):
                at = g * 2 * HD
                x = blocks[source, c, :, at : at + HD].astype(jnp.float32)
                keys[g, pl.ds(at_k, share), :] = turn(x, cos, sin).astype(jnp.bfloat16)

        each(NCH, one)

    own_copy.wait()
    rotate_share(me)

    def take(j):
        for g in range(kv_heads):
            block_copy(other_shift(j), g, 0).wait_recv()
        rotate_share(other(j))

    each(slots - 1, take)

    def settle(q):
        @pl.when(me > 0)
        def _():
            sum_copy(me, q, True).wait_recv()
            sums[q, me] = sums[q, me] + arrived[me + 1, q]

        @pl.when(me < slots - 1)
        def _():
            sum_copy(me, q, False).wait_recv()
            sums[q, me] = sums[q, me] + arrived[me, q]

    each(chunks, settle)

    qc, qs = qc_ref[...], qs_ref[...]
    for g in range(kv_heads):
        at = g * 2 * HD
        keys[g, past:, :] = turn(sums[chunks - 1, me, :, at : at + HD], qc, qs).astype(jnp.bfloat16)
        fresh[g] = sums[chunks - 1, me, :, at + HD : at + 2 * HD].astype(jnp.bfloat16)
    for h in range(heads):
        q, at = divmod(h * HD, width)
        queries[h * rows : (h + 1) * rows, :] = turn(
            sums[q, me, :, at : at + HD], qc, qs
        ).astype(jnp.bfloat16)

    block = 2 * rows
    span = 512
    factor = math.log2(math.e) / math.sqrt(HD)
    lower = lax.broadcasted_iota(jnp.int32, (block, rows), 0) % rows >= lax.broadcasted_iota(
        jnp.int32, (block, rows), 1
    )
    contract = (((1,), (1,)), ((), ()))

    def weigh(b):
        g = (b * 2) // sharing
        at = pl.ds(pl.multiple_of(b * block, block), block)
        q = queries[at, :]
        own = lax.dot_general(q, keys[g, past:, :], contract, preferred_element_type=jnp.float32)
        own = jnp.where(lower, own, -jnp.inf)
        top = own
        for j in range(past // span):
            s = lax.dot_general(
                q, keys[g, j * span : (j + 1) * span, :], contract,
                preferred_element_type=jnp.float32,
            )
            scores[:, j * span : (j + 1) * span] = s
            for k in range(span // HD):
                top = jnp.maximum(top, s[:, k * HD : (k + 1) * HD])
        top = jnp.max(top, axis=1, keepdims=True)
        w = jnp.exp2((own - top) * factor)
        total = w
        weights[at, past:] = w.astype(jnp.bfloat16)
        for j in range(past // span):
            w = jnp.exp2((scores[:, j * span : (j + 1) * span] - top) * factor)
            for k in range(span // HD):
                total = total + w[:, k * HD : (k + 1) * HD]
            weights[at, j * span : (j + 1) * span] = w.astype(jnp.bfloat16)
        totals[at, :] = total

    each(heads // 2, weigh)

    stack = sharing * rows
    some = NCH * share

    def mix(source, g, first):
        cols = pl.ds(pl.multiple_of(source * some, some), some)
        at = slice(g * stack, (g + 1) * stack)
        v = blocks[source, :, :, (2 * g + 1) * HD : (2 * g + 2) * HD].reshape(some, HD)
        term = jnp.dot(weights[at, cols], v, preferred_element_type=jnp.float32)
        if first:
            mixed[at, :] = term + jnp.dot(
                weights[at, past:], fresh[g], preferred_element_type=jnp.float32
            )
        else:
            mixed[at, :] = mixed[at, :] + term

    for g in range(kv_heads):
        mix(me, g, True)

    def take_values(j):
        for g in range(kv_heads):
            block_copy(other_shift(j), g, 1).wait_recv()
            mix(other(j), g, False)

    each(slots - 1, take_values)

    def finish(h):
        at = pl.ds(pl.multiple_of(h * rows, rows), rows)
        done = mixed[at, :] / jnp.sum(totals[at, :], axis=1, keepdims=True)
        out_ref[0, :, pl.ds(pl.multiple_of(h * HD, HD), HD)] = done.astype(out_ref.dtype)

    each(heads, finish)

    def drain(k):
        strip_copy(k).wait_send()
        for d in range(1, peers):
            spread_copy(k, d).wait_send()

    each(slots, drain, 1)

    def drain_blocks(k):
        for i in range(2 * kv_heads):
            block_copy(k, i // 2, i % 2).wait_send()

    each(slots, drain_blocks, 1)
    each(steps, drain_sums)


def per_device(hidden, query_weight, keyvalue_weight, block_store, block_ids, offsets, served):
    slots = lax.axis_size("store")
    peers = lax.axis_size("mp")
    rows, model = hidden.shape[1:]
    share, kv_cols = block_store.shape[1:]
    q_cols = query_weight.shape[1]
    heads = q_cols // HD
    kv_heads = kv_cols // (2 * HD)
    chunks = q_cols // kv_cols + 1
    depth = model // slots
    past = NCH * L
    sending, oc, os = gather_blocks(block_ids, served, offsets, block_store)
    qc, qs = signed_tables(past + GAP + np.arange(rows))
    tc, ts = signed_tables(np.arange(L))
    vmem = pl.BlockSpec(memory_space=pltpu.VMEM)
    hbm = pl.BlockSpec(memory_space=pl.ANY)
    dma = pltpu.SemaphoreType.DMA
    return pl.pallas_call(
        functools.partial(serve_body, slots, peers, heads, kv_heads),
        out_shape=jax.ShapeDtypeStruct((1, rows, q_cols), jnp.bfloat16),
        in_specs=[vmem, hbm, hbm, hbm] + [vmem] * 6,
        out_specs=vmem,
        scratch_shapes=[
            pltpu.VMEM((slots, rows, depth), jnp.bfloat16),
            pltpu.VMEM(query_weight.shape, jnp.bfloat16),
            pltpu.VMEM(keyvalue_weight.shape, jnp.bfloat16),
            pltpu.VMEM((chunks, slots, rows, kv_cols), jnp.float32),
            pltpu.VMEM((slots + 1, chunks, rows, kv_cols), jnp.float32),
            pltpu.VMEM((slots, NCH, share, kv_cols), jnp.bfloat16),
            pltpu.VMEM((kv_heads, past + rows, HD), jnp.bfloat16),
            pltpu.VMEM((kv_heads, rows, HD), jnp.bfloat16),
            pltpu.VMEM((heads * rows, HD), jnp.bfloat16),
            pltpu.VMEM((2 * rows, past), jnp.float32),
            pltpu.VMEM((heads * rows, past + rows), jnp.bfloat16),
            pltpu.VMEM((heads * rows, HD), jnp.float32),
            pltpu.VMEM((heads * rows, HD), jnp.float32),
            dma((2,)),
            dma((1,)),
            dma((slots,)),
            dma((slots,)),
            dma((slots, peers)),
            dma((slots, peers)),
            dma((slots, 2 * kv_heads)),
            dma((slots, 2 * kv_heads)),
            dma((slots + 1, chunks)),
            dma((slots + 1, chunks)),
        ],
        compiler_params=pltpu.CompilerParams(
            vmem_limit_bytes=63 << 20, collective_id=0, has_side_effects=True
        ),
        name="serve",
    )(hidden, query_weight, keyvalue_weight, sending, qc, qs, tc, ts, oc, os)


def solution(mesh):
    in_specs = (
        P(("groups", "store"), None, None),
        P("store", "mp"),
        P("store", "mp"),
        P("groups", "store", "mp"),
        P("groups", None),
        P("groups", None),
        P("groups"),
    )
    out_specs = P(("groups", "store"), None, "mp")
    return jax.shard_map(
        per_device, mesh=mesh, in_specs=in_specs, out_specs=out_specs, check_vma=False
    )
```

```python
import functools
import math

import jax
import jax.numpy as jnp
import numpy as np
from jax import lax
from jax.experimental import pallas as pl
from jax.experimental.pallas import tpu as pltpu
from jax.sharding import PartitionSpec as P

HD = 128
HALF = HD // 2
NCH = 4
L = 1024
GAP = 64
BASE = 500000.0


def periods():
    inverse = np.exp(
        np.arange(HALF, dtype=np.float32) * np.float32(-2.0 * math.log(BASE) / HD)
    ).astype(np.float32)
    return np.floor(np.float32(2.0 * math.pi) / inverse + np.float32(0.5)).astype(np.float64)


def signed_tables(positions):
    period = periods()[None, :]
    angles = np.mod(np.asarray(positions, np.float64)[:, None], period) / period * (2.0 * math.pi)
    cos, sin = np.cos(angles), np.sin(angles)
    return (
        np.concatenate([cos, cos], axis=1).astype(np.float32),
        np.concatenate([-sin, sin], axis=1).astype(np.float32),
    )


def gather_body(
    slots, ids_ref, served_ref, offsets_ref, store_ref, period_ref, out_ref, oc_ref, os_ref, sems
):
    copies = []
    for s in range(slots):
        request = served_ref[s]
        for c in range(NCH):
            copy = pltpu.make_async_copy(
                store_ref.at[ids_ref[request, c]], out_ref.at[s, c], sems.at[s, c]
            )
            copy.start()
            copies.append(copy)
    request = served_ref[lax.axis_index("store")]
    row = lax.broadcasted_iota(jnp.int32, oc_ref.shape, 0)
    lane = lax.broadcasted_iota(jnp.int32, oc_ref.shape, 1)
    first = jnp.zeros(oc_ref.shape, jnp.float32)
    for c in range(NCH):
        first = jnp.where(row == c, offsets_ref[request, c].astype(jnp.float32), first)
    period = period_ref[...]
    turns = (first - jnp.floor(first / period) * period) / period
    angles = turns * (2.0 * math.pi)
    sin = jnp.sin(angles)
    oc_ref[...] = jnp.cos(angles)
    os_ref[...] = jnp.where(lane < HALF, -sin, sin)
    for copy in copies:
        copy.wait()


def gather_blocks(block_ids, served, offsets, block_store):
    slots = served.shape[0]
    period = np.broadcast_to(np.tile(periods(), 2).astype(np.float32), (8, HD))
    table = jax.ShapeDtypeStruct((8, HD), jnp.float32)
    vmem = pl.BlockSpec(memory_space=pltpu.VMEM)
    return pl.pallas_call(
        functools.partial(gather_body, slots),
        grid_spec=pltpu.PrefetchScalarGridSpec(
            num_scalar_prefetch=3,
            grid=(),
            in_specs=[pl.BlockSpec(memory_space=pl.ANY), vmem],
            out_specs=[vmem, vmem, vmem],
            scratch_shapes=[pltpu.SemaphoreType.DMA((slots, NCH))],
        ),
        out_shape=[
            jax.ShapeDtypeStruct((slots, NCH) + block_store.shape[1:], block_store.dtype), table, table,
        ],
        compiler_params=pltpu.CompilerParams(vmem_limit_bytes=56 << 20),
        name="gather_blocks",
    )(block_ids, served, offsets, block_store, period)


def turn(x, cos, sin):
    return x * cos + pltpu.roll(x, HALF, 1) * sin


MESH = pl.DeviceIdType.MESH
STEPS = 8388000.0
LEAST = 1e-30


def encode(top, bottom, bound, code, first):
    half = top.shape[0]
    half_rows = code.shape[0] // 3
    factor = STEPS / jnp.maximum(bound, LEAST)
    top = jnp.round(top * factor).astype(jnp.int32)
    bottom = jnp.round(bottom * factor).astype(jnp.int32)
    code[pl.ds(first, half), :] = (top >> 8).astype(jnp.int16)
    code[pl.ds(half_rows + first, half), :] = (bottom >> 8).astype(jnp.int16)
    pair = (top & 255) | ((bottom & 255) << 8)
    code[pl.ds(2 * half_rows + first, half), :] = (pair - 32768).astype(jnp.int16)


def decode(bound, code, first, half):
    half_rows = code.shape[0] // 3
    pair = code[pl.ds(2 * half_rows + first, half), :].astype(jnp.int32) + 32768
    top = (code[pl.ds(first, half), :].astype(jnp.int32) << 8) | (pair & 255)
    bottom = (code[pl.ds(half_rows + first, half), :].astype(jnp.int32) << 8) | (pair >> 8)
    step = bound * (1.0 / STEPS)
    return top.astype(jnp.float32) * step, bottom.astype(jnp.float32) * step


def serve_body(
    slots, peers, heads, kv_heads,
    hidden_ref, wq_hbm, wkv_hbm, sending_ref, qc_ref, qs_ref, tc_ref, ts_ref, oc_ref, os_ref,
    out_ref,
    tokens, wq, wkv, sums, codes, own, bounds_in, bounds_out, blocks, keys, fresh, queries, scores, weights, totals, mixed,
    load_sem, own_sem, a_send, a_recv, b_send, b_recv, k_send, k_recv, p_send, p_recv, s_send, s_recv,
):
    me = lax.axis_index("store")
    part = lax.axis_index("mp")
    rows = hidden_ref.shape[1]
    depth = tokens.shape[2]
    chunks, _, _, width = sums.shape
    share = blocks.shape[2]
    sharing = heads // kv_heads
    past = NCH * L
    strip = rows // peers

    loads = [
        pltpu.make_async_copy(wq_hbm, wq, load_sem.at[0]),
        pltpu.make_async_copy(wkv_hbm, wkv, load_sem.at[1]),
    ]
    for load in loads:
        load.start()
    own_copy = pltpu.make_async_copy(sending_ref.at[me], blocks.at[me], own_sem.at[0])
    own_copy.start()

    barrier = pltpu.get_barrier_semaphore()
    for k in range(1, slots):
        pl.semaphore_signal(
            barrier, inc=1, device_id={"store": lax.rem(me + k, slots)}, device_id_type=MESH
        )
    for k in range(1, peers):
        pl.semaphore_signal(
            barrier, inc=1, device_id={"mp": lax.rem(part + k, peers)}, device_id_type=MESH
        )
    pl.semaphore_wait(barrier, slots + peers - 2)

    def strip_copy(k):
        to = lax.rem(me + k, slots)
        mine = pl.ds(pl.multiple_of(part * strip, strip), strip)
        return pltpu.make_async_remote_copy(
            src_ref=hidden_ref.at[0, mine, pl.ds(pl.multiple_of(to * depth, depth), depth)],
            dst_ref=tokens.at[me, mine, :],
            send_sem=a_send.at[k],
            recv_sem=a_recv.at[k],
            device_id={"store": to},
            device_id_type=MESH,
        )

    def spread_copy(k, d):
        source = lax.rem(me - k + slots, slots)
        mine = pl.ds(pl.multiple_of(part * strip, strip), strip)
        return pltpu.make_async_remote_copy(
            src_ref=tokens.at[source, mine, :],
            dst_ref=tokens.at[source, mine, :],
            send_sem=b_send.at[k, d],
            recv_sem=b_recv.at[k, d],
            device_id={"mp": lax.rem(part + d, peers)},
            device_id_type=MESH,
        )

    def block_copy(k, g, v):
        to = lax.rem(me + k, slots)
        cols = pl.ds(pl.multiple_of((2 * g + v) * HD, HD), HD)
        return pltpu.make_async_remote_copy(
            src_ref=sending_ref.at[to, :, :, cols],
            dst_ref=blocks.at[me, :, :, cols],
            send_sem=k_send.at[k, 2 * g + v],
            recv_sem=k_recv.at[k, 2 * g + v],
            device_id={"store": to},
            device_id_type=MESH,
        )

    low = me < slots // 2

    def other(j):
        far_first = jnp.where(low, slots - 1 - me, me)
        near = jnp.where(low, me + 1 + j, me - 1 - j)
        rest = jnp.where(low, slots - 2 - j, j + 1)
        return jnp.where(j < far_first, near, rest)

    def other_shift(j):
        return lax.rem(me - other(j) + slots, slots)

    def send_blocks(v, up):
        def one(j):
            d = slots - 1 - j
            fits = (me + d < slots) if up else (me >= d)

            @pl.when(fits)
            def _():
                for g in range(kv_heads):
                    block_copy(d if up else slots - d, g, v).start()

        each(slots - 1, one)

    def sum_copy(s, q, up):
        index = s + 1 if up else s
        return pltpu.make_async_remote_copy(
            src_ref=codes.at[index, q],
            dst_ref=codes.at[index, q],
            send_sem=p_send.at[index, q],
            recv_sem=p_recv.at[index, q],
            device_id={"store": lax.rem(me + 1, slots) if up else lax.rem(me + slots - 1, slots)},
            device_id_type=MESH,
        )

    def bound_copy(s, up):
        index = s + 1 if up else s
        return pltpu.make_async_remote_copy(
            src_ref=bounds_out.at[index],
            dst_ref=bounds_in.at[index],
            send_sem=s_send.at[index],
            recv_sem=s_recv.at[index],
            device_id={"store": lax.rem(me + 1, slots) if up else lax.rem(me + slots - 1, slots)},
            device_id_type=MESH,
        )

    strip_rows = 16

    def add_codes(q, s, index):
        code, bound = codes.at[index, q], bounds_in[index][:1, :1]

        def some(i):
            at = pl.multiple_of(i * strip_rows, strip_rows)
            top, bottom = decode(bound, code, at, strip_rows)
            lower = pl.ds(rows // 2 + at, strip_rows)
            at = pl.ds(at, strip_rows)
            sums[q, s, at] = sums[q, s, at] + top
            sums[q, s, lower] = sums[q, s, lower] + bottom

        each(rows // 2 // strip_rows, some)

    def make_codes(q, s, index):
        code, bound = codes.at[index, q], bounds_out[index][:1, :1]

        def some(i):
            at = pl.multiple_of(i * strip_rows, strip_rows)
            encode(
                sums[q, s, pl.ds(at, strip_rows)],
                sums[q, s, pl.ds(rows // 2 + at, strip_rows)],
                bound, code, at,
            )

        each(rows // 2 // strip_rows, some)

    def forward(q, s, up, begins):
        index = s + 1 if up else s

        @pl.when(q == 0)
        def _():
            @pl.when(begins)
            def _():
                bounds_out[index] = own[s]

            @pl.when(jnp.logical_not(begins))
            def _():
                bound_copy(s, up).wait_recv()
                bounds_out[index] = own[s] + bounds_in[index]

            bound_copy(s, up).start()

        @pl.when(jnp.logical_not(begins))
        def _():
            sum_copy(s, q, up).wait_recv()
            add_codes(q, s, index)

        make_codes(q, s, index)
        sum_copy(s, q, up).start()

    def each(count, body, first=0):
        def step(i, carry):
            body(i)
            return carry

        lax.fori_loop(first, count, step, 0)

    each(slots, lambda k: strip_copy(k).start(), 1)
    send_blocks(0, True)
    send_blocks(0, False)

    @pl.when(low)
    def _():
        send_blocks(1, False)

    @pl.when(jnp.logical_not(low))
    def _():
        send_blocks(1, True)

    tokens[me] = hidden_ref[0, :, pl.ds(pl.multiple_of(me * depth, depth), depth)]

    def spread(k):
        strip_copy(k).wait_recv()
        for d in range(1, peers):
            spread_copy(k, d).start()

    each(slots, spread, 1)

    def spread_wait(k):
        for d in range(1, peers):
            spread_copy(k, d).wait_recv()

    each(slots, spread_wait, 1)
    for load in loads:
        load.wait()

    group = 4 if slots % 4 == 0 else 1

    def project(q, panel):
        def some(i):
            t = tokens[pl.ds(i * group, group)].reshape(group * rows, depth)
            sums[q, pl.ds(i * group, group)] = jnp.dot(
                t, panel, preferred_element_type=jnp.float32
            ).reshape(group, rows, width)

        each(slots // group, some)

    def relay_up(k, q):
        @pl.when(slots - 1 - k > me)
        def _():
            forward(q, slots - 1 - k, True, me == 0)

    def relay_down(k, q):
        @pl.when(k < me)
        def _():
            forward(q, k, False, me == slots - 1)

    for q in range(chunks):
        if q < chunks - 1:
            project(q, wq[:, q * width : (q + 1) * width])
        else:
            project(q, wkv[...])

    def measure(s):
        largest = jnp.zeros((8, width), jnp.float32)
        for q in range(chunks):
            largest = jnp.maximum(
                largest, jnp.max(jnp.abs(sums[q, s]).reshape(rows // 8, 8, width), axis=0)
            )
        own[s] = jnp.broadcast_to(jnp.max(largest, keepdims=True), own.shape[1:])

    each(slots, measure)

    steps = (slots - 1) * chunks

    def relay(i):
        def at(i, move):
            @pl.when((i >= 0) & (i < steps))
            def _():
                move(i // chunks, i % chunks)

        @pl.when(low)
        def _():
            at(i, relay_up)
            at(i - chunks, relay_down)

        @pl.when(jnp.logical_not(low))
        def _():
            at(i, relay_down)
            at(i - chunks, relay_up)

    each(steps + chunks, relay)

    @pl.when(low)
    def _():
        send_blocks(1, True)

    @pl.when(jnp.logical_not(low))
    def _():
        send_blocks(1, False)

    def drain_sums(i):
        k, q = i // chunks, i % chunks

        @pl.when(slots - 1 - k > me)
        def _():
            sum_copy(slots - 1 - k, q, True).wait_send()

            @pl.when(q == 0)
            def _():
                bound_copy(slots - 1 - k, True).wait_send()

        @pl.when(k < me)
        def _():
            sum_copy(k, q, False).wait_send()

            @pl.when(q == 0)
            def _():
                bound_copy(k, False).wait_send()

    def rotate_share(source):
        at_t = pl.multiple_of(source * share, share)
        tc, ts = tc_ref[pl.ds(at_t, share), :], ts_ref[pl.ds(at_t, share), :]

        def one(c):
            at_k = pl.multiple_of((source * NCH + c) * share, share)
            oc, os = oc_ref[pl.ds(c, 1), :], os_ref[pl.ds(c, 1), :]
            cos = tc * oc - ts * os
            sin = ts * oc + tc * os
            for g in range(kv_heads):
                at = g * 2 * HD
                x = blocks[source, c, :, at : at + HD].astype(jnp.float32)
                keys[g, pl.ds(at_k, share), :] = turn(x, cos, sin).astype(jnp.bfloat16)

        each(NCH, one)

    own_copy.wait()
    rotate_share(me)

    def take(j):
        for g in range(kv_heads):
            block_copy(other_shift(j), g, 0).wait_recv()
        rotate_share(other(j))

    each(slots - 1, take)

    @pl.when(me > 0)
    def _():
        bound_copy(me, True).wait_recv()

    @pl.when(me < slots - 1)
    def _():
        bound_copy(me, False).wait_recv()

    def settle(q):
        @pl.when(me > 0)
        def _():
            sum_copy(me, q, True).wait_recv()
            add_codes(q, me, me + 1)

        @pl.when(me < slots - 1)
        def _():
            sum_copy(me, q, False).wait_recv()
            add_codes(q, me, me)

    each(chunks, settle)

    qc, qs = qc_ref[...], qs_ref[...]
    for g in range(kv_heads):
        at = g * 2 * HD
        keys[g, past:, :] = turn(sums[chunks - 1, me, :, at : at + HD], qc, qs).astype(jnp.bfloat16)
        fresh[g] = sums[chunks - 1, me, :, at + HD : at + 2 * HD].astype(jnp.bfloat16)
    for h in range(heads):
        q, at = divmod(h * HD, width)
        queries[h * rows : (h + 1) * rows, :] = turn(
            sums[q, me, :, at : at + HD], qc, qs
        ).astype(jnp.bfloat16)

    block = 2 * rows
    span = 512
    factor = math.log2(math.e) / math.sqrt(HD)
    lower = lax.broadcasted_iota(jnp.int32, (block, rows), 0) % rows >= lax.broadcasted_iota(
        jnp.int32, (block, rows), 1
    )
    contract = (((1,), (1,)), ((), ()))

    def weigh(b):
        g = (b * 2) // sharing
        at = pl.ds(pl.multiple_of(b * block, block), block)
        q = queries[at, :]
        own = lax.dot_general(q, keys[g, past:, :], contract, preferred_element_type=jnp.float32)
        own = jnp.where(lower, own, -jnp.inf)
        top = own
        for j in range(past // span):
            s = lax.dot_general(
                q, keys[g, j * span : (j + 1) * span, :], contract,
                preferred_element_type=jnp.float32,
            )
            scores[:, j * span : (j + 1) * span] = s
            for k in range(span // HD):
                top = jnp.maximum(top, s[:, k * HD : (k + 1) * HD])
        top = jnp.max(top, axis=1, keepdims=True)
        w = jnp.exp2((own - top) * factor)
        total = w
        weights[at, past:] = w.astype(jnp.bfloat16)
        for j in range(past // span):
            w = jnp.exp2((scores[:, j * span : (j + 1) * span] - top) * factor)
            for k in range(span // HD):
                total = total + w[:, k * HD : (k + 1) * HD]
            weights[at, j * span : (j + 1) * span] = w.astype(jnp.bfloat16)
        totals[at, :] = total

    each(heads // 2, weigh)

    stack = sharing * rows
    some = NCH * share

    def mix(source, g, first):
        cols = pl.ds(pl.multiple_of(source * some, some), some)
        at = slice(g * stack, (g + 1) * stack)
        v = blocks[source, :, :, (2 * g + 1) * HD : (2 * g + 2) * HD].reshape(some, HD)
        term = jnp.dot(weights[at, cols], v, preferred_element_type=jnp.float32)
        if first:
            mixed[at, :] = term + jnp.dot(
                weights[at, past:], fresh[g], preferred_element_type=jnp.float32
            )
        else:
            mixed[at, :] = mixed[at, :] + term

    for g in range(kv_heads):
        mix(me, g, True)

    def take_values(j):
        for g in range(kv_heads):
            block_copy(other_shift(j), g, 1).wait_recv()
            mix(other(j), g, False)

    each(slots - 1, take_values)

    def finish(h):
        at = pl.ds(pl.multiple_of(h * rows, rows), rows)
        done = mixed[at, :] / jnp.sum(totals[at, :], axis=1, keepdims=True)
        out_ref[0, :, pl.ds(pl.multiple_of(h * HD, HD), HD)] = done.astype(out_ref.dtype)

    each(heads, finish)

    def drain(k):
        strip_copy(k).wait_send()
        for d in range(1, peers):
            spread_copy(k, d).wait_send()

    each(slots, drain, 1)

    def drain_blocks(k):
        for i in range(2 * kv_heads):
            block_copy(k, i // 2, i % 2).wait_send()

    each(slots, drain_blocks, 1)
    each(steps, drain_sums)


def per_device(hidden, query_weight, keyvalue_weight, block_store, block_ids, offsets, served):
    slots = lax.axis_size("store")
    peers = lax.axis_size("mp")
    rows, model = hidden.shape[1:]
    share, kv_cols = block_store.shape[1:]
    q_cols = query_weight.shape[1]
    heads = q_cols // HD
    kv_heads = kv_cols // (2 * HD)
    chunks = q_cols // kv_cols + 1
    depth = model // slots
    past = NCH * L
    sending, oc, os = gather_blocks(block_ids, served, offsets, block_store)
    qc, qs = signed_tables(past + GAP + np.arange(rows))
    tc, ts = signed_tables(np.arange(L))
    vmem = pl.BlockSpec(memory_space=pltpu.VMEM)
    hbm = pl.BlockSpec(memory_space=pl.ANY)
    dma = pltpu.SemaphoreType.DMA
    return pl.pallas_call(
        functools.partial(serve_body, slots, peers, heads, kv_heads),
        out_shape=jax.ShapeDtypeStruct((1, rows, q_cols), jnp.bfloat16),
        in_specs=[vmem, hbm, hbm, hbm] + [vmem] * 6,
        out_specs=vmem,
        scratch_shapes=[
            pltpu.VMEM((slots, rows, depth), jnp.bfloat16),
            pltpu.VMEM(query_weight.shape, jnp.bfloat16),
            pltpu.VMEM(keyvalue_weight.shape, jnp.bfloat16),
            pltpu.VMEM((chunks, slots, rows, kv_cols), jnp.float32),
            pltpu.VMEM((slots + 1, chunks, 3 * rows // 2, kv_cols), jnp.int16),
            pltpu.VMEM((slots, 8, HD), jnp.float32),
            pltpu.VMEM((slots + 1, 8, HD), jnp.float32),
            pltpu.VMEM((slots + 1, 8, HD), jnp.float32),
            pltpu.VMEM((slots, NCH, share, kv_cols), jnp.bfloat16),
            pltpu.VMEM((kv_heads, past + rows, HD), jnp.bfloat16),
            pltpu.VMEM((kv_heads, rows, HD), jnp.bfloat16),
            pltpu.VMEM((heads * rows, HD), jnp.bfloat16),
            pltpu.VMEM((2 * rows, past), jnp.float32),
            pltpu.VMEM((heads * rows, past + rows), jnp.bfloat16),
            pltpu.VMEM((heads * rows, HD), jnp.float32),
            pltpu.VMEM((heads * rows, HD), jnp.float32),
            dma((2,)),
            dma((1,)),
            dma((slots,)),
            dma((slots,)),
            dma((slots, peers)),
            dma((slots, peers)),
            dma((slots, 2 * kv_heads)),
            dma((slots, 2 * kv_heads)),
            dma((slots + 1, chunks)),
            dma((slots + 1, chunks)),
            dma((slots + 1,)),
            dma((slots + 1,)),
        ],
        compiler_params=pltpu.CompilerParams(
            vmem_limit_bytes=63 << 20, collective_id=0, has_side_effects=True
        ),
        name="serve",
    )(hidden, query_weight, keyvalue_weight, sending, qc, qs, tc, ts, oc, os)


def solution(mesh):
    in_specs = (
        P(("groups", "store"), None, None),
        P("store", "mp"),
        P("store", "mp"),
        P("groups", "store", "mp"),
        P("groups", None),
        P("groups", None),
        P("groups"),
    )
    out_specs = P(("groups", "store"), None, "mp")
    return jax.shard_map(
        per_device, mesh=mesh, in_specs=in_specs, out_specs=out_specs, check_vma=False
    )
```

```python
import functools
import math

import jax
import jax.numpy as jnp
import numpy as np
from jax import lax
from jax.experimental import pallas as pl
from jax.experimental.pallas import tpu as pltpu
from jax.sharding import PartitionSpec as P

HD = 128
HALF = HD // 2
NCH = 4
L = 1024
GAP = 64
BASE = 500000.0


def periods():
    inverse = np.exp(
        np.arange(HALF, dtype=np.float32) * np.float32(-2.0 * math.log(BASE) / HD)
    ).astype(np.float32)
    return np.floor(np.float32(2.0 * math.pi) / inverse + np.float32(0.5)).astype(np.float64)


def signed_tables(positions):
    period = periods()[None, :]
    angles = np.mod(np.asarray(positions, np.float64)[:, None], period) / period * (2.0 * math.pi)
    cos, sin = np.cos(angles), np.sin(angles)
    return (
        np.concatenate([cos, cos], axis=1).astype(np.float32),
        np.concatenate([-sin, sin], axis=1).astype(np.float32),
    )


def gather_body(slots, ids_ref, served_ref, store_ref, out_ref, sems):
    copies = []
    for s in range(slots):
        request = served_ref[s]
        for c in range(NCH):
            copy = pltpu.make_async_copy(
                store_ref.at[ids_ref[request, c]], out_ref.at[s, c], sems.at[s, c]
            )
            copy.start()
            copies.append(copy)
    for copy in copies:
        copy.wait()


def gather_blocks(block_ids, served, block_store):
    slots = served.shape[0]
    return pl.pallas_call(
        functools.partial(gather_body, slots),
        grid_spec=pltpu.PrefetchScalarGridSpec(
            num_scalar_prefetch=2,
            grid=(),
            in_specs=[pl.BlockSpec(memory_space=pl.ANY)],
            out_specs=pl.BlockSpec(memory_space=pltpu.VMEM),
            scratch_shapes=[pltpu.SemaphoreType.DMA((slots, NCH))],
        ),
        out_shape=jax.ShapeDtypeStruct((slots, NCH) + block_store.shape[1:], block_store.dtype),
        compiler_params=pltpu.CompilerParams(vmem_limit_bytes=56 << 20),
        name="gather_blocks",
    )(block_ids, served, block_store)


def turn(x, cos, sin):
    return x * cos + pltpu.roll(x, HALF, 1) * sin


MESH = pl.DeviceIdType.MESH
STEPS = 8388000.0
LEAST = 1e-30


def encode(top, bottom, bound, code, first):
    half = top.shape[0]
    half_rows = code.shape[0] // 3
    factor = STEPS / jnp.maximum(bound, LEAST)
    top = jnp.round(top * factor).astype(jnp.int32)
    bottom = jnp.round(bottom * factor).astype(jnp.int32)
    code[pl.ds(first, half), :] = (top >> 8).astype(jnp.int16)
    code[pl.ds(half_rows + first, half), :] = (bottom >> 8).astype(jnp.int16)
    pair = (top & 255) | ((bottom & 255) << 8)
    code[pl.ds(2 * half_rows + first, half), :] = (pair - 32768).astype(jnp.int16)


def decode(bound, code, first, half):
    half_rows = code.shape[0] // 3
    pair = code[pl.ds(2 * half_rows + first, half), :].astype(jnp.int32) + 32768
    top = (code[pl.ds(first, half), :].astype(jnp.int32) << 8) | (pair & 255)
    bottom = (code[pl.ds(half_rows + first, half), :].astype(jnp.int32) << 8) | (pair >> 8)
    step = bound * (1.0 / STEPS)
    return top.astype(jnp.float32) * step, bottom.astype(jnp.float32) * step


def serve_body(
    slots, peers, heads, kv_heads,
    served_ref, offsets_ref, hidden_ref, wq_hbm, wkv_hbm, sending_ref, tables_hbm,
    out_hbm,
    tokens, wq, wkv, sums, codes, own, bounds_in, bounds_out, blocks, keys, fresh, queries, scores, weights, totals, mixed, tables, out,
    load_sem, own_sem, out_sem, a_send, a_recv, b_send, b_recv, k_send, k_recv, p_send, p_recv, s_send, s_recv,
):
    me = lax.axis_index("store")
    part = lax.axis_index("mp")
    rows = hidden_ref.shape[1]
    depth = tokens.shape[2]
    chunks, _, _, width = sums.shape
    share = blocks.shape[2]
    sharing = heads // kv_heads
    past = NCH * L
    strip = rows // peers

    barrier = pltpu.get_barrier_semaphore()
    for k in range(1, slots):
        pl.semaphore_signal(
            barrier, inc=1, device_id={"store": lax.rem(me + k, slots)}, device_id_type=MESH
        )
    for k in range(1, peers):
        pl.semaphore_signal(
            barrier, inc=1, device_id={"mp": lax.rem(part + k, peers)}, device_id_type=MESH
        )
    loads = [
        pltpu.make_async_copy(wq_hbm, wq, load_sem.at[0]),
        pltpu.make_async_copy(wkv_hbm, wkv, load_sem.at[1]),
        pltpu.make_async_copy(
            hidden_ref.at[0, :, pl.ds(pl.multiple_of(me * depth, depth), depth)],
            tokens.at[me], load_sem.at[2],
        ),
    ]
    own_copy = pltpu.make_async_copy(sending_ref.at[me], blocks.at[me], own_sem.at[0])
    tables_copy = pltpu.make_async_copy(tables_hbm, tables, own_sem.at[1])
    pl.semaphore_wait(barrier, slots + peers - 2)

    def strip_copy(k):
        to = lax.rem(me + k, slots)
        mine = pl.ds(pl.multiple_of(part * strip, strip), strip)
        return pltpu.make_async_remote_copy(
            src_ref=hidden_ref.at[0, mine, pl.ds(pl.multiple_of(to * depth, depth), depth)],
            dst_ref=tokens.at[me, mine, :],
            send_sem=a_send.at[k],
            recv_sem=a_recv.at[k],
            device_id={"store": to},
            device_id_type=MESH,
        )

    def spread_copy(k, d):
        source = lax.rem(me - k + slots, slots)
        mine = pl.ds(pl.multiple_of(part * strip, strip), strip)
        return pltpu.make_async_remote_copy(
            src_ref=tokens.at[source, mine, :],
            dst_ref=tokens.at[source, mine, :],
            send_sem=b_send.at[k, d],
            recv_sem=b_recv.at[k, d],
            device_id={"mp": lax.rem(part + d, peers)},
            device_id_type=MESH,
        )

    def block_copy(k, g, v):
        to = lax.rem(me + k, slots)
        cols = pl.ds(pl.multiple_of((2 * g + v) * HD, HD), HD)
        return pltpu.make_async_remote_copy(
            src_ref=sending_ref.at[to, :, :, cols],
            dst_ref=blocks.at[me, :, :, cols],
            send_sem=k_send.at[k, 2 * g + v],
            recv_sem=k_recv.at[k, 2 * g + v],
            device_id={"store": to},
            device_id_type=MESH,
        )

    low = me < slots // 2

    mirrored = jnp.where(low, me, slots - 1 - me)

    def other(j):
        far = jnp.where(mirrored == 0, 0, slots - 2 - mirrored)
        source = jnp.where(
            j < far, slots - 1 - j, jnp.where(j < far + mirrored, j - far, mirrored + 1 + jnp.where(mirrored == 0, j, 0))
        )
        return jnp.where(low, source, slots - 1 - source)

    def other_shift(j):
        return lax.rem(me - other(j) + slots, slots)

    def send_blocks(v, up):
        def one(j):
            d = slots - 1 - j
            fits = (me + d < slots) if up else (me >= d)

            @pl.when(fits)
            def _():
                for g in range(kv_heads):
                    block_copy(d if up else slots - d, g, v).start()

        each(slots - 1, one)

    def sum_copy(s, q, up):
        index = s + 1 if up else s
        return pltpu.make_async_remote_copy(
            src_ref=codes.at[index, q],
            dst_ref=codes.at[index, q],
            send_sem=p_send.at[index, q],
            recv_sem=p_recv.at[index, q],
            device_id={"store": lax.rem(me + 1, slots) if up else lax.rem(me + slots - 1, slots)},
            device_id_type=MESH,
        )

    def bound_copy(s, up):
        index = s + 1 if up else s
        return pltpu.make_async_remote_copy(
            src_ref=bounds_out.at[index],
            dst_ref=bounds_in.at[index],
            send_sem=s_send.at[index],
            recv_sem=s_recv.at[index],
            device_id={"store": lax.rem(me + 1, slots) if up else lax.rem(me + slots - 1, slots)},
            device_id_type=MESH,
        )

    strip_rows = 16

    def add_codes(q, s, index):
        code, bound = codes.at[index, q], bounds_in[index][:1, :1]

        def some(i):
            at = pl.multiple_of(i * strip_rows, strip_rows)
            top, bottom = decode(bound, code, at, strip_rows)
            lower = pl.ds(rows // 2 + at, strip_rows)
            at = pl.ds(at, strip_rows)
            sums[q, s, at] = sums[q, s, at] + top
            sums[q, s, lower] = sums[q, s, lower] + bottom

        each(rows // 2 // strip_rows, some)

    def make_codes(q, s, index):
        code, bound = codes.at[index, q], bounds_out[index][:1, :1]

        def some(i):
            at = pl.multiple_of(i * strip_rows, strip_rows)
            encode(
                sums[q, s, pl.ds(at, strip_rows)],
                sums[q, s, pl.ds(rows // 2 + at, strip_rows)],
                bound, code, at,
            )

        each(rows // 2 // strip_rows, some)

    def forward(q, s, up, begins):
        index = s + 1 if up else s

        @pl.when(q == 0)
        def _():
            @pl.when(begins)
            def _():
                bounds_out[index] = own[s]

            @pl.when(jnp.logical_not(begins))
            def _():
                bound_copy(s, up).wait_recv()
                bounds_out[index] = own[s] + bounds_in[index]

            bound_copy(s, up).start()

        @pl.when(jnp.logical_not(begins))
        def _():
            sum_copy(s, q, up).wait_recv()
            add_codes(q, s, index)

        make_codes(q, s, index)
        sum_copy(s, q, up).start()

    def each(count, body, first=0):
        def step(i, carry):
            body(i)
            return carry

        lax.fori_loop(first, count, step, 0)

    each(slots, lambda k: strip_copy(k).start(), 1)
    send_blocks(0, True)
    send_blocks(0, False)

    @pl.when(low)
    def _():
        send_blocks(1, False)

    @pl.when(jnp.logical_not(low))
    def _():
        send_blocks(1, True)

    for load in loads:
        load.start()
    own_copy.start()
    tables_copy.start()

    def spread(k):
        strip_copy(k).wait_recv()
        for d in range(1, peers):
            spread_copy(k, d).start()

    each(slots, spread, 1)

    def spread_wait(k):
        for d in range(1, peers):
            spread_copy(k, d).wait_recv()

    each(slots, spread_wait, 1)
    for load in loads:
        load.wait()

    group = 4 if slots % 4 == 0 else 1

    def project(q, panel):
        def some(i):
            t = tokens[pl.ds(i * group, group)].reshape(group * rows, depth)
            sums[q, pl.ds(i * group, group)] = jnp.dot(
                t, panel, preferred_element_type=jnp.float32
            ).reshape(group, rows, width)

        each(slots // group, some)

    def relay_up(k, q):
        @pl.when(slots - 1 - k > me)
        def _():
            forward(q, slots - 1 - k, True, me == 0)

    def relay_down(k, q):
        @pl.when(k < me)
        def _():
            forward(q, k, False, me == slots - 1)

    for q in range(chunks):
        if q < chunks - 1:
            project(q, wq[:, q * width : (q + 1) * width])
        else:
            project(q, wkv[...])

    def measure(s):
        largest = jnp.zeros((8, width), jnp.float32)
        for q in range(chunks):
            largest = jnp.maximum(
                largest, jnp.max(jnp.abs(sums[q, s]).reshape(rows // 8, 8, width), axis=0)
            )
        own[s] = jnp.broadcast_to(jnp.max(largest, keepdims=True), own.shape[1:])

    each(slots, measure)

    steps = (slots - 1) * chunks

    def relay(i):
        def at(i, move):
            @pl.when((i >= 0) & (i < steps))
            def _():
                move(i // chunks, i % chunks)

        @pl.when(low)
        def _():
            at(i, relay_up)
            at(i - chunks, relay_down)

        @pl.when(jnp.logical_not(low))
        def _():
            at(i, relay_down)
            at(i - chunks, relay_up)

    each(steps + chunks, relay)

    @pl.when(low)
    def _():
        send_blocks(1, True)

    @pl.when(jnp.logical_not(low))
    def _():
        send_blocks(1, False)

    def drain_sums(i):
        k, q = i // chunks, i % chunks

        @pl.when(slots - 1 - k > me)
        def _():
            sum_copy(slots - 1 - k, q, True).wait_send()

            @pl.when(q == 0)
            def _():
                bound_copy(slots - 1 - k, True).wait_send()

        @pl.when(k < me)
        def _():
            sum_copy(k, q, False).wait_send()

            @pl.when(q == 0)
            def _():
                bound_copy(k, False).wait_send()

    def rotate_share(source):
        at_t = pl.multiple_of(source * share, share)
        tc, ts = tables[0, pl.ds(at_t, share), :], tables[1, pl.ds(at_t, share), :]

        def one(c):
            at_k = pl.multiple_of((source * NCH + c) * share, share)
            jitter = jnp.clip(offsets_ref[served_ref[me], c] - c * L, 0, GAP - 1)
            start = L + c * GAP + jitter
            oc, os = tables[0, pl.ds(start, 1), :], tables[1, pl.ds(start, 1), :]
            cos = tc * oc - ts * os
            sin = ts * oc + tc * os
            for g in range(kv_heads):
                at = g * 2 * HD
                x = blocks[source, c, :, at : at + HD].astype(jnp.float32)
                keys[g, pl.ds(at_k, share), :] = turn(x, cos, sin).astype(jnp.bfloat16)

        each(NCH, one)

    own_copy.wait()
    tables_copy.wait()
    rotate_share(me)

    def take(j):
        for g in range(kv_heads):
            block_copy(other_shift(j), g, 0).wait_recv()
        rotate_share(other(j))

    each(slots - 1, take)

    @pl.when(me > 0)
    def _():
        bound_copy(me, True).wait_recv()

    @pl.when(me < slots - 1)
    def _():
        bound_copy(me, False).wait_recv()

    def settle(q):
        @pl.when(me > 0)
        def _():
            sum_copy(me, q, True).wait_recv()
            add_codes(q, me, me + 1)

        @pl.when(me < slots - 1)
        def _():
            sum_copy(me, q, False).wait_recv()
            add_codes(q, me, me)

    each(chunks, settle)

    at_q = L + NCH * GAP
    qc, qs = tables[0, at_q : at_q + rows, :], tables[1, at_q : at_q + rows, :]
    for g in range(kv_heads):
        at = g * 2 * HD
        keys[g, past:, :] = turn(sums[chunks - 1, me, :, at : at + HD], qc, qs).astype(jnp.bfloat16)
        fresh[g] = sums[chunks - 1, me, :, at + HD : at + 2 * HD].astype(jnp.bfloat16)
    for h in range(heads):
        q, at = divmod(h * HD, width)
        queries[h * rows : (h + 1) * rows, :] = turn(
            sums[q, me, :, at : at + HD], qc, qs
        ).astype(jnp.bfloat16)

    block = 2 * rows
    span = 512
    factor = math.log2(math.e) / math.sqrt(HD)
    lower = lax.broadcasted_iota(jnp.int32, (block, rows), 0) % rows >= lax.broadcasted_iota(
        jnp.int32, (block, rows), 1
    )
    contract = (((1,), (1,)), ((), ()))

    def weigh(b):
        g = (b * 2) // sharing
        at = pl.ds(pl.multiple_of(b * block, block), block)
        q = queries[at, :]
        own = lax.dot_general(q, keys[g, past:, :], contract, preferred_element_type=jnp.float32)
        own = jnp.where(lower, own, -jnp.inf)
        top = own
        for j in range(past // span):
            s = lax.dot_general(
                q, keys[g, j * span : (j + 1) * span, :], contract,
                preferred_element_type=jnp.float32,
            )
            scores[:, j * span : (j + 1) * span] = s
            for k in range(span // HD):
                top = jnp.maximum(top, s[:, k * HD : (k + 1) * HD])
        top = jnp.max(top, axis=1, keepdims=True)
        w = jnp.exp2((own - top) * factor)
        total = w
        weights[at, past:] = w.astype(jnp.bfloat16)
        for j in range(past // span):
            w = jnp.exp2((scores[:, j * span : (j + 1) * span] - top) * factor)
            for k in range(span // HD):
                total = total + w[:, k * HD : (k + 1) * HD]
            weights[at, j * span : (j + 1) * span] = w.astype(jnp.bfloat16)
        totals[at, :] = total

    each(heads // 2, weigh)

    stack = sharing * rows
    some = NCH * share

    def invert(h):
        at = pl.ds(pl.multiple_of(h * rows, rows), rows)
        totals[at, :] = jnp.broadcast_to(
            1.0 / jnp.sum(totals[at, :], axis=1, keepdims=True), (rows, HD)
        )

    each(heads, invert)

    def product(source, g):
        cols = pl.ds(pl.multiple_of(source * some, some), some)
        v = blocks[source, :, :, (2 * g + 1) * HD : (2 * g + 2) * HD].reshape(some, HD)
        return jnp.dot(
            weights[g * stack : (g + 1) * stack, cols], v, preferred_element_type=jnp.float32
        )

    for g in range(kv_heads):
        at = slice(g * stack, (g + 1) * stack)
        mixed[at, :] = product(me, g) + jnp.dot(
            weights[at, past:], fresh[g], preferred_element_type=jnp.float32
        )

    def take_values(j, g):
        at = slice(g * stack, (g + 1) * stack)
        block_copy(other_shift(j), g, 1).wait_recv()
        mixed[at, :] = mixed[at, :] + product(other(j), g)

    def out_copy(g):
        cols = slice(g * stack, (g + 1) * stack)
        return pltpu.make_async_copy(out.at[:, cols], out_hbm.at[0, :, cols], out_sem.at[g])

    early = slots - 3
    for j in range(early):
        for g in range(kv_heads):
            take_values(j, g)
    for g in range(kv_heads):
        for j in range(early, slots - 2):
            take_values(j, g)
        block_copy(other_shift(slots - 2), g, 1).wait_recv()
        at = slice(g * stack, (g + 1) * stack)
        done = (mixed[at, :] + product(other(slots - 2), g)) * totals[at, :]
        for h in range(sharing):
            first = (g * sharing + h) * HD
            out[:, first : first + HD] = done[h * rows : (h + 1) * rows].astype(out.dtype)
        out_copy(g).start()

    def drain(k):
        strip_copy(k).wait_send()
        for d in range(1, peers):
            spread_copy(k, d).wait_send()

    each(slots, drain, 1)

    def drain_blocks(k):
        for i in range(2 * kv_heads):
            block_copy(k, i // 2, i % 2).wait_send()

    each(slots, drain_blocks, 1)
    each(steps, drain_sums)
    for g in range(kv_heads):
        out_copy(g).wait()


def per_device(hidden, query_weight, keyvalue_weight, block_store, block_ids, offsets, served):
    slots = lax.axis_size("store")
    peers = lax.axis_size("mp")
    rows, model = hidden.shape[1:]
    share, kv_cols = block_store.shape[1:]
    q_cols = query_weight.shape[1]
    heads = q_cols // HD
    kv_heads = kv_cols // (2 * HD)
    chunks = q_cols // kv_cols + 1
    depth = model // slots
    past = NCH * L
    sending = gather_blocks(block_ids, served, block_store)
    starts = (np.arange(NCH)[:, None] * L + np.arange(GAP)[None, :]).reshape(-1)
    tables = np.stack(
        signed_tables(np.concatenate([np.arange(L), starts, past + GAP + np.arange(rows)]))
    )
    hbm = pl.BlockSpec(memory_space=pl.ANY)
    smem = pl.BlockSpec(memory_space=pltpu.SMEM)
    dma = pltpu.SemaphoreType.DMA
    return pl.pallas_call(
        functools.partial(serve_body, slots, peers, heads, kv_heads),
        out_shape=jax.ShapeDtypeStruct((1, rows, q_cols), jnp.bfloat16),
        in_specs=[smem, smem] + [hbm] * 5,
        out_specs=hbm,
        scratch_shapes=[
            pltpu.VMEM((slots, rows, depth), jnp.bfloat16),
            pltpu.VMEM(query_weight.shape, jnp.bfloat16),
            pltpu.VMEM(keyvalue_weight.shape, jnp.bfloat16),
            pltpu.VMEM((chunks, slots, rows, kv_cols), jnp.float32),
            pltpu.VMEM((slots + 1, chunks, 3 * rows // 2, kv_cols), jnp.int16),
            pltpu.VMEM((slots, 8, HD), jnp.float32),
            pltpu.VMEM((slots + 1, 8, HD), jnp.float32),
            pltpu.VMEM((slots + 1, 8, HD), jnp.float32),
            pltpu.VMEM((slots, NCH, share, kv_cols), jnp.bfloat16),
            pltpu.VMEM((kv_heads, past + rows, HD), jnp.bfloat16),
            pltpu.VMEM((kv_heads, rows, HD), jnp.bfloat16),
            pltpu.VMEM((heads * rows, HD), jnp.bfloat16),
            pltpu.VMEM((2 * rows, past), jnp.float32),
            pltpu.VMEM((heads * rows, past + rows), jnp.bfloat16),
            pltpu.VMEM((heads * rows, HD), jnp.float32),
            pltpu.VMEM((heads * rows, HD), jnp.float32),
            pltpu.VMEM(tables.shape, jnp.float32),
            pltpu.VMEM((rows, q_cols), jnp.bfloat16),
            dma((3,)),
            dma((2,)),
            dma((kv_heads,)),
            dma((slots,)),
            dma((slots,)),
            dma((slots, peers)),
            dma((slots, peers)),
            dma((slots, 2 * kv_heads)),
            dma((slots, 2 * kv_heads)),
            dma((slots + 1, chunks)),
            dma((slots + 1, chunks)),
            dma((slots + 1,)),
            dma((slots + 1,)),
        ],
        compiler_params=pltpu.CompilerParams(
            vmem_limit_bytes=63 << 20, collective_id=0, has_side_effects=True
        ),
        name="serve",
    )(served, offsets, hidden, query_weight, keyvalue_weight, sending, tables)


def solution(mesh):
    in_specs = (
        P(("groups", "store"), None, None),
        P("store", "mp"),
        P("store", "mp"),
        P("groups", "store", "mp"),
        P("groups", None),
        P("groups", None),
        P("groups"),
    )
    out_specs = P(("groups", "store"), None, "mp")
    return jax.shard_map(
        per_device, mesh=mesh, in_specs=in_specs, out_specs=out_specs, check_vma=False
    )
```

```python
import functools
import math

import jax
import jax.numpy as jnp
import numpy as np
from jax import lax
from jax.experimental import pallas as pl
from jax.experimental.pallas import tpu as pltpu
from jax.sharding import PartitionSpec as P

HD = 128
HALF = HD // 2
NCH = 4
L = 1024
GAP = 64
BASE = 500000.0


def periods():
    inverse = np.exp(
        np.arange(HALF, dtype=np.float32) * np.float32(-2.0 * math.log(BASE) / HD)
    ).astype(np.float32)
    return np.floor(np.float32(2.0 * math.pi) / inverse + np.float32(0.5)).astype(np.float64)


def signed_tables(positions):
    period = periods()[None, :]
    angles = np.mod(np.asarray(positions, np.float64)[:, None], period) / period * (2.0 * math.pi)
    cos, sin = np.cos(angles), np.sin(angles)
    return (
        np.concatenate([cos, cos], axis=1).astype(np.float32),
        np.concatenate([-sin, sin], axis=1).astype(np.float32),
    )


def turn(x, cos, sin):
    return x * cos + pltpu.roll(x, HALF, 1) * sin


MESH = pl.DeviceIdType.MESH
STEPS = 8388000.0
LEAST = 1e-30


def encode(top, bottom, bound, code, first):
    half = top.shape[0]
    half_rows = code.shape[0] // 3
    factor = STEPS / jnp.maximum(bound, LEAST)
    top = jnp.round(top * factor).astype(jnp.int32)
    bottom = jnp.round(bottom * factor).astype(jnp.int32)
    code[pl.ds(first, half), :] = (top >> 8).astype(jnp.int16)
    code[pl.ds(half_rows + first, half), :] = (bottom >> 8).astype(jnp.int16)
    pair = (top & 255) | ((bottom & 255) << 8)
    code[pl.ds(2 * half_rows + first, half), :] = (pair - 32768).astype(jnp.int16)


def decode(bound, code, first, half):
    half_rows = code.shape[0] // 3
    pair = code[pl.ds(2 * half_rows + first, half), :].astype(jnp.int32) + 32768
    top = (code[pl.ds(first, half), :].astype(jnp.int32) << 8) | (pair & 255)
    bottom = (code[pl.ds(half_rows + first, half), :].astype(jnp.int32) << 8) | (pair >> 8)
    step = bound * (1.0 / STEPS)
    return top.astype(jnp.float32) * step, bottom.astype(jnp.float32) * step


def serve_body(
    slots, peers, heads, kv_heads,
    ids_ref, served_ref, offsets_ref, hidden_ref, wq_hbm, wkv_hbm, store_hbm, tables_hbm,
    out_hbm,
    tokens, wq, wkv, sums, codes, own, bounds_in, bounds_out, blocks, keys, fresh, queries, scores, weights, own_weights, stored, sending, totals, mixed, tables, out,
    load_sem, own_sem, store_sem, out_sem, a_send, a_recv, b_send, b_recv, k_send, k_recv, p_send, p_recv, s_send, s_recv,
):
    me = lax.axis_index("store")
    part = lax.axis_index("mp")
    rows = hidden_ref.shape[1]
    depth = tokens.shape[2]
    chunks, _, _, width = sums.shape
    share = blocks.shape[2]
    sharing = heads // kv_heads
    past = NCH * L
    strip = rows // peers

    def each(count, body, first=0):
        def step(i, carry):
            body(i)
            return carry

        lax.fori_loop(first, count, step, 0)

    if stored is None:
        several = weights.shape[1]
        store_loads = [
            pltpu.make_async_copy(
                store_hbm.at[pl.ds(i * several, several)], weights.at[i], store_sem.at[i]
            )
            for i in range(store_hbm.shape[0] // several)
        ]
    else:
        store_loads = [pltpu.make_async_copy(store_hbm, stored, store_sem.at[0])]
    for load in store_loads:
        load.start()

    def pick(s, target):
        request = served_ref[s]

        def one(c):
            block = ids_ref[request, c]
            if stored is None:
                target[s, c] = weights[block // several, block % several]
            else:
                target[s, c] = stored[block]

        each(NCH, one)

    barrier = pltpu.get_barrier_semaphore()
    for k in range(1, slots):
        pl.semaphore_signal(
            barrier, inc=1, device_id={"store": lax.rem(me + k, slots)}, device_id_type=MESH
        )
    for k in range(1, peers):
        pl.semaphore_signal(
            barrier, inc=1, device_id={"mp": lax.rem(part + k, peers)}, device_id_type=MESH
        )
    loads = [
        pltpu.make_async_copy(wq_hbm, wq, load_sem.at[0]),
        pltpu.make_async_copy(wkv_hbm, wkv, load_sem.at[1]),
        pltpu.make_async_copy(
            hidden_ref.at[0, :, pl.ds(pl.multiple_of(me * depth, depth), depth)],
            tokens.at[me], load_sem.at[2],
        ),
    ]
    tables_copy = pltpu.make_async_copy(tables_hbm, tables, own_sem.at[0])
    pl.semaphore_wait(barrier, slots + peers - 2)

    def strip_copy(k):
        to = lax.rem(me + k, slots)
        mine = pl.ds(pl.multiple_of(part * strip, strip), strip)
        return pltpu.make_async_remote_copy(
            src_ref=hidden_ref.at[0, mine, pl.ds(pl.multiple_of(to * depth, depth), depth)],
            dst_ref=tokens.at[me, mine, :],
            send_sem=a_send.at[k],
            recv_sem=a_recv.at[k],
            device_id={"store": to},
            device_id_type=MESH,
        )

    def spread_copy(k, d):
        source = lax.rem(me - k + slots, slots)
        mine = pl.ds(pl.multiple_of(part * strip, strip), strip)
        return pltpu.make_async_remote_copy(
            src_ref=tokens.at[source, mine, :],
            dst_ref=tokens.at[source, mine, :],
            send_sem=b_send.at[k, d],
            recv_sem=b_recv.at[k, d],
            device_id={"mp": lax.rem(part + d, peers)},
            device_id_type=MESH,
        )

    def block_copy(k, g, v):
        to = lax.rem(me + k, slots)
        cols = pl.ds(pl.multiple_of((2 * g + v) * HD, HD), HD)
        return pltpu.make_async_remote_copy(
            src_ref=sending.at[to, :, :, cols],
            dst_ref=blocks.at[me, :, :, cols],
            send_sem=k_send.at[k, 2 * g + v],
            recv_sem=k_recv.at[k, 2 * g + v],
            device_id={"store": to},
            device_id_type=MESH,
        )

    low = me < slots // 2

    mirrored = jnp.where(low, me, slots - 1 - me)

    def other(j):
        far = jnp.where(mirrored == 0, 0, slots - 2 - mirrored)
        source = jnp.where(
            j < far, slots - 1 - j, jnp.where(j < far + mirrored, j - far, mirrored + 1 + jnp.where(mirrored == 0, j, 0))
        )
        return jnp.where(low, source, slots - 1 - source)

    def other_shift(j):
        return lax.rem(me - other(j) + slots, slots)

    def send_blocks(v, up):
        def one(j):
            d = slots - 1 - j
            fits = (me + d < slots) if up else (me >= d)

            @pl.when(fits)
            def _():
                for g in range(kv_heads):
                    block_copy(d if up else slots - d, g, v).start()

        each(slots - 1, one)

    def sum_copy(s, q, up):
        index = s + 1 if up else s
        return pltpu.make_async_remote_copy(
            src_ref=codes.at[index, q],
            dst_ref=codes.at[index, q],
            send_sem=p_send.at[index, q],
            recv_sem=p_recv.at[index, q],
            device_id={"store": lax.rem(me + 1, slots) if up else lax.rem(me + slots - 1, slots)},
            device_id_type=MESH,
        )

    def bound_copy(s, up):
        index = s + 1 if up else s
        return pltpu.make_async_remote_copy(
            src_ref=bounds_out.at[index],
            dst_ref=bounds_in.at[index],
            send_sem=s_send.at[index],
            recv_sem=s_recv.at[index],
            device_id={"store": lax.rem(me + 1, slots) if up else lax.rem(me + slots - 1, slots)},
            device_id_type=MESH,
        )

    strip_rows = 16

    def add_codes(q, s, index):
        code, bound = codes.at[index, q], bounds_in[index][:1, :1]

        def some(i):
            at = pl.multiple_of(i * strip_rows, strip_rows)
            top, bottom = decode(bound, code, at, strip_rows)
            lower = pl.ds(rows // 2 + at, strip_rows)
            at = pl.ds(at, strip_rows)
            sums[q, s, at] = sums[q, s, at] + top
            sums[q, s, lower] = sums[q, s, lower] + bottom

        each(rows // 2 // strip_rows, some)

    def make_codes(q, s, index):
        code, bound = codes.at[index, q], bounds_out[index][:1, :1]

        def some(i):
            at = pl.multiple_of(i * strip_rows, strip_rows)
            encode(
                sums[q, s, pl.ds(at, strip_rows)],
                sums[q, s, pl.ds(rows // 2 + at, strip_rows)],
                bound, code, at,
            )

        each(rows // 2 // strip_rows, some)

    def forward(q, s, up, begins):
        index = s + 1 if up else s

        @pl.when(q == 0)
        def _():
            @pl.when(begins)
            def _():
                bounds_out[index] = own[s]

            @pl.when(jnp.logical_not(begins))
            def _():
                bound_copy(s, up).wait_recv()
                bounds_out[index] = own[s] + bounds_in[index]

            bound_copy(s, up).start()

        @pl.when(jnp.logical_not(begins))
        def _():
            sum_copy(s, q, up).wait_recv()
            add_codes(q, s, index)

        make_codes(q, s, index)
        sum_copy(s, q, up).start()

    each(slots, lambda k: strip_copy(k).start(), 1)
    for load in loads:
        load.start()
    tables_copy.start()
    for load in store_loads:
        load.wait()

    def send_keys(j):
        d = slots - 1 - j
        for up in (True, False):
            to = me + d if up else me - d

            @pl.when((to < slots) if up else (to >= 0))
            def _():
                pick(to, sending)
                for g in range(kv_heads):
                    block_copy(d if up else slots - d, g, 0).start()

    each(slots - 1, send_keys)
    pick(me, blocks)

    @pl.when(low)
    def _():
        send_blocks(1, False)

    @pl.when(jnp.logical_not(low))
    def _():
        send_blocks(1, True)


    def spread(k):
        strip_copy(k).wait_recv()
        for d in range(1, peers):
            spread_copy(k, d).start()

    each(slots, spread, 1)

    def spread_wait(k):
        for d in range(1, peers):
            spread_copy(k, d).wait_recv()

    each(slots, spread_wait, 1)
    for load in loads:
        load.wait()

    group = 4 if slots % 4 == 0 else 1

    def project(q, panel):
        def some(i):
            t = tokens[pl.ds(i * group, group)].reshape(group * rows, depth)
            sums[q, pl.ds(i * group, group)] = jnp.dot(
                t, panel, preferred_element_type=jnp.float32
            ).reshape(group, rows, width)

        each(slots // group, some)

    def relay_up(k, q):
        @pl.when(slots - 1 - k > me)
        def _():
            forward(q, slots - 1 - k, True, me == 0)

    def relay_down(k, q):
        @pl.when(k < me)
        def _():
            forward(q, k, False, me == slots - 1)

    for q in range(chunks):
        if q < chunks - 1:
            project(q, wq[:, q * width : (q + 1) * width])
        else:
            project(q, wkv[...])

    def measure(s):
        largest = jnp.zeros((8, width), jnp.float32)
        for q in range(chunks):
            largest = jnp.maximum(
                largest, jnp.max(jnp.abs(sums[q, s]).reshape(rows // 8, 8, width), axis=0)
            )
        own[s] = jnp.broadcast_to(jnp.max(largest, keepdims=True), own.shape[1:])

    each(slots, measure)

    steps = (slots - 1) * chunks

    def relay(i):
        def at(i, move):
            @pl.when((i >= 0) & (i < steps))
            def _():
                move(i // chunks, i % chunks)

        @pl.when(low)
        def _():
            at(i, relay_up)
            at(i - chunks, relay_down)

        @pl.when(jnp.logical_not(low))
        def _():
            at(i, relay_down)
            at(i - chunks, relay_up)

    each(steps + chunks, relay)

    @pl.when(low)
    def _():
        send_blocks(1, True)

    @pl.when(jnp.logical_not(low))
    def _():
        send_blocks(1, False)

    def drain_sums(i):
        k, q = i // chunks, i % chunks

        @pl.when(slots - 1 - k > me)
        def _():
            sum_copy(slots - 1 - k, q, True).wait_send()

            @pl.when(q == 0)
            def _():
                bound_copy(slots - 1 - k, True).wait_send()

        @pl.when(k < me)
        def _():
            sum_copy(k, q, False).wait_send()

            @pl.when(q == 0)
            def _():
                bound_copy(k, False).wait_send()

    def rotate_share(source):
        at_t = pl.multiple_of(source * share, share)
        tc, ts = tables[0, pl.ds(at_t, share), :], tables[1, pl.ds(at_t, share), :]

        def one(c):
            at_k = pl.multiple_of((source * NCH + c) * share, share)
            jitter = jnp.clip(offsets_ref[served_ref[me], c] - c * L, 0, GAP - 1)
            start = L + c * GAP + jitter
            oc, os = tables[0, pl.ds(start, 1), :], tables[1, pl.ds(start, 1), :]
            cos = tc * oc - ts * os
            sin = ts * oc + tc * os
            for g in range(kv_heads):
                at = g * 2 * HD
                x = blocks[source, c, :, at : at + HD].astype(jnp.float32)
                keys[g, pl.ds(at_k, share), :] = turn(x, cos, sin).astype(jnp.bfloat16)

        each(NCH, one)

    tables_copy.wait()
    rotate_share(me)

    def take(j):
        for g in range(kv_heads):
            block_copy(other_shift(j), g, 0).wait_recv()
        rotate_share(other(j))

    each(slots - 1, take)

    @pl.when(me > 0)
    def _():
        bound_copy(me, True).wait_recv()

    @pl.when(me < slots - 1)
    def _():
        bound_copy(me, False).wait_recv()

    def settle(q):
        @pl.when(me > 0)
        def _():
            sum_copy(me, q, True).wait_recv()
            add_codes(q, me, me + 1)

        @pl.when(me < slots - 1)
        def _():
            sum_copy(me, q, False).wait_recv()
            add_codes(q, me, me)

    each(chunks, settle)

    at_q = L + NCH * GAP
    qc, qs = tables[0, at_q : at_q + rows, :], tables[1, at_q : at_q + rows, :]
    for g in range(kv_heads):
        at = g * 2 * HD
        keys[g, past:, :] = turn(sums[chunks - 1, me, :, at : at + HD], qc, qs).astype(jnp.bfloat16)
        fresh[g] = sums[chunks - 1, me, :, at + HD : at + 2 * HD].astype(jnp.bfloat16)
    for h in range(heads):
        q, at = divmod(h * HD, width)
        queries[h * rows : (h + 1) * rows, :] = turn(
            sums[q, me, :, at : at + HD], qc, qs
        ).astype(jnp.bfloat16)

    block = 2 * rows
    span = weights.shape[3]
    factor = math.log2(math.e) / math.sqrt(HD)
    lower = lax.broadcasted_iota(jnp.int32, (block, rows), 0) % rows >= lax.broadcasted_iota(
        jnp.int32, (block, rows), 1
    )
    contract = (((1,), (1,)), ((), ()))

    def weigh(b):
        g = (b * 2) // sharing
        at = pl.ds(pl.multiple_of(b * block, block), block)
        q = queries[at, :]
        own = lax.dot_general(q, keys[g, past:, :], contract, preferred_element_type=jnp.float32)
        own = jnp.where(lower, own, -jnp.inf)
        top = own
        for j in range(past // span):
            s = lax.dot_general(
                q, keys[g, j * span : (j + 1) * span, :], contract,
                preferred_element_type=jnp.float32,
            )
            scores[:, j * span : (j + 1) * span] = s
            for k in range(span // HD):
                top = jnp.maximum(top, s[:, k * HD : (k + 1) * HD])
        top = jnp.max(top, axis=1, keepdims=True)
        w = jnp.exp2((own - top) * factor)
        total = w
        own_weights[at, :] = w.astype(jnp.bfloat16)
        for j in range(past // span):
            w = jnp.exp2((scores[:, j * span : (j + 1) * span] - top) * factor)
            for k in range(span // HD):
                total = total + w[:, k * HD : (k + 1) * HD]
            weights[b, j] = w.astype(jnp.bfloat16)
        totals[at, :] = total

    each(heads // 2, weigh)

    stack = sharing * rows
    some = NCH * share

    def invert(h):
        at = pl.ds(pl.multiple_of(h * rows, rows), rows)
        totals[at, :] = jnp.broadcast_to(
            1.0 / jnp.sum(totals[at, :], axis=1, keepdims=True), (rows, HD)
        )

    each(heads, invert)

    pairs = sharing // 2

    def product(source, g):
        v = blocks[source, :, :, (2 * g + 1) * HD : (2 * g + 2) * HD].reshape(some, HD)
        mine = slice(g * pairs, (g + 1) * pairs)
        size = min(some, span)
        total = None
        for i in range(some // size):
            start = source * some + i * size
            at = pl.ds(pl.multiple_of(lax.rem(start, span), size), size)
            w = weights[mine, start // span] if size == span else weights[mine, start // span, :, at]
            w = w.reshape(stack, size)
            term = jnp.dot(w, v[i * size : (i + 1) * size], preferred_element_type=jnp.float32)
            total = term if total is None else total + term
        return total

    for g in range(kv_heads):
        at = slice(g * stack, (g + 1) * stack)
        mixed[at, :] = product(me, g) + jnp.dot(
            own_weights[at, :], fresh[g], preferred_element_type=jnp.float32
        )

    def take_values(j, g):
        at = slice(g * stack, (g + 1) * stack)
        block_copy(other_shift(j), g, 1).wait_recv()
        mixed[at, :] = mixed[at, :] + product(other(j), g)

    def out_copy(g):
        cols = slice(g * stack, (g + 1) * stack)
        return pltpu.make_async_copy(out.at[:, cols], out_hbm.at[0, :, cols], out_sem.at[g])

    early = slots - 3
    for j in range(early):
        for g in range(kv_heads):
            take_values(j, g)
    for g in range(kv_heads):
        for j in range(early, slots - 2):
            take_values(j, g)
        block_copy(other_shift(slots - 2), g, 1).wait_recv()
        at = slice(g * stack, (g + 1) * stack)
        done = (mixed[at, :] + product(other(slots - 2), g)) * totals[at, :]
        for h in range(sharing):
            first = (g * sharing + h) * HD
            out[:, first : first + HD] = done[h * rows : (h + 1) * rows].astype(out.dtype)
        out_copy(g).start()

    def drain(k):
        strip_copy(k).wait_send()
        for d in range(1, peers):
            spread_copy(k, d).wait_send()

    each(slots, drain, 1)

    def drain_blocks(k):
        for i in range(2 * kv_heads):
            block_copy(k, i // 2, i % 2).wait_send()

    each(slots, drain_blocks, 1)
    each(steps, drain_sums)
    for g in range(kv_heads):
        out_copy(g).wait()


def per_device(hidden, query_weight, keyvalue_weight, block_store, block_ids, offsets, served):
    slots = lax.axis_size("store")
    peers = lax.axis_size("mp")
    rows, model = hidden.shape[1:]
    share, kv_cols = block_store.shape[1:]
    q_cols = query_weight.shape[1]
    heads = q_cols // HD
    kv_heads = kv_cols // (2 * HD)
    chunks = q_cols // kv_cols + 1
    depth = model // slots
    past = NCH * L
    span = 512
    staged = (2 * rows, span) == (share, kv_cols) and block_store.shape[0] <= heads // 2 * past // span
    starts = (np.arange(NCH)[:, None] * L + np.arange(GAP)[None, :]).reshape(-1)
    tables = np.stack(
        signed_tables(np.concatenate([np.arange(L), starts, past + GAP + np.arange(rows)]))
    )
    hbm = pl.BlockSpec(memory_space=pl.ANY)
    smem = pl.BlockSpec(memory_space=pltpu.SMEM)
    dma = pltpu.SemaphoreType.DMA
    return pl.pallas_call(
        functools.partial(serve_body, slots, peers, heads, kv_heads),
        out_shape=jax.ShapeDtypeStruct((1, rows, q_cols), jnp.bfloat16),
        in_specs=[smem] * 3 + [hbm] * 5,
        out_specs=hbm,
        scratch_shapes=[
            pltpu.VMEM((slots, rows, depth), jnp.bfloat16),
            pltpu.VMEM(query_weight.shape, jnp.bfloat16),
            pltpu.VMEM(keyvalue_weight.shape, jnp.bfloat16),
            pltpu.VMEM((chunks, slots, rows, kv_cols), jnp.float32),
            pltpu.VMEM((slots + 1, chunks, 3 * rows // 2, kv_cols), jnp.int16),
            pltpu.VMEM((slots, 8, HD), jnp.float32),
            pltpu.VMEM((slots + 1, 8, HD), jnp.float32),
            pltpu.VMEM((slots + 1, 8, HD), jnp.float32),
            pltpu.VMEM((slots, NCH, share, kv_cols), jnp.bfloat16),
            pltpu.VMEM((kv_heads, past + rows, HD), jnp.bfloat16),
            pltpu.VMEM((kv_heads, rows, HD), jnp.bfloat16),
            pltpu.VMEM((heads * rows, HD), jnp.bfloat16),
            pltpu.VMEM((2 * rows, past), jnp.float32),
            pltpu.VMEM((heads // 2, past // span, 2 * rows, span), jnp.bfloat16),
            pltpu.VMEM((heads * rows, rows), jnp.bfloat16),
            None if staged else pltpu.VMEM(block_store.shape, jnp.bfloat16),
            pltpu.VMEM((slots, NCH, share, kv_cols), jnp.bfloat16),
            pltpu.VMEM((heads * rows, HD), jnp.float32),
            pltpu.VMEM((heads * rows, HD), jnp.float32),
            pltpu.VMEM(tables.shape, jnp.float32),
            pltpu.VMEM((rows, q_cols), jnp.bfloat16),
            dma((3,)),
            dma((1,)),
            dma((heads // 2,)),
            dma((kv_heads,)),
            dma((slots,)),
            dma((slots,)),
            dma((slots, peers)),
            dma((slots, peers)),
            dma((slots, 2 * kv_heads)),
            dma((slots, 2 * kv_heads)),
            dma((slots + 1, chunks)),
            dma((slots + 1, chunks)),
            dma((slots + 1,)),
            dma((slots + 1,)),
        ],
        compiler_params=pltpu.CompilerParams(
            vmem_limit_bytes=63 << 20, collective_id=0, has_side_effects=True
        ),
        name="serve",
    )(block_ids, served, offsets, hidden, query_weight, keyvalue_weight, block_store, tables)


def solution(mesh):
    in_specs = (
        P(("groups", "store"), None, None),
        P("store", "mp"),
        P("store", "mp"),
        P("groups", "store", "mp"),
        P("groups", None),
        P("groups", None),
        P("groups"),
    )
    out_specs = P(("groups", "store"), None, "mp")
    return jax.shard_map(
        per_device, mesh=mesh, in_specs=in_specs, out_specs=out_specs, check_vma=False
    )
```

```python
import functools
import math

import jax
import jax.numpy as jnp
import numpy as np
from jax import lax
from jax.experimental import pallas as pl
from jax.experimental.pallas import tpu as pltpu
from jax.sharding import PartitionSpec as P

HD = 128
HALF = HD // 2
NCH = 4
L = 1024
GAP = 64
BASE = 500000.0


def periods():
    inverse = np.exp(
        np.arange(HALF, dtype=np.float32) * np.float32(-2.0 * math.log(BASE) / HD)
    ).astype(np.float32)
    return np.floor(np.float32(2.0 * math.pi) / inverse + np.float32(0.5)).astype(np.float64)


def signed_tables(positions):
    period = periods()[None, :]
    angles = np.mod(np.asarray(positions, np.float64)[:, None], period) / period * (2.0 * math.pi)
    cos, sin = np.cos(angles), np.sin(angles)
    return (
        np.concatenate([cos, cos], axis=1).astype(np.float32),
        np.concatenate([-sin, sin], axis=1).astype(np.float32),
    )


def turn(x, cos, sin):
    return x * cos + pltpu.roll(x, HALF, 1) * sin


MESH = pl.DeviceIdType.MESH
STEPS = 2097000.0
LEAST = 1e-30
LOW = 6
BANDS = 8
PACKED = 3


def pack(low):
    words = (
        low[0] | (low[1] << 6) | ((low[2] & 15) << 12),
        (low[2] >> 4) | (low[3] << 2) | (low[4] << 8) | ((low[5] & 3) << 14),
        (low[5] >> 2) | (low[6] << 4) | (low[7] << 10),
    )
    return [(word - 32768).astype(jnp.int16) for word in words]


def unpack(words):
    a, b, c = [word.astype(jnp.int32) + 32768 for word in words]
    return (
        a & 63, (a >> 6) & 63, (a >> 12) | ((b & 3) << 4), (b >> 2) & 63,
        (b >> 8) & 63, (b >> 14) | ((c & 15) << 2), (c >> 4) & 63, c >> 10,
    )


def serve_body(
    slots, peers, heads, kv_heads,
    ids_ref, served_ref, offsets_ref, hidden_ref, wq_hbm, wkv_hbm, store_hbm, tables_hbm,
    out_hbm,
    tokens, wq, wkv, sums, codes, own, bounds_in, bounds_out, blocks, keys, fresh, queries, scores, weights, own_weights, stored, sending, totals, mixed, tables, out,
    load_sem, own_sem, store_sem, out_sem, a_send, a_recv, b_send, b_recv, k_send, k_recv, p_send, p_recv, s_send, s_recv,
):
    me = lax.axis_index("store")
    part = lax.axis_index("mp")
    rows = hidden_ref.shape[1]
    depth = tokens.shape[2]
    chunks, _, _, width = sums.shape
    share = blocks.shape[2]
    sharing = heads // kv_heads
    past = NCH * L
    strip = rows // peers

    def each(count, body, first=0):
        def step(i, carry):
            body(i)
            return carry

        lax.fori_loop(first, count, step, 0)

    if stored is None:
        several = weights.shape[1]
        store_loads = [
            pltpu.make_async_copy(
                store_hbm.at[pl.ds(i * several, several)], weights.at[i], store_sem.at[i]
            )
            for i in range(store_hbm.shape[0] // several)
        ]
    else:
        store_loads = [pltpu.make_async_copy(store_hbm, stored, store_sem.at[0])]
    for load in store_loads:
        load.start()

    def pick(s, target):
        request = served_ref[s]

        def one(c):
            block = ids_ref[request, c]
            if stored is None:
                target[s, c] = weights[block // several, block % several]
            else:
                target[s, c] = stored[block]

        each(NCH, one)

    barrier = pltpu.get_barrier_semaphore()
    for k in range(1, slots):
        pl.semaphore_signal(
            barrier, inc=1, device_id={"store": lax.rem(me + k, slots)}, device_id_type=MESH
        )
    for k in range(1, peers):
        pl.semaphore_signal(
            barrier, inc=1, device_id={"mp": lax.rem(part + k, peers)}, device_id_type=MESH
        )
    loads = [
        pltpu.make_async_copy(wq_hbm, wq, load_sem.at[0]),
        pltpu.make_async_copy(wkv_hbm, wkv, load_sem.at[1]),
        pltpu.make_async_copy(
            hidden_ref.at[0, :, pl.ds(pl.multiple_of(me * depth, depth), depth)],
            tokens.at[me], load_sem.at[2],
        ),
    ]
    tables_copy = pltpu.make_async_copy(tables_hbm, tables, own_sem.at[0])
    pl.semaphore_wait(barrier, slots + peers - 2)

    def strip_copy(k):
        to = lax.rem(me + k, slots)
        mine = pl.ds(pl.multiple_of(part * strip, strip), strip)
        return pltpu.make_async_remote_copy(
            src_ref=hidden_ref.at[0, mine, pl.ds(pl.multiple_of(to * depth, depth), depth)],
            dst_ref=tokens.at[me, mine, :],
            send_sem=a_send.at[k],
            recv_sem=a_recv.at[k],
            device_id={"store": to},
            device_id_type=MESH,
        )

    def spread_copy(k, d):
        source = lax.rem(me - k + slots, slots)
        mine = pl.ds(pl.multiple_of(part * strip, strip), strip)
        return pltpu.make_async_remote_copy(
            src_ref=tokens.at[source, mine, :],
            dst_ref=tokens.at[source, mine, :],
            send_sem=b_send.at[k, d],
            recv_sem=b_recv.at[k, d],
            device_id={"mp": lax.rem(part + d, peers)},
            device_id_type=MESH,
        )

    def block_copy(k, g, v):
        to = lax.rem(me + k, slots)
        cols = pl.ds(pl.multiple_of((2 * g + v) * HD, HD), HD)
        return pltpu.make_async_remote_copy(
            src_ref=sending.at[to, :, :, cols],
            dst_ref=blocks.at[me, :, :, cols],
            send_sem=k_send.at[k, 2 * g + v],
            recv_sem=k_recv.at[k, 2 * g + v],
            device_id={"store": to},
            device_id_type=MESH,
        )

    low = me < slots // 2

    mirrored = jnp.where(low, me, slots - 1 - me)

    def other(j):
        far = jnp.where(mirrored == 0, 0, slots - 2 - mirrored)
        source = jnp.where(
            j < far, slots - 1 - j, jnp.where(j < far + mirrored, j - far, mirrored + 1 + jnp.where(mirrored == 0, j, 0))
        )
        return jnp.where(low, source, slots - 1 - source)

    def other_shift(j):
        return lax.rem(me - other(j) + slots, slots)

    def send_blocks(v, up):
        def one(j):
            d = slots - 1 - j
            fits = (me + d < slots) if up else (me >= d)

            @pl.when(fits)
            def _():
                for g in range(kv_heads):
                    block_copy(d if up else slots - d, g, v).start()

        each(slots - 1, one)

    def sum_copy(s, q, up):
        index = s + 1 if up else s
        return pltpu.make_async_remote_copy(
            src_ref=codes.at[index, q],
            dst_ref=codes.at[index, q],
            send_sem=p_send.at[index, q],
            recv_sem=p_recv.at[index, q],
            device_id={"store": lax.rem(me + 1, slots) if up else lax.rem(me + slots - 1, slots)},
            device_id_type=MESH,
        )

    def bound_copy(s, up):
        index = s + 1 if up else s
        return pltpu.make_async_remote_copy(
            src_ref=bounds_out.at[index],
            dst_ref=bounds_in.at[index],
            send_sem=s_send.at[index],
            recv_sem=s_recv.at[index],
            device_id={"store": lax.rem(me + 1, slots) if up else lax.rem(me + slots - 1, slots)},
            device_id_type=MESH,
        )

    tall = rows // BANDS
    bands = [slice(i * tall, (i + 1) * tall) for i in range(BANDS)]
    extra = [slice(rows + i * tall, rows + (i + 1) * tall) for i in range(PACKED)]

    def columns_of(i):
        return pl.ds(pl.multiple_of(i * HD, HD), HD)

    def add_codes(q, s, index):
        step = bounds_in[index][:1, :1] * (1.0 / STEPS)

        def some(i):
            at = columns_of(i)
            low = unpack([codes[index, q, band, at] for band in extra])
            for band, part in zip(bands, low):
                value = (codes[index, q, band, at].astype(jnp.int32) << LOW) | part
                sums[q, s, band, at] = sums[q, s, band, at] + value.astype(jnp.float32) * step

        each(width // HD, some)

    def make_codes(q, s, index):
        factor = STEPS / jnp.maximum(bounds_out[index][:1, :1], LEAST)

        def some(i):
            at = columns_of(i)
            low = []
            for band in bands:
                value = jnp.round(sums[q, s, band, at] * factor).astype(jnp.int32)
                codes[index, q, band, at] = (value >> LOW).astype(jnp.int16)
                low.append(value & 63)
            for band, word in zip(extra, pack(low)):
                codes[index, q, band, at] = word

        each(width // HD, some)

    def forward(q, s, up, begins):
        index = s + 1 if up else s

        @pl.when(q == 0)
        def _():
            @pl.when(begins)
            def _():
                bounds_out[index] = own[s]

            @pl.when(jnp.logical_not(begins))
            def _():
                bound_copy(s, up).wait_recv()
                bounds_out[index] = own[s] + bounds_in[index]

            bound_copy(s, up).start()

        @pl.when(jnp.logical_not(begins))
        def _():
            sum_copy(s, q, up).wait_recv()
            add_codes(q, s, index)

        make_codes(q, s, index)
        sum_copy(s, q, up).start()

    each(slots, lambda k: strip_copy(k).start(), 1)
    for load in loads:
        load.start()
    tables_copy.start()
    for load in store_loads:
        load.wait()

    def send_keys(j):
        d = slots - 1 - j
        for up in (True, False):
            to = me + d if up else me - d

            @pl.when((to < slots) if up else (to >= 0))
            def _():
                pick(to, sending)
                for g in range(kv_heads):
                    block_copy(d if up else slots - d, g, 0).start()

    each(slots - 1, send_keys)
    pick(me, blocks)

    @pl.when(low)
    def _():
        send_blocks(1, False)

    @pl.when(jnp.logical_not(low))
    def _():
        send_blocks(1, True)


    def spread(k):
        strip_copy(k).wait_recv()
        for d in range(1, peers):
            spread_copy(k, d).start()

    each(slots, spread, 1)

    def spread_wait(k):
        for d in range(1, peers):
            spread_copy(k, d).wait_recv()

    each(slots, spread_wait, 1)
    for load in loads:
        load.wait()

    group = 4 if slots % 4 == 0 else 1

    def project(q, panel):
        def some(i):
            t = tokens[pl.ds(i * group, group)].reshape(group * rows, depth)
            sums[q, pl.ds(i * group, group)] = jnp.dot(
                t, panel, preferred_element_type=jnp.float32
            ).reshape(group, rows, width)

        each(slots // group, some)

    def relay_up(k, q):
        @pl.when(slots - 1 - k > me)
        def _():
            forward(q, slots - 1 - k, True, me == 0)

    def relay_down(k, q):
        @pl.when(k < me)
        def _():
            forward(q, k, False, me == slots - 1)

    for q in range(chunks):
        if q < chunks - 1:
            project(q, wq[:, q * width : (q + 1) * width])
        else:
            project(q, wkv[...])

    def measure(s):
        largest = jnp.zeros((8, width), jnp.float32)
        for q in range(chunks):
            largest = jnp.maximum(
                largest, jnp.max(jnp.abs(sums[q, s]).reshape(rows // 8, 8, width), axis=0)
            )
        own[s] = jnp.broadcast_to(jnp.max(largest, keepdims=True), own.shape[1:])

    each(slots, measure)

    steps = (slots - 1) * chunks

    def relay(i):
        def at(i, move):
            @pl.when((i >= 0) & (i < steps))
            def _():
                move(i // chunks, i % chunks)

        @pl.when(low)
        def _():
            at(i, relay_up)
            at(i - chunks, relay_down)

        @pl.when(jnp.logical_not(low))
        def _():
            at(i, relay_down)
            at(i - chunks, relay_up)

    each(steps + chunks, relay)

    @pl.when(low)
    def _():
        send_blocks(1, True)

    @pl.when(jnp.logical_not(low))
    def _():
        send_blocks(1, False)

    def drain_sums(i):
        k, q = i // chunks, i % chunks

        @pl.when(slots - 1 - k > me)
        def _():
            sum_copy(slots - 1 - k, q, True).wait_send()

            @pl.when(q == 0)
            def _():
                bound_copy(slots - 1 - k, True).wait_send()

        @pl.when(k < me)
        def _():
            sum_copy(k, q, False).wait_send()

            @pl.when(q == 0)
            def _():
                bound_copy(k, False).wait_send()

    def rotate_share(source):
        at_t = pl.multiple_of(source * share, share)
        tc, ts = tables[0, pl.ds(at_t, share), :], tables[1, pl.ds(at_t, share), :]

        def one(c):
            at_k = pl.multiple_of((source * NCH + c) * share, share)
            jitter = jnp.clip(offsets_ref[served_ref[me], c] - c * L, 0, GAP - 1)
            start = L + c * GAP + jitter
            oc, os = tables[0, pl.ds(start, 1), :], tables[1, pl.ds(start, 1), :]
            cos = tc * oc - ts * os
            sin = ts * oc + tc * os
            for g in range(kv_heads):
                at = g * 2 * HD
                x = blocks[source, c, :, at : at + HD].astype(jnp.float32)
                keys[g, pl.ds(at_k, share), :] = turn(x, cos, sin).astype(jnp.bfloat16)

        each(NCH, one)

    tables_copy.wait()
    rotate_share(me)

    def take(j):
        for g in range(kv_heads):
            block_copy(other_shift(j), g, 0).wait_recv()
        rotate_share(other(j))

    each(slots - 1, take)

    @pl.when(me > 0)
    def _():
        bound_copy(me, True).wait_recv()

    @pl.when(me < slots - 1)
    def _():
        bound_copy(me, False).wait_recv()

    def settle(q):
        @pl.when(me > 0)
        def _():
            sum_copy(me, q, True).wait_recv()
            add_codes(q, me, me + 1)

        @pl.when(me < slots - 1)
        def _():
            sum_copy(me, q, False).wait_recv()
            add_codes(q, me, me)

    each(chunks, settle)

    at_q = L + NCH * GAP
    qc, qs = tables[0, at_q : at_q + rows, :], tables[1, at_q : at_q + rows, :]
    for g in range(kv_heads):
        at = g * 2 * HD
        keys[g, past:, :] = turn(sums[chunks - 1, me, :, at : at + HD], qc, qs).astype(jnp.bfloat16)
        fresh[g] = sums[chunks - 1, me, :, at + HD : at + 2 * HD].astype(jnp.bfloat16)
    for h in range(heads):
        q, at = divmod(h * HD, width)
        queries[h * rows : (h + 1) * rows, :] = turn(
            sums[q, me, :, at : at + HD], qc, qs
        ).astype(jnp.bfloat16)

    block = 2 * rows
    span = weights.shape[3]
    factor = math.log2(math.e) / math.sqrt(HD)
    lower = lax.broadcasted_iota(jnp.int32, (block, rows), 0) % rows >= lax.broadcasted_iota(
        jnp.int32, (block, rows), 1
    )
    contract = (((1,), (1,)), ((), ()))

    def weigh(b):
        g = (b * 2) // sharing
        at = pl.ds(pl.multiple_of(b * block, block), block)
        q = queries[at, :]
        own = lax.dot_general(q, keys[g, past:, :], contract, preferred_element_type=jnp.float32)
        own = jnp.where(lower, own, -jnp.inf)
        top = own
        for j in range(past // span):
            s = lax.dot_general(
                q, keys[g, j * span : (j + 1) * span, :], contract,
                preferred_element_type=jnp.float32,
            )
            scores[:, j * span : (j + 1) * span] = s
            for k in range(span // HD):
                top = jnp.maximum(top, s[:, k * HD : (k + 1) * HD])
        top = jnp.max(top, axis=1, keepdims=True)
        w = jnp.exp2((own - top) * factor)
        total = w
        own_weights[at, :] = w.astype(jnp.bfloat16)
        for j in range(past // span):
            w = jnp.exp2((scores[:, j * span : (j + 1) * span] - top) * factor)
            for k in range(span // HD):
                total = total + w[:, k * HD : (k + 1) * HD]
            weights[b, j] = w.astype(jnp.bfloat16)
        totals[at, :] = total

    each(heads // 2, weigh)

    stack = sharing * rows
    some = NCH * share

    def invert(h):
        at = pl.ds(pl.multiple_of(h * rows, rows), rows)
        totals[at, :] = jnp.broadcast_to(
            1.0 / jnp.sum(totals[at, :], axis=1, keepdims=True), (rows, HD)
        )

    each(heads, invert)

    pairs = sharing // 2

    def product(source, g):
        v = blocks[source, :, :, (2 * g + 1) * HD : (2 * g + 2) * HD].reshape(some, HD)
        mine = slice(g * pairs, (g + 1) * pairs)
        size = min(some, span)
        total = None
        for i in range(some // size):
            start = source * some + i * size
            at = pl.ds(pl.multiple_of(lax.rem(start, span), size), size)
            w = weights[mine, start // span] if size == span else weights[mine, start // span, :, at]
            w = w.reshape(stack, size)
            term = jnp.dot(w, v[i * size : (i + 1) * size], preferred_element_type=jnp.float32)
            total = term if total is None else total + term
        return total

    for g in range(kv_heads):
        at = slice(g * stack, (g + 1) * stack)
        mixed[at, :] = product(me, g) + jnp.dot(
            own_weights[at, :], fresh[g], preferred_element_type=jnp.float32
        )

    def take_values(j, g):
        at = slice(g * stack, (g + 1) * stack)
        block_copy(other_shift(j), g, 1).wait_recv()
        mixed[at, :] = mixed[at, :] + product(other(j), g)

    def out_copy(g):
        cols = slice(g * stack, (g + 1) * stack)
        return pltpu.make_async_copy(out.at[:, cols], out_hbm.at[0, :, cols], out_sem.at[g])

    early = slots - 3
    for j in range(early):
        for g in range(kv_heads):
            take_values(j, g)
    for g in range(kv_heads):
        for j in range(early, slots - 2):
            take_values(j, g)
        block_copy(other_shift(slots - 2), g, 1).wait_recv()
        at = slice(g * stack, (g + 1) * stack)
        done = (mixed[at, :] + product(other(slots - 2), g)) * totals[at, :]
        for h in range(sharing):
            first = (g * sharing + h) * HD
            out[:, first : first + HD] = done[h * rows : (h + 1) * rows].astype(out.dtype)
        out_copy(g).start()

    def drain(k):
        strip_copy(k).wait_send()
        for d in range(1, peers):
            spread_copy(k, d).wait_send()

    each(slots, drain, 1)

    def drain_blocks(k):
        for i in range(2 * kv_heads):
            block_copy(k, i // 2, i % 2).wait_send()

    each(slots, drain_blocks, 1)
    each(steps, drain_sums)
    for g in range(kv_heads):
        out_copy(g).wait()


def per_device(hidden, query_weight, keyvalue_weight, block_store, block_ids, offsets, served):
    slots = lax.axis_size("store")
    peers = lax.axis_size("mp")
    rows, model = hidden.shape[1:]
    share, kv_cols = block_store.shape[1:]
    q_cols = query_weight.shape[1]
    heads = q_cols // HD
    kv_heads = kv_cols // (2 * HD)
    chunks = q_cols // kv_cols + 1
    depth = model // slots
    past = NCH * L
    span = 512
    staged = (2 * rows, span) == (share, kv_cols) and block_store.shape[0] <= heads // 2 * past // span
    starts = (np.arange(NCH)[:, None] * L + np.arange(GAP)[None, :]).reshape(-1)
    tables = np.stack(
        signed_tables(np.concatenate([np.arange(L), starts, past + GAP + np.arange(rows)]))
    )
    hbm = pl.BlockSpec(memory_space=pl.ANY)
    smem = pl.BlockSpec(memory_space=pltpu.SMEM)
    dma = pltpu.SemaphoreType.DMA
    return pl.pallas_call(
        functools.partial(serve_body, slots, peers, heads, kv_heads),
        out_shape=jax.ShapeDtypeStruct((1, rows, q_cols), jnp.bfloat16),
        in_specs=[smem] * 3 + [hbm] * 5,
        out_specs=hbm,
        scratch_shapes=[
            pltpu.VMEM((slots, rows, depth), jnp.bfloat16),
            pltpu.VMEM(query_weight.shape, jnp.bfloat16),
            pltpu.VMEM(keyvalue_weight.shape, jnp.bfloat16),
            pltpu.VMEM((chunks, slots, rows, kv_cols), jnp.float32),
            pltpu.VMEM((slots + 1, chunks, rows + rows // BANDS * PACKED, kv_cols), jnp.int16),
            pltpu.VMEM((slots, 8, HD), jnp.float32),
            pltpu.VMEM((slots + 1, 8, HD), jnp.float32),
            pltpu.VMEM((slots + 1, 8, HD), jnp.float32),
            pltpu.VMEM((slots, NCH, share, kv_cols), jnp.bfloat16),
            pltpu.VMEM((kv_heads, past + rows, HD), jnp.bfloat16),
            pltpu.VMEM((kv_heads, rows, HD), jnp.bfloat16),
            pltpu.VMEM((heads * rows, HD), jnp.bfloat16),
            pltpu.VMEM((2 * rows, past), jnp.float32),
            pltpu.VMEM((heads // 2, past // span, 2 * rows, span), jnp.bfloat16),
            pltpu.VMEM((heads * rows, rows), jnp.bfloat16),
            None if staged else pltpu.VMEM(block_store.shape, jnp.bfloat16),
            pltpu.VMEM((slots, NCH, share, kv_cols), jnp.bfloat16),
            pltpu.VMEM((heads * rows, HD), jnp.float32),
            pltpu.VMEM((heads * rows, HD), jnp.float32),
            pltpu.VMEM(tables.shape, jnp.float32),
            pltpu.VMEM((rows, q_cols), jnp.bfloat16),
            dma((3,)),
            dma((1,)),
            dma((heads // 2,)),
            dma((kv_heads,)),
            dma((slots,)),
            dma((slots,)),
            dma((slots, peers)),
            dma((slots, peers)),
            dma((slots, 2 * kv_heads)),
            dma((slots, 2 * kv_heads)),
            dma((slots + 1, chunks)),
            dma((slots + 1, chunks)),
            dma((slots + 1,)),
            dma((slots + 1,)),
        ],
        compiler_params=pltpu.CompilerParams(
            vmem_limit_bytes=63 << 20, collective_id=0, has_side_effects=True
        ),
        name="serve",
    )(block_ids, served, offsets, hidden, query_weight, keyvalue_weight, block_store, tables)


def solution(mesh):
    in_specs = (
        P(("groups", "store"), None, None),
        P("store", "mp"),
        P("store", "mp"),
        P("groups", "store", "mp"),
        P("groups", None),
        P("groups", None),
        P("groups"),
    )
    out_specs = P(("groups", "store"), None, "mp")
    return jax.shard_map(
        per_device, mesh=mesh, in_specs=in_specs, out_specs=out_specs, check_vma=False
    )
```

```python
import functools
import math

import jax
import jax.numpy as jnp
import numpy as np
from jax import lax
from jax.experimental import pallas as pl
from jax.experimental.pallas import tpu as pltpu
from jax.sharding import PartitionSpec as P

HD = 128
HALF = HD // 2
NCH = 4
L = 1024
GAP = 64
BASE = 500000.0


def periods():
    inverse = np.exp(
        np.arange(HALF, dtype=np.float32) * np.float32(-2.0 * math.log(BASE) / HD)
    ).astype(np.float32)
    return np.floor(np.float32(2.0 * math.pi) / inverse + np.float32(0.5)).astype(np.float64)


def signed_tables(positions):
    period = periods()[None, :]
    angles = np.mod(np.asarray(positions, np.float64)[:, None], period) / period * (2.0 * math.pi)
    cos, sin = np.cos(angles), np.sin(angles)
    return (
        np.concatenate([cos, cos], axis=1).astype(np.float32),
        np.concatenate([-sin, sin], axis=1).astype(np.float32),
    )


def turn(x, cos, sin):
    return x * cos + pltpu.roll(x, HALF, 1) * sin


MESH = pl.DeviceIdType.MESH
STEPS = 2097000.0
LEAST = 1e-30
LOW = 6
BANDS = 8
PACKED = 3


def pack(low):
    words = (
        low[0] | (low[1] << 6) | ((low[2] & 15) << 12),
        (low[2] >> 4) | (low[3] << 2) | (low[4] << 8) | ((low[5] & 3) << 14),
        (low[5] >> 2) | (low[6] << 4) | (low[7] << 10),
    )
    return [(word - 32768).astype(jnp.int16) for word in words]


def unpack(words):
    a, b, c = [word.astype(jnp.int32) + 32768 for word in words]
    return (
        a & 63, (a >> 6) & 63, (a >> 12) | ((b & 3) << 4), (b >> 2) & 63,
        (b >> 8) & 63, (b >> 14) | ((c & 15) << 2), (c >> 4) & 63, c >> 10,
    )


def serve_body(
    slots, peers, heads, kv_heads,
    ids_hbm, served_hbm, offsets_hbm, hidden_ref, wq_hbm, wkv_hbm, store_hbm, tables_hbm,
    out_hbm,
    ids_ref, served_ref, offsets_ref, tokens, wq, wkv, sums, codes, own, bounds_in, bounds_out, blocks, keys, fresh, queries, scores, weights, own_weights, stored, sending, totals, mixed, tables, out,
    small_sem, load_sem, own_sem, store_sem, out_sem, a_send, a_recv, b_send, b_recv, k_send, k_recv, p_send, p_recv, s_send, s_recv,
):
    me = lax.axis_index("store")
    part = lax.axis_index("mp")
    rows = hidden_ref.shape[1]
    depth = tokens.shape[2]
    chunks, _, _, width = sums.shape
    share = blocks.shape[2]
    sharing = heads // kv_heads
    past = NCH * L
    span = weights.shape[3]
    parts = 2 if NCH // 2 * share % span == 0 else 1
    some = NCH // parts
    strip = rows // peers

    def each(count, body, first=0):
        def step(i, carry):
            body(i)
            return carry

        lax.fori_loop(first, count, step, 0)

    small = [
        pltpu.make_async_copy(source, target, small_sem.at[i])
        for i, (source, target) in enumerate(
            ((ids_hbm, ids_ref), (served_hbm, served_ref), (offsets_hbm, offsets_ref))
        )
    ]
    for load in small:
        load.start()

    if stored is None:
        several = weights.shape[1]
        store_loads = [
            pltpu.make_async_copy(
                store_hbm.at[pl.ds(i * several, several)], weights.at[i], store_sem.at[i]
            )
            for i in range(store_hbm.shape[0] // several)
        ]
    else:
        store_loads = [pltpu.make_async_copy(store_hbm, stored, store_sem.at[0])]
    for load in store_loads:
        load.start()

    def pick(s, target):
        request = served_ref[s]

        def one(c):
            block = ids_ref[request, c]
            if stored is None:
                target[s, c] = weights[block // several, block % several]
            else:
                target[s, c] = stored[block]

        each(NCH, one)

    barrier = pltpu.get_barrier_semaphore()
    for k in range(1, slots):
        pl.semaphore_signal(
            barrier, inc=1, device_id={"store": lax.rem(me + k, slots)}, device_id_type=MESH
        )
    for k in range(1, peers):
        pl.semaphore_signal(
            barrier, inc=1, device_id={"mp": lax.rem(part + k, peers)}, device_id_type=MESH
        )
    loads = [
        pltpu.make_async_copy(wq_hbm, wq, load_sem.at[0]),
        pltpu.make_async_copy(wkv_hbm, wkv, load_sem.at[1]),
        pltpu.make_async_copy(
            hidden_ref.at[0, :, pl.ds(pl.multiple_of(me * depth, depth), depth)],
            tokens.at[me], load_sem.at[2],
        ),
    ]
    tables_copy = pltpu.make_async_copy(tables_hbm, tables, own_sem.at[0])
    pl.semaphore_wait(barrier, slots + peers - 2)

    def strip_copy(k):
        to = lax.rem(me + k, slots)
        mine = pl.ds(pl.multiple_of(part * strip, strip), strip)
        return pltpu.make_async_remote_copy(
            src_ref=hidden_ref.at[0, mine, pl.ds(pl.multiple_of(to * depth, depth), depth)],
            dst_ref=tokens.at[me, mine, :],
            send_sem=a_send.at[k],
            recv_sem=a_recv.at[k],
            device_id={"store": to},
            device_id_type=MESH,
        )

    def spread_copy(k, d):
        source = lax.rem(me - k + slots, slots)
        mine = pl.ds(pl.multiple_of(part * strip, strip), strip)
        return pltpu.make_async_remote_copy(
            src_ref=tokens.at[source, mine, :],
            dst_ref=tokens.at[source, mine, :],
            send_sem=b_send.at[k, d],
            recv_sem=b_recv.at[k, d],
            device_id={"mp": lax.rem(part + d, peers)},
            device_id_type=MESH,
        )

    def block_copy(k, g, piece):
        to = lax.rem(me + k, slots)
        cols = pl.ds(pl.multiple_of((2 * g + min(piece, 1)) * HD, HD), HD)
        chosen = slice(0, NCH) if piece == 0 else slice((piece - 1) * some, piece * some)
        return pltpu.make_async_remote_copy(
            src_ref=sending.at[to, chosen, :, cols],
            dst_ref=blocks.at[me, chosen, :, cols],
            send_sem=k_send.at[k, (1 + parts) * g + piece],
            recv_sem=k_recv.at[k, (1 + parts) * g + piece],
            device_id={"store": to},
            device_id_type=MESH,
        )

    low = me < slots // 2

    mirrored = jnp.where(low, me, slots - 1 - me)

    def other(j):
        far = jnp.where(mirrored == 0, 0, slots - 2 - mirrored)
        source = jnp.where(
            j < far, slots - 1 - j, jnp.where(j < far + mirrored, j - far, mirrored + 1 + jnp.where(mirrored == 0, j, 0))
        )
        return jnp.where(low, source, slots - 1 - source)

    def other_shift(j):
        return lax.rem(me - other(j) + slots, slots)

    def send_values(up):
        def one(j):
            d = slots - 1 - j
            fits = (me + d < slots) if up else (me >= d)

            @pl.when(fits)
            def _():
                for g in range(kv_heads):
                    for piece in range(parts):
                        block_copy(d if up else slots - d, g, 1 + piece).start()

        each(slots - 1, one)

    def sum_copy(s, q, up):
        index = s + 1 if up else s
        return pltpu.make_async_remote_copy(
            src_ref=codes.at[index, q],
            dst_ref=codes.at[index, q],
            send_sem=p_send.at[index, q],
            recv_sem=p_recv.at[index, q],
            device_id={"store": lax.rem(me + 1, slots) if up else lax.rem(me + slots - 1, slots)},
            device_id_type=MESH,
        )

    def bound_copy(s, up):
        index = s + 1 if up else s
        return pltpu.make_async_remote_copy(
            src_ref=bounds_out.at[index],
            dst_ref=bounds_in.at[index],
            send_sem=s_send.at[index],
            recv_sem=s_recv.at[index],
            device_id={"store": lax.rem(me + 1, slots) if up else lax.rem(me + slots - 1, slots)},
            device_id_type=MESH,
        )

    tall = rows // BANDS
    bands = [slice(i * tall, (i + 1) * tall) for i in range(BANDS)]
    extra = [slice(rows + i * tall, rows + (i + 1) * tall) for i in range(PACKED)]

    def columns_of(i):
        return pl.ds(pl.multiple_of(i * HD, HD), HD)

    def add_codes(q, s, index):
        step = bounds_in[index, pl.ds(q, 1), :] * (1.0 / STEPS)

        def some_columns(i):
            at = columns_of(i)
            low = unpack([codes[index, q, band, at] for band in extra])
            for band, part in zip(bands, low):
                value = (codes[index, q, band, at].astype(jnp.int32) << LOW) | part
                sums[q, s, band, at] = sums[q, s, band, at] + value.astype(jnp.float32) * step

        each(width // HD, some_columns)

    def make_codes(q, s, index):
        factor = STEPS / jnp.maximum(bounds_out[index, pl.ds(q, 1), :], LEAST)

        def some_columns(i):
            at = columns_of(i)
            low = []
            for band in bands:
                value = jnp.round(sums[q, s, band, at] * factor).astype(jnp.int32)
                codes[index, q, band, at] = (value >> LOW).astype(jnp.int16)
                low.append(value & 63)
            for band, word in zip(extra, pack(low)):
                codes[index, q, band, at] = word

        each(width // HD, some_columns)

    def forward(q, s, up, begins):
        index = s + 1 if up else s

        @pl.when(q == 0)
        def _():
            @pl.when(begins)
            def _():
                bounds_out[index] = own[s]

            @pl.when(jnp.logical_not(begins))
            def _():
                bound_copy(s, up).wait_recv()
                bounds_out[index] = own[s] + bounds_in[index]

            bound_copy(s, up).start()

        @pl.when(jnp.logical_not(begins))
        def _():
            sum_copy(s, q, up).wait_recv()
            add_codes(q, s, index)

        make_codes(q, s, index)
        sum_copy(s, q, up).start()

    each(slots, lambda k: strip_copy(k).start(), 1)
    for load in loads:
        load.start()
    tables_copy.start()
    for load in small + store_loads:
        load.wait()

    def send_keys(j):
        d = slots - 1 - j
        for up in (True, False):
            to = me + d if up else me - d

            @pl.when((to < slots) if up else (to >= 0))
            def _():
                pick(to, sending)
                for g in range(kv_heads):
                    block_copy(d if up else slots - d, g, 0).start()

    each(slots - 1, send_keys)
    pick(me, blocks)

    @pl.when(low)
    def _():
        send_values(False)

    @pl.when(jnp.logical_not(low))
    def _():
        send_values(True)


    def spread(k):
        strip_copy(k).wait_recv()
        for d in range(1, peers):
            spread_copy(k, d).start()

    each(slots, spread, 1)

    def spread_wait(k):
        for d in range(1, peers):
            spread_copy(k, d).wait_recv()

    each(slots, spread_wait, 1)
    for load in loads:
        load.wait()

    group = 4 if slots % 4 == 0 else 1

    def project(q, panel):
        def some_slots(i):
            t = tokens[pl.ds(i * group, group)].reshape(group * rows, depth)
            sums[q, pl.ds(i * group, group)] = jnp.dot(
                t, panel, preferred_element_type=jnp.float32
            ).reshape(group, rows, width)

        each(slots // group, some_slots)

    def relay_up(k, q):
        @pl.when(slots - 1 - k > me)
        def _():
            forward(q, slots - 1 - k, True, me == 0)

    def relay_down(k, q):
        @pl.when(k < me)
        def _():
            forward(q, k, False, me == slots - 1)

    for q in range(chunks):
        if q < chunks - 1:
            project(q, wq[:, q * width : (q + 1) * width])
        else:
            project(q, wkv[...])

    def measure(s):
        own[s] = jnp.zeros(own.shape[1:], jnp.float32)
        for q in range(chunks):
            largest = jnp.max(jnp.abs(sums[q, s]), keepdims=True)
            own[s, q : q + 1, :] = jnp.broadcast_to(largest, (1, HD))

    each(slots, measure)

    steps = (slots - 1) * chunks

    def relay(i):
        def at(i, move):
            @pl.when((i >= 0) & (i < steps))
            def _():
                move(i // chunks, i % chunks)

        @pl.when(low)
        def _():
            at(i, relay_up)
            at(i - chunks, relay_down)

        @pl.when(jnp.logical_not(low))
        def _():
            at(i, relay_down)
            at(i - chunks, relay_up)

    each(steps + chunks, relay)

    @pl.when(low)
    def _():
        send_values(True)

    @pl.when(jnp.logical_not(low))
    def _():
        send_values(False)

    def drain_sums(i):
        k, q = i // chunks, i % chunks

        @pl.when(slots - 1 - k > me)
        def _():
            sum_copy(slots - 1 - k, q, True).wait_send()

            @pl.when(q == 0)
            def _():
                bound_copy(slots - 1 - k, True).wait_send()

        @pl.when(k < me)
        def _():
            sum_copy(k, q, False).wait_send()

            @pl.when(q == 0)
            def _():
                bound_copy(k, False).wait_send()

    def rotate_share(source):
        at_t = pl.multiple_of(source * share, share)
        tc, ts = tables[0, pl.ds(at_t, share), :], tables[1, pl.ds(at_t, share), :]

        def one(c):
            at_k = pl.multiple_of((source * NCH + c) * share, share)
            jitter = jnp.clip(offsets_ref[served_ref[me], c] - c * L, 0, GAP - 1)
            start = L + c * GAP + jitter
            oc, os = tables[0, pl.ds(start, 1), :], tables[1, pl.ds(start, 1), :]
            cos = tc * oc - ts * os
            sin = ts * oc + tc * os
            for g in range(kv_heads):
                at = g * 2 * HD
                x = blocks[source, c, :, at : at + HD].astype(jnp.float32)
                keys[g, pl.ds(at_k, share), :] = turn(x, cos, sin).astype(jnp.bfloat16)

        each(NCH, one)

    tables_copy.wait()
    rotate_share(me)

    def take(j):
        for g in range(kv_heads):
            block_copy(other_shift(j), g, 0).wait_recv()
        rotate_share(other(j))

    each(slots - 1, take)

    @pl.when(me > 0)
    def _():
        bound_copy(me, True).wait_recv()

    @pl.when(me < slots - 1)
    def _():
        bound_copy(me, False).wait_recv()

    def settle(q):
        @pl.when(me > 0)
        def _():
            sum_copy(me, q, True).wait_recv()
            add_codes(q, me, me + 1)

        @pl.when(me < slots - 1)
        def _():
            sum_copy(me, q, False).wait_recv()
            add_codes(q, me, me)

    each(chunks, settle)

    at_q = L + NCH * GAP
    qc, qs = tables[0, at_q : at_q + rows, :], tables[1, at_q : at_q + rows, :]
    for g in range(kv_heads):
        at = g * 2 * HD
        keys[g, past:, :] = turn(sums[chunks - 1, me, :, at : at + HD], qc, qs).astype(jnp.bfloat16)
        fresh[g] = sums[chunks - 1, me, :, at + HD : at + 2 * HD].astype(jnp.bfloat16)
    for h in range(heads):
        q, at = divmod(h * HD, width)
        queries[h * rows : (h + 1) * rows, :] = turn(
            sums[q, me, :, at : at + HD], qc, qs
        ).astype(jnp.bfloat16)

    block = 2 * rows
    factor = math.log2(math.e) / math.sqrt(HD)
    lower = lax.broadcasted_iota(jnp.int32, (block, rows), 0) % rows >= lax.broadcasted_iota(
        jnp.int32, (block, rows), 1
    )
    contract = (((1,), (1,)), ((), ()))

    def weigh(b):
        g = (b * 2) // sharing
        at = pl.ds(pl.multiple_of(b * block, block), block)
        q = queries[at, :]
        own = lax.dot_general(q, keys[g, past:, :], contract, preferred_element_type=jnp.float32)
        own = jnp.where(lower, own, -jnp.inf)
        top = own
        for j in range(past // span):
            s = lax.dot_general(
                q, keys[g, j * span : (j + 1) * span, :], contract,
                preferred_element_type=jnp.float32,
            )
            scores[:, j * span : (j + 1) * span] = s
            for k in range(span // HD):
                top = jnp.maximum(top, s[:, k * HD : (k + 1) * HD])
        top = jnp.max(top, axis=1, keepdims=True)
        w = jnp.exp2((own - top) * factor)
        total = w
        own_weights[at, :] = w.astype(jnp.bfloat16)
        for j in range(past // span):
            w = jnp.exp2((scores[:, j * span : (j + 1) * span] - top) * factor)
            for k in range(span // HD):
                total = total + w[:, k * HD : (k + 1) * HD]
            weights[b, j] = w.astype(jnp.bfloat16)
        totals[at, :] = total

    each(heads // 2, weigh)

    stack = sharing * rows

    def invert(h):
        at = pl.ds(pl.multiple_of(h * rows, rows), rows)
        totals[at, :] = jnp.broadcast_to(
            1.0 / jnp.sum(totals[at, :], axis=1, keepdims=True), (rows, HD)
        )

    each(heads, invert)

    pairs = sharing // 2

    pairs = sharing // 2
    keys_each = some * share
    size = min(keys_each, span)

    def product(source, g, piece):
        v = blocks[
            source, piece * some : (piece + 1) * some, :, (2 * g + 1) * HD : (2 * g + 2) * HD
        ].reshape(keys_each, HD)
        mine = slice(g * pairs, (g + 1) * pairs)
        total = None
        for i in range(keys_each // size):
            start = (source * parts + piece) * keys_each + i * size
            at = pl.ds(pl.multiple_of(lax.rem(start, span), size), size)
            w = weights[mine, start // span] if size == span else weights[mine, start // span, :, at]
            w = w.reshape(stack, size)
            term = jnp.dot(w, v[i * size : (i + 1) * size], preferred_element_type=jnp.float32)
            total = term if total is None else total + term
        return total

    for g in range(kv_heads):
        at = slice(g * stack, (g + 1) * stack)
        mixed[at, :] = jnp.dot(
            own_weights[at, :], fresh[g], preferred_element_type=jnp.float32
        )
        for piece in range(parts):
            mixed[at, :] = mixed[at, :] + product(me, g, piece)

    def take_value(j, g, piece):
        at = slice(g * stack, (g + 1) * stack)
        block_copy(other_shift(j), g, 1 + piece).wait_recv()
        return mixed[at, :] + product(other(j), g, piece)

    def take_values(j, g, count):
        at = slice(g * stack, (g + 1) * stack)
        for piece in range(count):
            mixed[at, :] = take_value(j, g, piece)

    def out_copy(g):
        cols = slice(g * stack, (g + 1) * stack)
        return pltpu.make_async_copy(out.at[:, cols], out_hbm.at[0, :, cols], out_sem.at[g])

    early = slots - 3
    for j in range(early):
        for g in range(kv_heads):
            take_values(j, g, parts)
    for g in range(kv_heads):
        for j in range(early, slots - 2):
            take_values(j, g, parts)
        take_values(slots - 2, g, parts - 1)
        at = slice(g * stack, (g + 1) * stack)
        done = take_value(slots - 2, g, parts - 1) * totals[at, :]
        for h in range(sharing):
            first = (g * sharing + h) * HD
            out[:, first : first + HD] = done[h * rows : (h + 1) * rows].astype(out.dtype)
        out_copy(g).start()

    def drain(k):
        strip_copy(k).wait_send()
        for d in range(1, peers):
            spread_copy(k, d).wait_send()

    each(slots, drain, 1)

    def drain_blocks(k):
        for g in range(kv_heads):
            for piece in range(1 + parts):
                block_copy(k, g, piece).wait_send()

    each(slots, drain_blocks, 1)
    each(steps, drain_sums)
    for g in range(kv_heads):
        out_copy(g).wait()


def per_device(hidden, query_weight, keyvalue_weight, block_store, block_ids, offsets, served):
    slots = lax.axis_size("store")
    peers = lax.axis_size("mp")
    rows, model = hidden.shape[1:]
    share, kv_cols = block_store.shape[1:]
    q_cols = query_weight.shape[1]
    heads = q_cols // HD
    kv_heads = kv_cols // (2 * HD)
    chunks = q_cols // kv_cols + 1
    depth = model // slots
    past = NCH * L
    span = 512
    staged = (2 * rows, span) == (share, kv_cols) and block_store.shape[0] <= heads // 2 * past // span
    starts = (np.arange(NCH)[:, None] * L + np.arange(GAP)[None, :]).reshape(-1)
    tables = np.stack(
        signed_tables(np.concatenate([np.arange(L), starts, past + GAP + np.arange(rows)]))
    )
    hbm = pl.BlockSpec(memory_space=pl.ANY)
    dma = pltpu.SemaphoreType.DMA
    return pl.pallas_call(
        functools.partial(serve_body, slots, peers, heads, kv_heads),
        out_shape=jax.ShapeDtypeStruct((1, rows, q_cols), jnp.bfloat16),
        in_specs=[hbm] * 8,
        out_specs=hbm,
        scratch_shapes=[
            pltpu.SMEM(block_ids.shape, jnp.int32),
            pltpu.SMEM(served.shape, jnp.int32),
            pltpu.SMEM(offsets.shape, jnp.int32),
            pltpu.VMEM((slots, rows, depth), jnp.bfloat16),
            pltpu.VMEM(query_weight.shape, jnp.bfloat16),
            pltpu.VMEM(keyvalue_weight.shape, jnp.bfloat16),
            pltpu.VMEM((chunks, slots, rows, kv_cols), jnp.float32),
            pltpu.VMEM((slots + 1, chunks, rows + rows // BANDS * PACKED, kv_cols), jnp.int16),
            pltpu.VMEM((slots, 8, HD), jnp.float32),
            pltpu.VMEM((slots + 1, 8, HD), jnp.float32),
            pltpu.VMEM((slots + 1, 8, HD), jnp.float32),
            pltpu.VMEM((slots, NCH, share, kv_cols), jnp.bfloat16),
            pltpu.VMEM((kv_heads, past + rows, HD), jnp.bfloat16),
            pltpu.VMEM((kv_heads, rows, HD), jnp.bfloat16),
            pltpu.VMEM((heads * rows, HD), jnp.bfloat16),
            pltpu.VMEM((2 * rows, past), jnp.float32),
            pltpu.VMEM((heads // 2, past // span, 2 * rows, span), jnp.bfloat16),
            pltpu.VMEM((heads * rows, rows), jnp.bfloat16),
            None if staged else pltpu.VMEM(block_store.shape, jnp.bfloat16),
            pltpu.VMEM((slots, NCH, share, kv_cols), jnp.bfloat16),
            pltpu.VMEM((heads * rows, HD), jnp.float32),
            pltpu.VMEM((heads * rows, HD), jnp.float32),
            pltpu.VMEM(tables.shape, jnp.float32),
            pltpu.VMEM((rows, q_cols), jnp.bfloat16),
            dma((3,)),
            dma((3,)),
            dma((1,)),
            dma((heads // 2,)),
            dma((kv_heads,)),
            dma((slots,)),
            dma((slots,)),
            dma((slots, peers)),
            dma((slots, peers)),
            dma((slots, 3 * kv_heads)),
            dma((slots, 3 * kv_heads)),
            dma((slots + 1, chunks)),
            dma((slots + 1, chunks)),
            dma((slots + 1,)),
            dma((slots + 1,)),
        ],
        compiler_params=pltpu.CompilerParams(
            vmem_limit_bytes=63 << 20, collective_id=0, has_side_effects=True
        ),
        name="serve",
    )(block_ids, served, offsets, hidden, query_weight, keyvalue_weight, block_store, tables)


def solution(mesh):
    in_specs = (
        P(("groups", "store"), None, None),
        P("store", "mp"),
        P("store", "mp"),
        P("groups", "store", "mp"),
        P("groups", None),
        P("groups", None),
        P("groups"),
    )
    out_specs = P(("groups", "store"), None, "mp")
    return jax.shard_map(
        per_device, mesh=mesh, in_specs=in_specs, out_specs=out_specs, check_vma=False
    )
```

```python
import functools
import math

import jax
import jax.numpy as jnp
import numpy as np
from jax import lax
from jax.experimental import pallas as pl
from jax.experimental.pallas import tpu as pltpu
from jax.sharding import PartitionSpec as P

HD = 128
HALF = HD // 2
NCH = 4
L = 1024
GAP = 64
BASE = 500000.0


def periods():
    inverse = np.exp(
        np.arange(HALF, dtype=np.float32) * np.float32(-2.0 * math.log(BASE) / HD)
    ).astype(np.float32)
    return np.floor(np.float32(2.0 * math.pi) / inverse + np.float32(0.5)).astype(np.float64)


def signed_tables(positions):
    period = periods()[None, :]
    angles = np.mod(np.asarray(positions, np.float64)[:, None], period) / period * (2.0 * math.pi)
    cos, sin = np.cos(angles), np.sin(angles)
    return (
        np.concatenate([cos, cos], axis=1).astype(np.float32),
        np.concatenate([-sin, sin], axis=1).astype(np.float32),
    )


def turn(x, cos, sin):
    return x * cos + pltpu.roll(x, HALF, 1) * sin


MESH = pl.DeviceIdType.MESH
STEPS = 2097000.0
LEAST = 1e-30
LOW = 6
BANDS = 8
PACKED = 3


def pack(low):
    words = (
        low[0] | (low[1] << 6) | ((low[2] & 15) << 12),
        (low[2] >> 4) | (low[3] << 2) | (low[4] << 8) | ((low[5] & 3) << 14),
        (low[5] >> 2) | (low[6] << 4) | (low[7] << 10),
    )
    return [(word - 32768).astype(jnp.int16) for word in words]


def unpack(words):
    a, b, c = [word.astype(jnp.int32) + 32768 for word in words]
    return (
        a & 63, (a >> 6) & 63, (a >> 12) | ((b & 3) << 4), (b >> 2) & 63,
        (b >> 8) & 63, (b >> 14) | ((c & 15) << 2), (c >> 4) & 63, c >> 10,
    )


def serve_body(
    slots, peers, heads, kv_heads,
    ids_hbm, served_hbm, offsets_hbm, hidden_ref, wq_hbm, wkv_hbm, store_hbm, tables_hbm,
    out_hbm,
    ids_ref, served_ref, offsets_ref, tokens, wq, wkv, sums, codes, own, bounds_in, bounds_out, blocks, keys, fresh, queries, scores, weights, own_weights, stored, sending, totals, mixed, tables, out,
    small_sem, load_sem, own_sem, store_sem, out_sem, a_send, a_recv, b_send, b_recv, k_send, k_recv, p_send, p_recv, s_send, s_recv,
):
    me = lax.axis_index("store")
    part = lax.axis_index("mp")
    rows = hidden_ref.shape[1]
    depth = tokens.shape[2]
    chunks, _, _, width = sums.shape
    share = blocks.shape[2]
    sharing = heads // kv_heads
    past = NCH * L
    span = weights.shape[3]
    parts = 2 if NCH // 2 * share % span == 0 else 1
    some = NCH // parts
    strip = rows // peers

    def each(count, body, first=0):
        def step(i, carry):
            body(i)
            return carry

        lax.fori_loop(first, count, step, 0)

    small = [
        pltpu.make_async_copy(source, target, small_sem.at[i])
        for i, (source, target) in enumerate(
            ((ids_hbm, ids_ref), (served_hbm, served_ref), (offsets_hbm, offsets_ref))
        )
    ]
    for load in small:
        load.start()

    if stored is None:
        several = weights.shape[1]
        store_loads = [
            pltpu.make_async_copy(
                store_hbm.at[pl.ds(i * several, several)], weights.at[i], store_sem.at[i]
            )
            for i in range(store_hbm.shape[0] // several)
        ]
    else:
        store_loads = [pltpu.make_async_copy(store_hbm, stored, store_sem.at[0])]
    for load in store_loads:
        load.start()

    def pick(s, target):
        request = served_ref[s]

        def one(c):
            block = ids_ref[request, c]
            if stored is None:
                target[s, c] = weights[block // several, block % several]
            else:
                target[s, c] = stored[block]

        each(NCH, one)

    barrier = pltpu.get_barrier_semaphore()
    for k in range(1, slots):
        pl.semaphore_signal(
            barrier, inc=1, device_id={"store": lax.rem(me + k, slots)}, device_id_type=MESH
        )
    for k in range(1, peers):
        pl.semaphore_signal(
            barrier, inc=1, device_id={"mp": lax.rem(part + k, peers)}, device_id_type=MESH
        )
    loads = [
        pltpu.make_async_copy(wq_hbm, wq, load_sem.at[0]),
        pltpu.make_async_copy(wkv_hbm, wkv, load_sem.at[1]),
        pltpu.make_async_copy(
            hidden_ref.at[0, :, pl.ds(pl.multiple_of(me * depth, depth), depth)],
            tokens.at[me], load_sem.at[2],
        ),
    ]
    tables_copy = pltpu.make_async_copy(tables_hbm, tables, own_sem.at[0])
    pl.semaphore_wait(barrier, slots + peers - 2)

    def strip_copy(k):
        to = lax.rem(me + k, slots)
        mine = pl.ds(pl.multiple_of(part * strip, strip), strip)
        return pltpu.make_async_remote_copy(
            src_ref=hidden_ref.at[0, mine, pl.ds(pl.multiple_of(to * depth, depth), depth)],
            dst_ref=tokens.at[me, mine, :],
            send_sem=a_send.at[k],
            recv_sem=a_recv.at[k],
            device_id={"store": to},
            device_id_type=MESH,
        )

    def spread_copy(k, d):
        source = lax.rem(me - k + slots, slots)
        mine = pl.ds(pl.multiple_of(part * strip, strip), strip)
        return pltpu.make_async_remote_copy(
            src_ref=tokens.at[source, mine, :],
            dst_ref=tokens.at[source, mine, :],
            send_sem=b_send.at[k, d],
            recv_sem=b_recv.at[k, d],
            device_id={"mp": lax.rem(part + d, peers)},
            device_id_type=MESH,
        )

    def block_copy(k, g, piece):
        to = lax.rem(me + k, slots)
        cols = pl.ds(pl.multiple_of((2 * g + min(piece, 1)) * HD, HD), HD)
        chosen = slice(0, NCH) if piece == 0 else slice((piece - 1) * some, piece * some)
        return pltpu.make_async_remote_copy(
            src_ref=sending.at[to, chosen, :, cols],
            dst_ref=blocks.at[me, chosen, :, cols],
            send_sem=k_send.at[k, (1 + parts) * g + piece],
            recv_sem=k_recv.at[k, (1 + parts) * g + piece],
            device_id={"store": to},
            device_id_type=MESH,
        )

    low = me < slots // 2

    mirrored = jnp.where(low, me, slots - 1 - me)

    def other(j):
        far = jnp.where(mirrored == 0, 0, slots - 2 - mirrored)
        source = jnp.where(
            j < far, slots - 1 - j, jnp.where(j < far + mirrored, j - far, mirrored + 1 + jnp.where(mirrored == 0, j, 0))
        )
        return jnp.where(low, source, slots - 1 - source)

    def other_shift(j):
        return lax.rem(me - other(j) + slots, slots)

    def send_values(up):
        def one(j):
            d = slots - 1 - j
            fits = (me + d < slots) if up else (me >= d)

            @pl.when(fits)
            def _():
                for g in range(kv_heads):
                    for piece in range(parts):
                        block_copy(d if up else slots - d, g, 1 + piece).start()

        each(slots - 1, one)

    def sum_copy(s, q, up):
        index = s + 1 if up else s
        return pltpu.make_async_remote_copy(
            src_ref=codes.at[index, q],
            dst_ref=codes.at[index, q],
            send_sem=p_send.at[index, q],
            recv_sem=p_recv.at[index, q],
            device_id={"store": lax.rem(me + 1, slots) if up else lax.rem(me + slots - 1, slots)},
            device_id_type=MESH,
        )

    def bound_copy(s, up):
        index = s + 1 if up else s
        return pltpu.make_async_remote_copy(
            src_ref=bounds_out.at[index],
            dst_ref=bounds_in.at[index],
            send_sem=s_send.at[index],
            recv_sem=s_recv.at[index],
            device_id={"store": lax.rem(me + 1, slots) if up else lax.rem(me + slots - 1, slots)},
            device_id_type=MESH,
        )

    tall = rows // BANDS
    bands = [slice(i * tall, (i + 1) * tall) for i in range(BANDS)]
    extra = [slice(rows + i * tall, rows + (i + 1) * tall) for i in range(PACKED)]

    def columns_of(i):
        return pl.ds(pl.multiple_of(i * HD, HD), HD)

    def add_codes(q, s, index):
        step = bounds_in[index, pl.ds(q, 1), :] * (1.0 / STEPS)

        def some_columns(i):
            at = columns_of(i)
            low = unpack([codes[index, q, band, at] for band in extra])
            for band, part in zip(bands, low):
                value = (codes[index, q, band, at].astype(jnp.int32) << LOW) | part
                sums[q, s, band, at] = sums[q, s, band, at] + value.astype(jnp.float32) * step

        each(width // HD, some_columns)

    def make_codes(q, s, index):
        factor = STEPS / bounds_out[index, pl.ds(q, 1), :]

        def some_columns(i):
            at = columns_of(i)
            low = []
            for band in bands:
                value = jnp.round(sums[q, s, band, at] * factor).astype(jnp.int32)
                codes[index, q, band, at] = (value >> LOW).astype(jnp.int16)
                low.append(value & 63)
            for band, word in zip(extra, pack(low)):
                codes[index, q, band, at] = word

        each(width // HD, some_columns)

    def forward(q, s, up, begins):
        index = s + 1 if up else s

        @pl.when(q == 0)
        def _():
            @pl.when(begins)
            def _():
                bounds_out[index] = own[s]

            @pl.when(jnp.logical_not(begins))
            def _():
                bound_copy(s, up).wait_recv()
                bounds_out[index] = own[s] + bounds_in[index]

            bound_copy(s, up).start()

        @pl.when(jnp.logical_not(begins))
        def _():
            sum_copy(s, q, up).wait_recv()
            add_codes(q, s, index)

        make_codes(q, s, index)
        sum_copy(s, q, up).start()

    each(slots, lambda k: strip_copy(k).start(), 1)
    for load in loads:
        load.start()
    tables_copy.start()
    for load in small + store_loads:
        load.wait()

    def send_keys(j):
        d = slots - 1 - j
        for up in (True, False):
            to = me + d if up else me - d

            @pl.when((to < slots) if up else (to >= 0))
            def _():
                pick(to, sending)
                for g in range(kv_heads):
                    block_copy(d if up else slots - d, g, 0).start()

    each(slots - 1, send_keys)
    pick(me, blocks)

    @pl.when(low)
    def _():
        send_values(False)

    @pl.when(jnp.logical_not(low))
    def _():
        send_values(True)


    def spread(k):
        strip_copy(k).wait_recv()
        for d in range(1, peers):
            spread_copy(k, d).start()

    each(slots, spread, 1)

    def spread_wait(k):
        for d in range(1, peers):
            spread_copy(k, d).wait_recv()

    each(slots, spread_wait, 1)
    for load in loads:
        load.wait()

    group = 4 if slots % 4 == 0 else 1

    def project(q, panel):
        def some_slots(i):
            t = tokens[pl.ds(i * group, group)].reshape(group * rows, depth)
            sums[q, pl.ds(i * group, group)] = jnp.dot(
                t, panel, preferred_element_type=jnp.float32
            ).reshape(group, rows, width)

        each(slots // group, some_slots)

    def relay_up(k, q):
        @pl.when(slots - 1 - k > me)
        def _():
            forward(q, slots - 1 - k, True, me == 0)

    def relay_down(k, q):
        @pl.when(k < me)
        def _():
            forward(q, k, False, me == slots - 1)

    for q in range(chunks):
        if q < chunks - 1:
            project(q, wq[:, q * width : (q + 1) * width])
        else:
            project(q, wkv[...])

    def measure(s):
        own[s] = jnp.zeros(own.shape[1:], jnp.float32)
        for q in range(chunks):
            largest = jnp.maximum(jnp.max(jnp.abs(sums[q, s]), keepdims=True), LEAST)
            own[s, q : q + 1, :] = jnp.broadcast_to(largest, (1, HD))

    each(slots, measure)

    steps = (slots - 1) * chunks

    def relay(i):
        def at(i, move):
            @pl.when((i >= 0) & (i < steps))
            def _():
                move(i // chunks, i % chunks)

        @pl.when(low)
        def _():
            at(i, relay_up)
            at(i - chunks, relay_down)

        @pl.when(jnp.logical_not(low))
        def _():
            at(i, relay_down)
            at(i - chunks, relay_up)

    each(steps + chunks, relay)

    @pl.when(low)
    def _():
        send_values(True)

    @pl.when(jnp.logical_not(low))
    def _():
        send_values(False)

    def drain_sums(i):
        k, q = i // chunks, i % chunks

        @pl.when(slots - 1 - k > me)
        def _():
            sum_copy(slots - 1 - k, q, True).wait_send()

            @pl.when(q == 0)
            def _():
                bound_copy(slots - 1 - k, True).wait_send()

        @pl.when(k < me)
        def _():
            sum_copy(k, q, False).wait_send()

            @pl.when(q == 0)
            def _():
                bound_copy(k, False).wait_send()

    def rotate_share(source):
        at_t = pl.multiple_of(source * share, share)
        tc, ts = tables[0, pl.ds(at_t, share), :], tables[1, pl.ds(at_t, share), :]

        def one(c):
            at_k = pl.multiple_of((source * NCH + c) * share, share)
            jitter = jnp.clip(offsets_ref[served_ref[me], c] - c * L, 0, GAP - 1)
            start = L + c * GAP + jitter
            oc, os = tables[0, pl.ds(start, 1), :], tables[1, pl.ds(start, 1), :]
            cos = tc * oc - ts * os
            sin = ts * oc + tc * os
            for g in range(kv_heads):
                at = g * 2 * HD
                x = blocks[source, c, :, at : at + HD].astype(jnp.float32)
                keys[g, pl.ds(at_k, share), :] = turn(x, cos, sin).astype(jnp.bfloat16)

        each(NCH, one)

    tables_copy.wait()
    rotate_share(me)

    def take(j):
        for g in range(kv_heads):
            block_copy(other_shift(j), g, 0).wait_recv()
        rotate_share(other(j))

    each(slots - 1, take)

    @pl.when(me > 0)
    def _():
        bound_copy(me, True).wait_recv()

    @pl.when(me < slots - 1)
    def _():
        bound_copy(me, False).wait_recv()

    def settle(q):
        @pl.when(me > 0)
        def _():
            sum_copy(me, q, True).wait_recv()
            add_codes(q, me, me + 1)

        @pl.when(me < slots - 1)
        def _():
            sum_copy(me, q, False).wait_recv()
            add_codes(q, me, me)

    each(chunks, settle)

    at_q = L + NCH * GAP
    qc, qs = tables[0, at_q : at_q + rows, :], tables[1, at_q : at_q + rows, :]
    for g in range(kv_heads):
        at = g * 2 * HD
        keys[g, past:, :] = turn(sums[chunks - 1, me, :, at : at + HD], qc, qs).astype(jnp.bfloat16)
        fresh[g] = sums[chunks - 1, me, :, at + HD : at + 2 * HD].astype(jnp.bfloat16)
    for h in range(heads):
        q, at = divmod(h * HD, width)
        queries[h * rows : (h + 1) * rows, :] = turn(
            sums[q, me, :, at : at + HD], qc, qs
        ).astype(jnp.bfloat16)

    block = 2 * rows
    factor = math.log2(math.e) / math.sqrt(HD)
    lower = lax.broadcasted_iota(jnp.int32, (block, rows), 0) % rows >= lax.broadcasted_iota(
        jnp.int32, (block, rows), 1
    )
    contract = (((1,), (1,)), ((), ()))

    def weigh(b):
        g = (b * 2) // sharing
        at = pl.ds(pl.multiple_of(b * block, block), block)
        q = queries[at, :]
        own = lax.dot_general(q, keys[g, past:, :], contract, preferred_element_type=jnp.float32)
        own = jnp.where(lower, own, -jnp.inf)
        top = own
        for j in range(past // span):
            s = lax.dot_general(
                q, keys[g, j * span : (j + 1) * span, :], contract,
                preferred_element_type=jnp.float32,
            )
            scores[:, j * span : (j + 1) * span] = s
            for k in range(span // HD):
                top = jnp.maximum(top, s[:, k * HD : (k + 1) * HD])
        top = jnp.max(top, axis=1, keepdims=True)
        w = jnp.exp2((own - top) * factor)
        total = w
        own_weights[at, :] = w.astype(jnp.bfloat16)
        for j in range(past // span):
            w = jnp.exp2((scores[:, j * span : (j + 1) * span] - top) * factor)
            for k in range(span // HD):
                total = total + w[:, k * HD : (k + 1) * HD]
            weights[b, j] = w.astype(jnp.bfloat16)
        totals[at, :] = total

    each(heads // 2, weigh)

    stack = sharing * rows

    def invert(h):
        at = pl.ds(pl.multiple_of(h * rows, rows), rows)
        totals[at, :] = jnp.broadcast_to(
            1.0 / jnp.sum(totals[at, :], axis=1, keepdims=True), (rows, HD)
        )

    each(heads, invert)

    pairs = sharing // 2

    pairs = sharing // 2
    keys_each = some * share
    size = min(keys_each, span)

    def product(source, g, piece):
        v = blocks[
            source, piece * some : (piece + 1) * some, :, (2 * g + 1) * HD : (2 * g + 2) * HD
        ].reshape(keys_each, HD)
        mine = slice(g * pairs, (g + 1) * pairs)
        total = None
        for i in range(keys_each // size):
            start = (source * parts + piece) * keys_each + i * size
            at = pl.ds(pl.multiple_of(lax.rem(start, span), size), size)
            w = weights[mine, start // span] if size == span else weights[mine, start // span, :, at]
            w = w.reshape(stack, size)
            term = jnp.dot(w, v[i * size : (i + 1) * size], preferred_element_type=jnp.float32)
            total = term if total is None else total + term
        return total

    for g in range(kv_heads):
        at = slice(g * stack, (g + 1) * stack)
        mixed[at, :] = jnp.dot(
            own_weights[at, :], fresh[g], preferred_element_type=jnp.float32
        )
        for piece in range(parts):
            mixed[at, :] = mixed[at, :] + product(me, g, piece)

    def take_value(j, g, piece):
        at = slice(g * stack, (g + 1) * stack)
        block_copy(other_shift(j), g, 1 + piece).wait_recv()
        return mixed[at, :] + product(other(j), g, piece)

    def take_values(j, g, count):
        at = slice(g * stack, (g + 1) * stack)
        for piece in range(count):
            mixed[at, :] = take_value(j, g, piece)

    def out_copy(g):
        cols = slice(g * stack, (g + 1) * stack)
        return pltpu.make_async_copy(out.at[:, cols], out_hbm.at[0, :, cols], out_sem.at[g])

    def drain(k):
        strip_copy(k).wait_send()
        for d in range(1, peers):
            spread_copy(k, d).wait_send()
        for g in range(kv_heads):
            block_copy(k, g, 0).wait_send()

    each(slots, drain, 1)
    each(steps, drain_sums)

    early = slots - 3
    for j in range(early):
        for g in range(kv_heads):
            take_values(j, g, parts)
    for g in range(kv_heads):
        for j in range(early, slots - 2):
            take_values(j, g, parts)
        take_values(slots - 2, g, parts - 1)
        at = slice(g * stack, (g + 1) * stack)
        done = take_value(slots - 2, g, parts - 1) * totals[at, :]
        for h in range(sharing):
            first = (g * sharing + h) * HD
            out[:, first : first + HD] = done[h * rows : (h + 1) * rows].astype(out.dtype)
        out_copy(g).start()

    def drain_values(k):
        for g in range(kv_heads):
            for piece in range(parts):
                block_copy(k, g, 1 + piece).wait_send()

    each(slots, drain_values, 1)
    for g in range(kv_heads):
        out_copy(g).wait()


def per_device(hidden, query_weight, keyvalue_weight, block_store, block_ids, offsets, served):
    slots = lax.axis_size("store")
    peers = lax.axis_size("mp")
    rows, model = hidden.shape[1:]
    share, kv_cols = block_store.shape[1:]
    q_cols = query_weight.shape[1]
    heads = q_cols // HD
    kv_heads = kv_cols // (2 * HD)
    chunks = q_cols // kv_cols + 1
    depth = model // slots
    past = NCH * L
    span = 512
    staged = (2 * rows, span) == (share, kv_cols) and block_store.shape[0] <= heads // 2 * past // span
    starts = (np.arange(NCH)[:, None] * L + np.arange(GAP)[None, :]).reshape(-1)
    tables = np.stack(
        signed_tables(np.concatenate([np.arange(L), starts, past + GAP + np.arange(rows)]))
    )
    hbm = pl.BlockSpec(memory_space=pl.ANY)
    dma = pltpu.SemaphoreType.DMA
    return pl.pallas_call(
        functools.partial(serve_body, slots, peers, heads, kv_heads),
        out_shape=jax.ShapeDtypeStruct((1, rows, q_cols), jnp.bfloat16),
        in_specs=[hbm] * 8,
        out_specs=hbm,
        scratch_shapes=[
            pltpu.SMEM(block_ids.shape, jnp.int32),
            pltpu.SMEM(served.shape, jnp.int32),
            pltpu.SMEM(offsets.shape, jnp.int32),
            pltpu.VMEM((slots, rows, depth), jnp.bfloat16),
            pltpu.VMEM(query_weight.shape, jnp.bfloat16),
            pltpu.VMEM(keyvalue_weight.shape, jnp.bfloat16),
            pltpu.VMEM((chunks, slots, rows, kv_cols), jnp.float32),
            pltpu.VMEM((slots + 1, chunks, rows + rows // BANDS * PACKED, kv_cols), jnp.int16),
            pltpu.VMEM((slots, 8, HD), jnp.float32),
            pltpu.VMEM((slots + 1, 8, HD), jnp.float32),
            pltpu.VMEM((slots + 1, 8, HD), jnp.float32),
            pltpu.VMEM((slots, NCH, share, kv_cols), jnp.bfloat16),
            pltpu.VMEM((kv_heads, past + rows, HD), jnp.bfloat16),
            pltpu.VMEM((kv_heads, rows, HD), jnp.bfloat16),
            pltpu.VMEM((heads * rows, HD), jnp.bfloat16),
            pltpu.VMEM((2 * rows, past), jnp.float32),
            pltpu.VMEM((heads // 2, past // span, 2 * rows, span), jnp.bfloat16),
            pltpu.VMEM((heads * rows, rows), jnp.bfloat16),
            None if staged else pltpu.VMEM(block_store.shape, jnp.bfloat16),
            pltpu.VMEM((slots, NCH, share, kv_cols), jnp.bfloat16),
            pltpu.VMEM((heads * rows, HD), jnp.float32),
            pltpu.VMEM((heads * rows, HD), jnp.float32),
            pltpu.VMEM(tables.shape, jnp.float32),
            pltpu.VMEM((rows, q_cols), jnp.bfloat16),
            dma((3,)),
            dma((3,)),
            dma((1,)),
            dma((heads // 2,)),
            dma((kv_heads,)),
            dma((slots,)),
            dma((slots,)),
            dma((slots, peers)),
            dma((slots, peers)),
            dma((slots, 3 * kv_heads)),
            dma((slots, 3 * kv_heads)),
            dma((slots + 1, chunks)),
            dma((slots + 1, chunks)),
            dma((slots + 1,)),
            dma((slots + 1,)),
        ],
        compiler_params=pltpu.CompilerParams(
            vmem_limit_bytes=63 << 20, collective_id=0, has_side_effects=True
        ),
        name="serve",
    )(block_ids, served, offsets, hidden, query_weight, keyvalue_weight, block_store, tables)


def solution(mesh):
    in_specs = (
        P(("groups", "store"), None, None),
        P("store", "mp"),
        P("store", "mp"),
        P("groups", "store", "mp"),
        P("groups", None),
        P("groups", None),
        P("groups"),
    )
    out_specs = P(("groups", "store"), None, "mp")
    return jax.shard_map(
        per_device, mesh=mesh, in_specs=in_specs, out_specs=out_specs, check_vma=False
    )
```

```python
import functools
import math

import jax
import jax.numpy as jnp
import numpy as np
from jax import lax
from jax.experimental import pallas as pl
from jax.experimental.pallas import tpu as pltpu
from jax.sharding import PartitionSpec as P

HD = 128
HALF = HD // 2
NCH = 4
L = 1024
GAP = 64
BASE = 500000.0


def periods():
    inverse = np.exp(
        np.arange(HALF, dtype=np.float32) * np.float32(-2.0 * math.log(BASE) / HD)
    ).astype(np.float32)
    return np.floor(np.float32(2.0 * math.pi) / inverse + np.float32(0.5)).astype(np.float64)


def signed_tables(positions):
    period = periods()[None, :]
    angles = np.mod(np.asarray(positions, np.float64)[:, None], period) / period * (2.0 * math.pi)
    cos, sin = np.cos(angles), np.sin(angles)
    return (
        np.concatenate([cos, cos], axis=1).astype(np.float32),
        np.concatenate([-sin, sin], axis=1).astype(np.float32),
    )


def turn(x, cos, sin):
    return x * cos + pltpu.roll(x, HALF, 1) * sin


MESH = pl.DeviceIdType.MESH
STEPS = 2097000.0
LEAST = 1e-30
LOW = 6
BANDS = 8
PACKED = 3


def pack(low):
    words = (
        low[0] | (low[1] << 6) | ((low[2] & 15) << 12),
        (low[2] >> 4) | (low[3] << 2) | (low[4] << 8) | ((low[5] & 3) << 14),
        (low[5] >> 2) | (low[6] << 4) | (low[7] << 10),
    )
    return [(word - 32768).astype(jnp.int16) for word in words]


def unpack(words):
    a, b, c = [word.astype(jnp.int32) + 32768 for word in words]
    return (
        a & 63, (a >> 6) & 63, (a >> 12) | ((b & 3) << 4), (b >> 2) & 63,
        (b >> 8) & 63, (b >> 14) | ((c & 15) << 2), (c >> 4) & 63, c >> 10,
    )


def serve_body(
    slots, peers, heads, kv_heads,
    ids_hbm, served_hbm, offsets_hbm, hidden_ref, wq_hbm, wkv_hbm, store_hbm, tables_hbm,
    out_hbm,
    ids_ref, served_ref, offsets_ref, tokens, wq, wkv, sums, codes, own, bounds_in, bounds_out, blocks, keys, fresh, queries, scores, weights, own_weights, stored, sending, totals, mixed, tables, out,
    small_sem, load_sem, own_sem, store_sem, out_sem, a_send, a_recv, b_send, b_recv, k_send, k_recv, p_send, p_recv, s_send, s_recv,
):
    me = lax.axis_index("store")
    part = lax.axis_index("mp")
    rows = hidden_ref.shape[1]
    depth = tokens.shape[2]
    chunks, _, _, width = sums.shape
    share = blocks.shape[3]
    sharing = heads // kv_heads
    past = NCH * L
    span = weights.shape[3]
    parts = 2 if NCH // 2 * share % span == 0 else 1
    some = NCH // parts
    strip = rows // peers

    def each(count, body, first=0):
        def step(i, carry):
            body(i)
            return carry

        lax.fori_loop(first, count, step, 0)

    small = [
        pltpu.make_async_copy(source, target, small_sem.at[i])
        for i, (source, target) in enumerate(
            ((ids_hbm, ids_ref), (served_hbm, served_ref), (offsets_hbm, offsets_ref))
        )
    ]
    for load in small:
        load.start()

    if stored is None:
        several = weights.shape[1]
        store_loads = [
            pltpu.make_async_copy(
                store_hbm.at[pl.ds(i * several, several)], weights.at[i], store_sem.at[i]
            )
            for i in range(store_hbm.shape[0] // several)
        ]
    else:
        store_loads = [pltpu.make_async_copy(store_hbm, stored, store_sem.at[0])]
    for load in store_loads:
        load.start()

    def pick(s, target):
        request = served_ref[s]

        def one(c):
            block = ids_ref[request, c]
            for i in range(2 * kv_heads):
                at = slice(i * HD, (i + 1) * HD)
                if stored is None:
                    target[s, i, c] = weights[block // several, block % several, :, at]
                else:
                    target[s, i, c] = stored[block, :, at]

        each(NCH, one)

    barrier = pltpu.get_barrier_semaphore()
    for k in range(1, slots):
        pl.semaphore_signal(
            barrier, inc=1, device_id={"store": lax.rem(me + k, slots)}, device_id_type=MESH
        )
    for k in range(1, peers):
        pl.semaphore_signal(
            barrier, inc=1, device_id={"mp": lax.rem(part + k, peers)}, device_id_type=MESH
        )
    loads = [
        pltpu.make_async_copy(wq_hbm, wq, load_sem.at[0]),
        pltpu.make_async_copy(wkv_hbm, wkv, load_sem.at[1]),
        pltpu.make_async_copy(
            hidden_ref.at[0, :, pl.ds(pl.multiple_of(me * depth, depth), depth)],
            tokens.at[me], load_sem.at[2],
        ),
    ]
    tables_copy = pltpu.make_async_copy(tables_hbm, tables, own_sem.at[0])
    pl.semaphore_wait(barrier, slots + peers - 2)

    def strip_copy(k):
        to = lax.rem(me + k, slots)
        mine = pl.ds(pl.multiple_of(part * strip, strip), strip)
        return pltpu.make_async_remote_copy(
            src_ref=hidden_ref.at[0, mine, pl.ds(pl.multiple_of(to * depth, depth), depth)],
            dst_ref=tokens.at[me, mine, :],
            send_sem=a_send.at[k],
            recv_sem=a_recv.at[k],
            device_id={"store": to},
            device_id_type=MESH,
        )

    def spread_copy(k, d):
        source = lax.rem(me - k + slots, slots)
        mine = pl.ds(pl.multiple_of(part * strip, strip), strip)
        return pltpu.make_async_remote_copy(
            src_ref=tokens.at[source, mine, :],
            dst_ref=tokens.at[source, mine, :],
            send_sem=b_send.at[k, d],
            recv_sem=b_recv.at[k, d],
            device_id={"mp": lax.rem(part + d, peers)},
            device_id_type=MESH,
        )

    def block_copy(k, g, piece):
        to = lax.rem(me + k, slots)
        column = 2 * g + min(piece, 1)
        chosen = slice(0, NCH) if piece == 0 else slice((piece - 1) * some, piece * some)
        return pltpu.make_async_remote_copy(
            src_ref=sending.at[to, column, chosen],
            dst_ref=blocks.at[me, column, chosen],
            send_sem=k_send.at[k, (1 + parts) * g + piece],
            recv_sem=k_recv.at[k, (1 + parts) * g + piece],
            device_id={"store": to},
            device_id_type=MESH,
        )

    low = me < slots // 2

    mirrored = jnp.where(low, me, slots - 1 - me)

    def other(j):
        far = jnp.where(mirrored == 0, 0, slots - 2 - mirrored)
        source = jnp.where(
            j < far, slots - 1 - j, jnp.where(j < far + mirrored, j - far, mirrored + 1 + jnp.where(mirrored == 0, j, 0))
        )
        return jnp.where(low, source, slots - 1 - source)

    def other_shift(j):
        return lax.rem(me - other(j) + slots, slots)

    def send_values(up):
        def one(j):
            d = slots - 1 - j
            fits = (me + d < slots) if up else (me >= d)

            @pl.when(fits)
            def _():
                for g in range(kv_heads):
                    for piece in range(parts):
                        block_copy(d if up else slots - d, g, 1 + piece).start()

        each(slots - 1, one)

    def sum_copy(s, q, up):
        index = s + 1 if up else s
        return pltpu.make_async_remote_copy(
            src_ref=codes.at[index, q],
            dst_ref=codes.at[index, q],
            send_sem=p_send.at[index, q],
            recv_sem=p_recv.at[index, q],
            device_id={"store": lax.rem(me + 1, slots) if up else lax.rem(me + slots - 1, slots)},
            device_id_type=MESH,
        )

    def bound_copy(s, up):
        index = s + 1 if up else s
        return pltpu.make_async_remote_copy(
            src_ref=bounds_out.at[index],
            dst_ref=bounds_in.at[index],
            send_sem=s_send.at[index],
            recv_sem=s_recv.at[index],
            device_id={"store": lax.rem(me + 1, slots) if up else lax.rem(me + slots - 1, slots)},
            device_id_type=MESH,
        )

    tall = rows // BANDS
    bands = [slice(i * tall, (i + 1) * tall) for i in range(BANDS)]
    extra = [slice(rows + i * tall, rows + (i + 1) * tall) for i in range(PACKED)]

    def columns_of(i):
        return pl.ds(pl.multiple_of(i * HD, HD), HD)

    def add_codes(q, s, index):
        step = bounds_in[index, pl.ds(q, 1), :] * (1.0 / STEPS)

        def some_columns(i):
            at = columns_of(i)
            low = unpack([codes[index, q, band, at] for band in extra])
            for band, part in zip(bands, low):
                value = (codes[index, q, band, at].astype(jnp.int32) << LOW) | part
                sums[q, s, band, at] = sums[q, s, band, at] + value.astype(jnp.float32) * step

        each(width // HD, some_columns)

    def make_codes(q, s, index):
        factor = STEPS / bounds_out[index, pl.ds(q, 1), :]

        def some_columns(i):
            at = columns_of(i)
            low = []
            for band in bands:
                value = jnp.round(sums[q, s, band, at] * factor).astype(jnp.int32)
                codes[index, q, band, at] = (value >> LOW).astype(jnp.int16)
                low.append(value & 63)
            for band, word in zip(extra, pack(low)):
                codes[index, q, band, at] = word

        each(width // HD, some_columns)

    def forward(q, s, up, begins):
        index = s + 1 if up else s

        @pl.when(q == 0)
        def _():
            @pl.when(begins)
            def _():
                bounds_out[index] = own[s]

            @pl.when(jnp.logical_not(begins))
            def _():
                bound_copy(s, up).wait_recv()
                bounds_out[index] = own[s] + bounds_in[index]

            bound_copy(s, up).start()

        @pl.when(jnp.logical_not(begins))
        def _():
            sum_copy(s, q, up).wait_recv()
            add_codes(q, s, index)

        make_codes(q, s, index)
        sum_copy(s, q, up).start()

    each(slots, lambda k: strip_copy(k).start(), 1)
    for load in loads:
        load.start()
    tables_copy.start()
    for load in small + store_loads:
        load.wait()

    def send_keys(j):
        d = slots - 1 - j
        for up in (True, False):
            to = me + d if up else me - d

            @pl.when((to < slots) if up else (to >= 0))
            def _():
                pick(to, sending)
                for g in range(kv_heads):
                    block_copy(d if up else slots - d, g, 0).start()

    each(slots - 1, send_keys)
    pick(me, blocks)

    @pl.when(low)
    def _():
        send_values(False)

    @pl.when(jnp.logical_not(low))
    def _():
        send_values(True)


    def spread(k):
        strip_copy(k).wait_recv()
        for d in range(1, peers):
            spread_copy(k, d).start()

    each(slots, spread, 1)

    def spread_wait(k):
        for d in range(1, peers):
            spread_copy(k, d).wait_recv()

    each(slots, spread_wait, 1)
    for load in loads:
        load.wait()

    group = 4 if slots % 4 == 0 else 1

    def project(q, panel):
        def some_slots(i):
            t = tokens[pl.ds(i * group, group)].reshape(group * rows, depth)
            sums[q, pl.ds(i * group, group)] = jnp.dot(
                t, panel, preferred_element_type=jnp.float32
            ).reshape(group, rows, width)

        each(slots // group, some_slots)

    def relay_up(k, q):
        @pl.when(slots - 1 - k > me)
        def _():
            forward(q, slots - 1 - k, True, me == 0)

    def relay_down(k, q):
        @pl.when(k < me)
        def _():
            forward(q, k, False, me == slots - 1)

    for q in range(chunks):
        if q < chunks - 1:
            project(q, wq[:, q * width : (q + 1) * width])
        else:
            project(q, wkv[...])

    def measure(s):
        own[s] = jnp.zeros(own.shape[1:], jnp.float32)
        for q in range(chunks):
            largest = jnp.maximum(jnp.max(jnp.abs(sums[q, s]), keepdims=True), LEAST)
            own[s, q : q + 1, :] = jnp.broadcast_to(largest, (1, HD))

    each(slots, measure)

    steps = (slots - 1) * chunks

    def relay(i):
        def at(i, move):
            @pl.when((i >= 0) & (i < steps))
            def _():
                move(i // chunks, i % chunks)

        @pl.when(low)
        def _():
            at(i, relay_up)
            at(i - chunks, relay_down)

        @pl.when(jnp.logical_not(low))
        def _():
            at(i, relay_down)
            at(i - chunks, relay_up)

    each(steps + chunks, relay)

    @pl.when(low)
    def _():
        send_values(True)

    @pl.when(jnp.logical_not(low))
    def _():
        send_values(False)

    def drain_sums(i):
        k, q = i // chunks, i % chunks

        @pl.when(slots - 1 - k > me)
        def _():
            sum_copy(slots - 1 - k, q, True).wait_send()

            @pl.when(q == 0)
            def _():
                bound_copy(slots - 1 - k, True).wait_send()

        @pl.when(k < me)
        def _():
            sum_copy(k, q, False).wait_send()

            @pl.when(q == 0)
            def _():
                bound_copy(k, False).wait_send()

    def rotate_share(source):
        at_t = pl.multiple_of(source * share, share)
        tc, ts = tables[0, pl.ds(at_t, share), :], tables[1, pl.ds(at_t, share), :]

        def one(c):
            at_k = pl.multiple_of((source * NCH + c) * share, share)
            jitter = jnp.clip(offsets_ref[served_ref[me], c] - c * L, 0, GAP - 1)
            start = L + c * GAP + jitter
            oc, os = tables[0, pl.ds(start, 1), :], tables[1, pl.ds(start, 1), :]
            cos = tc * oc - ts * os
            sin = ts * oc + tc * os
            for g in range(kv_heads):
                x = blocks[source, 2 * g, c].astype(jnp.float32)
                keys[g, pl.ds(at_k, share), :] = turn(x, cos, sin).astype(jnp.bfloat16)

        each(NCH, one)

    tables_copy.wait()
    rotate_share(me)

    def take(j):
        for g in range(kv_heads):
            block_copy(other_shift(j), g, 0).wait_recv()
        rotate_share(other(j))

    each(slots - 1, take)

    @pl.when(me > 0)
    def _():
        bound_copy(me, True).wait_recv()

    @pl.when(me < slots - 1)
    def _():
        bound_copy(me, False).wait_recv()

    def settle(q):
        @pl.when(me > 0)
        def _():
            sum_copy(me, q, True).wait_recv()
            add_codes(q, me, me + 1)

        @pl.when(me < slots - 1)
        def _():
            sum_copy(me, q, False).wait_recv()
            add_codes(q, me, me)

    each(chunks, settle)

    at_q = L + NCH * GAP
    qc, qs = tables[0, at_q : at_q + rows, :], tables[1, at_q : at_q + rows, :]
    for g in range(kv_heads):
        at = g * 2 * HD
        keys[g, past:, :] = turn(sums[chunks - 1, me, :, at : at + HD], qc, qs).astype(jnp.bfloat16)
        fresh[g] = sums[chunks - 1, me, :, at + HD : at + 2 * HD].astype(jnp.bfloat16)
    for h in range(heads):
        q, at = divmod(h * HD, width)
        queries[h * rows : (h + 1) * rows, :] = turn(
            sums[q, me, :, at : at + HD], qc, qs
        ).astype(jnp.bfloat16)

    block = 2 * rows
    factor = math.log2(math.e) / math.sqrt(HD)
    lower = lax.broadcasted_iota(jnp.int32, (block, rows), 0) % rows >= lax.broadcasted_iota(
        jnp.int32, (block, rows), 1
    )
    contract = (((1,), (1,)), ((), ()))

    def weigh(b):
        g = (b * 2) // sharing
        at = pl.ds(pl.multiple_of(b * block, block), block)
        q = queries[at, :]
        own = lax.dot_general(q, keys[g, past:, :], contract, preferred_element_type=jnp.float32)
        own = jnp.where(lower, own, -jnp.inf)
        top = own
        for j in range(past // span):
            s = lax.dot_general(
                q, keys[g, j * span : (j + 1) * span, :], contract,
                preferred_element_type=jnp.float32,
            )
            scores[:, j * span : (j + 1) * span] = s
            for k in range(span // HD):
                top = jnp.maximum(top, s[:, k * HD : (k + 1) * HD])
        top = jnp.max(top, axis=1, keepdims=True)
        w = jnp.exp2((own - top) * factor)
        total = w
        own_weights[at, :] = w.astype(jnp.bfloat16)
        for j in range(past // span):
            w = jnp.exp2((scores[:, j * span : (j + 1) * span] - top) * factor)
            for k in range(span // HD):
                total = total + w[:, k * HD : (k + 1) * HD]
            weights[b, j] = w.astype(jnp.bfloat16)
        totals[at, :] = total

    each(heads // 2, weigh)

    stack = sharing * rows

    def invert(h):
        at = pl.ds(pl.multiple_of(h * rows, rows), rows)
        totals[at, :] = jnp.broadcast_to(
            1.0 / jnp.sum(totals[at, :], axis=1, keepdims=True), (rows, HD)
        )

    each(heads, invert)

    pairs = sharing // 2

    pairs = sharing // 2
    keys_each = some * share
    size = min(keys_each, span)

    def product(source, g, piece):
        v = blocks[source, 2 * g + 1, piece * some : (piece + 1) * some].reshape(keys_each, HD)
        mine = slice(g * pairs, (g + 1) * pairs)
        total = None
        for i in range(keys_each // size):
            start = (source * parts + piece) * keys_each + i * size
            at = pl.ds(pl.multiple_of(lax.rem(start, span), size), size)
            w = weights[mine, start // span] if size == span else weights[mine, start // span, :, at]
            w = w.reshape(stack, size)
            term = jnp.dot(w, v[i * size : (i + 1) * size], preferred_element_type=jnp.float32)
            total = term if total is None else total + term
        return total

    for g in range(kv_heads):
        at = slice(g * stack, (g + 1) * stack)
        mixed[at, :] = jnp.dot(
            own_weights[at, :], fresh[g], preferred_element_type=jnp.float32
        )
        for piece in range(parts):
            mixed[at, :] = mixed[at, :] + product(me, g, piece)

    def take_value(j, g, piece):
        at = slice(g * stack, (g + 1) * stack)
        block_copy(other_shift(j), g, 1 + piece).wait_recv()
        return mixed[at, :] + product(other(j), g, piece)

    def take_values(j, g, count):
        at = slice(g * stack, (g + 1) * stack)
        for piece in range(count):
            mixed[at, :] = take_value(j, g, piece)

    def out_copy(g):
        cols = slice(g * stack, (g + 1) * stack)
        return pltpu.make_async_copy(out.at[:, cols], out_hbm.at[0, :, cols], out_sem.at[g])

    def drain(k):
        strip_copy(k).wait_send()
        for d in range(1, peers):
            spread_copy(k, d).wait_send()
        for g in range(kv_heads):
            block_copy(k, g, 0).wait_send()

    each(slots, drain, 1)
    each(steps, drain_sums)

    early = slots - 3
    for j in range(early):
        for g in range(kv_heads):
            take_values(j, g, parts)
    for g in range(kv_heads):
        for j in range(early, slots - 2):
            take_values(j, g, parts)
        take_values(slots - 2, g, parts - 1)
        at = slice(g * stack, (g + 1) * stack)
        block_copy(other_shift(slots - 2), g, parts).wait_recv()
        last = product(other(slots - 2), g, parts - 1)
        for h in range(sharing):
            at = slice((g * sharing + h) * rows, (g * sharing + h + 1) * rows)
            done = (mixed[at, :] + last[h * rows : (h + 1) * rows]) * totals[at, :]
            out[:, (g * sharing + h) * HD : (g * sharing + h + 1) * HD] = done.astype(out.dtype)
        out_copy(g).start()

    def drain_values(k):
        for g in range(kv_heads):
            for piece in range(parts):
                block_copy(k, g, 1 + piece).wait_send()

    each(slots, drain_values, 1)
    for g in range(kv_heads):
        out_copy(g).wait()


def per_device(hidden, query_weight, keyvalue_weight, block_store, block_ids, offsets, served):
    slots = lax.axis_size("store")
    peers = lax.axis_size("mp")
    rows, model = hidden.shape[1:]
    share, kv_cols = block_store.shape[1:]
    q_cols = query_weight.shape[1]
    heads = q_cols // HD
    kv_heads = kv_cols // (2 * HD)
    chunks = q_cols // kv_cols + 1
    depth = model // slots
    past = NCH * L
    span = 512
    staged = (2 * rows, span) == (share, kv_cols) and block_store.shape[0] <= heads // 2 * past // span
    starts = (np.arange(NCH)[:, None] * L + np.arange(GAP)[None, :]).reshape(-1)
    tables = np.stack(
        signed_tables(np.concatenate([np.arange(L), starts, past + GAP + np.arange(rows)]))
    )
    hbm = pl.BlockSpec(memory_space=pl.ANY)
    dma = pltpu.SemaphoreType.DMA
    return pl.pallas_call(
        functools.partial(serve_body, slots, peers, heads, kv_heads),
        out_shape=jax.ShapeDtypeStruct((1, rows, q_cols), jnp.bfloat16),
        in_specs=[hbm] * 8,
        out_specs=hbm,
        scratch_shapes=[
            pltpu.SMEM(block_ids.shape, jnp.int32),
            pltpu.SMEM(served.shape, jnp.int32),
            pltpu.SMEM(offsets.shape, jnp.int32),
            pltpu.VMEM((slots, rows, depth), jnp.bfloat16),
            pltpu.VMEM(query_weight.shape, jnp.bfloat16),
            pltpu.VMEM(keyvalue_weight.shape, jnp.bfloat16),
            pltpu.VMEM((chunks, slots, rows, kv_cols), jnp.float32),
            pltpu.VMEM((slots + 1, chunks, rows + rows // BANDS * PACKED, kv_cols), jnp.int16),
            pltpu.VMEM((slots, 8, HD), jnp.float32),
            pltpu.VMEM((slots + 1, 8, HD), jnp.float32),
            pltpu.VMEM((slots + 1, 8, HD), jnp.float32),
            pltpu.VMEM((slots, 2 * kv_heads, NCH, share, HD), jnp.bfloat16),
            pltpu.VMEM((kv_heads, past + rows, HD), jnp.bfloat16),
            pltpu.VMEM((kv_heads, rows, HD), jnp.bfloat16),
            pltpu.VMEM((heads * rows, HD), jnp.bfloat16),
            pltpu.VMEM((2 * rows, past), jnp.float32),
            pltpu.VMEM((heads // 2, past // span, 2 * rows, span), jnp.bfloat16),
            pltpu.VMEM((heads * rows, rows), jnp.bfloat16),
            None if staged else pltpu.VMEM(block_store.shape, jnp.bfloat16),
            pltpu.VMEM((slots, 2 * kv_heads, NCH, share, HD), jnp.bfloat16),
            pltpu.VMEM((heads * rows, HD), jnp.float32),
            pltpu.VMEM((heads * rows, HD), jnp.float32),
            pltpu.VMEM(tables.shape, jnp.float32),
            pltpu.VMEM((rows, q_cols), jnp.bfloat16),
            dma((3,)),
            dma((3,)),
            dma((1,)),
            dma((heads // 2,)),
            dma((kv_heads,)),
            dma((slots,)),
            dma((slots,)),
            dma((slots, peers)),
            dma((slots, peers)),
            dma((slots, 3 * kv_heads)),
            dma((slots, 3 * kv_heads)),
            dma((slots + 1, chunks)),
            dma((slots + 1, chunks)),
            dma((slots + 1,)),
            dma((slots + 1,)),
        ],
        compiler_params=pltpu.CompilerParams(
            vmem_limit_bytes=63 << 20, collective_id=0, has_side_effects=True
        ),
        name="serve",
    )(block_ids, served, offsets, hidden, query_weight, keyvalue_weight, block_store, tables)


def solution(mesh):
    in_specs = (
        P(("groups", "store"), None, None),
        P("store", "mp"),
        P("store", "mp"),
        P("groups", "store", "mp"),
        P("groups", None),
        P("groups", None),
        P("groups"),
    )
    out_specs = P(("groups", "store"), None, "mp")
    return jax.shard_map(
        per_device, mesh=mesh, in_specs=in_specs, out_specs=out_specs, check_vma=False
    )
```

```python
import functools
import math

import jax
import jax.numpy as jnp
import numpy as np
from jax import lax
from jax.experimental import pallas as pl
from jax.experimental.pallas import tpu as pltpu
from jax.sharding import PartitionSpec as P

HD = 128
HALF = HD // 2
NCH = 4
L = 1024
GAP = 64
BASE = 500000.0


def periods():
    inverse = np.exp(
        np.arange(HALF, dtype=np.float32) * np.float32(-2.0 * math.log(BASE) / HD)
    ).astype(np.float32)
    return np.floor(np.float32(2.0 * math.pi) / inverse + np.float32(0.5)).astype(np.float64)


def signed_tables(positions):
    period = periods()[None, :]
    angles = np.mod(np.asarray(positions, np.float64)[:, None], period) / period * (2.0 * math.pi)
    cos, sin = np.cos(angles), np.sin(angles)
    return (
        np.concatenate([cos, cos], axis=1).astype(np.float32),
        np.concatenate([-sin, sin], axis=1).astype(np.float32),
    )


def turn(x, cos, sin):
    return x * cos + pltpu.roll(x, HALF, 1) * sin


MESH = pl.DeviceIdType.MESH
STEPS = 2097000.0
LEAST = 1e-30
LOW = 6
BANDS = 8
PACKED = 3


def pack(low):
    words = (
        low[0] | (low[1] << 6) | ((low[2] & 15) << 12),
        (low[2] >> 4) | (low[3] << 2) | (low[4] << 8) | ((low[5] & 3) << 14),
        (low[5] >> 2) | (low[6] << 4) | (low[7] << 10),
    )
    return [(word - 32768).astype(jnp.int16) for word in words]


def unpack(words):
    a, b, c = [word.astype(jnp.int32) + 32768 for word in words]
    return (
        a & 63, (a >> 6) & 63, (a >> 12) | ((b & 3) << 4), (b >> 2) & 63,
        (b >> 8) & 63, (b >> 14) | ((c & 15) << 2), (c >> 4) & 63, c >> 10,
    )


def serve_body(
    slots, peers, heads, kv_heads,
    ids_hbm, served_hbm, offsets_hbm, hidden_ref, wq_hbm, wkv_hbm, store_hbm, tables_hbm,
    out_hbm,
    ids_ref, served_ref, offsets_ref, tokens, wq, wkv, sums, codes, own, bounds_in, bounds_out, blocks, keys, fresh, queries, scores, weights, own_weights, stored, sending, totals, mixed, tables, out,
    small_sem, load_sem, own_sem, store_sem, out_sem, a_send, a_recv, b_send, b_recv, k_send, k_recv, p_send, p_recv, s_send, s_recv,
):
    me = lax.axis_index("store")
    part = lax.axis_index("mp")
    rows = hidden_ref.shape[1]
    depth = tokens.shape[2]
    chunks, _, _, width = sums.shape
    share = blocks.shape[2]
    sharing = heads // kv_heads
    past = NCH * L
    span = weights.shape[3]
    parts = 2 if NCH // 2 * share % span == 0 else 1
    some = NCH // parts
    strip = rows // peers

    barrier = pltpu.get_barrier_semaphore()
    for k in range(1, slots):
        pl.semaphore_signal(
            barrier, inc=1, device_id={"store": lax.rem(me + k, slots)}, device_id_type=MESH
        )
    for k in range(1, peers):
        pl.semaphore_signal(
            barrier, inc=1, device_id={"mp": lax.rem(part + k, peers)}, device_id_type=MESH
        )
    def each(count, body, first=0):
        def step(i, carry):
            body(i)
            return carry

        lax.fori_loop(first, count, step, 0)

    small = [
        pltpu.make_async_copy(source, target, small_sem.at[i])
        for i, (source, target) in enumerate(
            ((ids_hbm, ids_ref), (served_hbm, served_ref), (offsets_hbm, offsets_ref))
        )
    ]
    for load in small:
        load.start()

    if stored is None:
        several = weights.shape[1]
        store_loads = [
            pltpu.make_async_copy(
                store_hbm.at[pl.ds(i * several, several)], weights.at[i], store_sem.at[i]
            )
            for i in range(store_hbm.shape[0] // several)
        ]
    else:
        store_loads = [pltpu.make_async_copy(store_hbm, stored, store_sem.at[0])]
    for load in store_loads:
        load.start()

    def pick(s, target):
        request = served_ref[s]

        def one(c):
            block = ids_ref[request, c]
            if stored is None:
                target[s, c] = weights[block // several, block % several]
            else:
                target[s, c] = stored[block]

        each(NCH, one)

    loads = [
        pltpu.make_async_copy(wq_hbm, wq, load_sem.at[0]),
        pltpu.make_async_copy(wkv_hbm, wkv, load_sem.at[1]),
        pltpu.make_async_copy(
            hidden_ref.at[0, :, pl.ds(pl.multiple_of(me * depth, depth), depth)],
            tokens.at[me], load_sem.at[2],
        ),
    ]
    tables_copy = pltpu.make_async_copy(tables_hbm, tables, own_sem.at[0])
    pl.semaphore_wait(barrier, slots + peers - 2)

    def strip_copy(k):
        to = lax.rem(me + k, slots)
        mine = pl.ds(pl.multiple_of(part * strip, strip), strip)
        return pltpu.make_async_remote_copy(
            src_ref=hidden_ref.at[0, mine, pl.ds(pl.multiple_of(to * depth, depth), depth)],
            dst_ref=tokens.at[me, mine, :],
            send_sem=a_send.at[k],
            recv_sem=a_recv.at[k],
            device_id={"store": to},
            device_id_type=MESH,
        )

    def spread_copy(k, d):
        source = lax.rem(me - k + slots, slots)
        mine = pl.ds(pl.multiple_of(part * strip, strip), strip)
        return pltpu.make_async_remote_copy(
            src_ref=tokens.at[source, mine, :],
            dst_ref=tokens.at[source, mine, :],
            send_sem=b_send.at[k, d],
            recv_sem=b_recv.at[k, d],
            device_id={"mp": lax.rem(part + d, peers)},
            device_id_type=MESH,
        )

    def block_copy(k, g, piece):
        to = lax.rem(me + k, slots)
        cols = pl.ds(pl.multiple_of((2 * g + min(piece, 1)) * HD, HD), HD)
        chosen = slice(0, NCH) if piece == 0 else slice((piece - 1) * some, piece * some)
        return pltpu.make_async_remote_copy(
            src_ref=sending.at[to, chosen, :, cols],
            dst_ref=blocks.at[me, chosen, :, cols],
            send_sem=k_send.at[k, (1 + parts) * g + piece],
            recv_sem=k_recv.at[k, (1 + parts) * g + piece],
            device_id={"store": to},
            device_id_type=MESH,
        )

    low = me < slots // 2

    mirrored = jnp.where(low, me, slots - 1 - me)

    def other(j):
        far = jnp.where(mirrored == 0, 0, slots - 2 - mirrored)
        source = jnp.where(
            j < far, slots - 1 - j, jnp.where(j < far + mirrored, j - far, mirrored + 1 + jnp.where(mirrored == 0, j, 0))
        )
        return jnp.where(low, source, slots - 1 - source)

    def other_shift(j):
        return lax.rem(me - other(j) + slots, slots)

    def send_values(up):
        def one(j):
            d = slots - 1 - j
            fits = (me + d < slots) if up else (me >= d)

            @pl.when(fits)
            def _():
                for g in range(kv_heads):
                    for piece in range(parts):
                        block_copy(d if up else slots - d, g, 1 + piece).start()

        each(slots - 1, one)

    def sum_copy(s, q, up):
        index = s + 1 if up else s
        return pltpu.make_async_remote_copy(
            src_ref=codes.at[index, q],
            dst_ref=codes.at[index, q],
            send_sem=p_send.at[index, q],
            recv_sem=p_recv.at[index, q],
            device_id={"store": lax.rem(me + 1, slots) if up else lax.rem(me + slots - 1, slots)},
            device_id_type=MESH,
        )

    def bound_copy(s, up):
        index = s + 1 if up else s
        return pltpu.make_async_remote_copy(
            src_ref=bounds_out.at[index],
            dst_ref=bounds_in.at[index],
            send_sem=s_send.at[index],
            recv_sem=s_recv.at[index],
            device_id={"store": lax.rem(me + 1, slots) if up else lax.rem(me + slots - 1, slots)},
            device_id_type=MESH,
        )

    tall = rows // BANDS
    bands = [slice(i * tall, (i + 1) * tall) for i in range(BANDS)]
    extra = [slice(rows + i * tall, rows + (i + 1) * tall) for i in range(PACKED)]

    def columns_of(i):
        return pl.ds(pl.multiple_of(i * HD, HD), HD)

    def add_codes(q, s, index):
        step = bounds_in[index, pl.ds(q, 1), :] * (1.0 / STEPS)

        def some_columns(i):
            at = columns_of(i)
            low = unpack([codes[index, q, band, at] for band in extra])
            for band, part in zip(bands, low):
                value = (codes[index, q, band, at].astype(jnp.int32) << LOW) | part
                sums[q, s, band, at] = sums[q, s, band, at] + value.astype(jnp.float32) * step

        each(width // HD, some_columns)

    def make_codes(q, s, index):
        factor = STEPS / bounds_out[index, pl.ds(q, 1), :]

        def some_columns(i):
            at = columns_of(i)
            low = []
            for band in bands:
                value = jnp.round(sums[q, s, band, at] * factor).astype(jnp.int32)
                codes[index, q, band, at] = (value >> LOW).astype(jnp.int16)
                low.append(value & 63)
            for band, word in zip(extra, pack(low)):
                codes[index, q, band, at] = word

        each(width // HD, some_columns)

    def forward(q, s, up, begins):
        index = s + 1 if up else s

        @pl.when(q == 0)
        def _():
            @pl.when(begins)
            def _():
                bounds_out[index] = own[s]

            @pl.when(jnp.logical_not(begins))
            def _():
                bound_copy(s, up).wait_recv()
                bounds_out[index] = own[s] + bounds_in[index]

            bound_copy(s, up).start()

        @pl.when(jnp.logical_not(begins))
        def _():
            sum_copy(s, q, up).wait_recv()
            add_codes(q, s, index)

        make_codes(q, s, index)
        sum_copy(s, q, up).start()

    each(slots, lambda k: strip_copy(k).start(), 1)
    for load in loads:
        load.start()
    tables_copy.start()
    for load in small + store_loads:
        load.wait()

    def send_keys(j):
        d = slots - 1 - j
        for up in (True, False):
            to = me + d if up else me - d

            @pl.when((to < slots) if up else (to >= 0))
            def _():
                pick(to, sending)
                for g in range(kv_heads):
                    block_copy(d if up else slots - d, g, 0).start()

    each(slots - 1, send_keys)
    pick(me, blocks)

    @pl.when(low)
    def _():
        send_values(False)

    @pl.when(jnp.logical_not(low))
    def _():
        send_values(True)


    def spread(k):
        strip_copy(k).wait_recv()
        for d in range(1, peers):
            spread_copy(k, d).start()

    each(slots, spread, 1)

    def spread_wait(k):
        for d in range(1, peers):
            spread_copy(k, d).wait_recv()

    each(slots, spread_wait, 1)
    for load in loads:
        load.wait()

    group = 4 if slots % 4 == 0 else 1

    def project(q, panel):
        def some_slots(i):
            t = tokens[pl.ds(i * group, group)].reshape(group * rows, depth)
            sums[q, pl.ds(i * group, group)] = jnp.dot(
                t, panel, preferred_element_type=jnp.float32
            ).reshape(group, rows, width)

        each(slots // group, some_slots)

    def relay_up(k, q):
        @pl.when(slots - 1 - k > me)
        def _():
            forward(q, slots - 1 - k, True, me == 0)

    def relay_down(k, q):
        @pl.when(k < me)
        def _():
            forward(q, k, False, me == slots - 1)

    for q in range(chunks):
        if q < chunks - 1:
            project(q, wq[:, q * width : (q + 1) * width])
        else:
            project(q, wkv[...])

    def measure(s):
        own[s] = jnp.zeros(own.shape[1:], jnp.float32)
        for q in range(chunks):
            largest = jnp.maximum(jnp.max(jnp.abs(sums[q, s]), keepdims=True), LEAST)
            own[s, q : q + 1, :] = jnp.broadcast_to(largest, (1, HD))

    each(slots, measure)

    steps = (slots - 1) * chunks

    def relay(i):
        def at(i, move):
            @pl.when((i >= 0) & (i < steps))
            def _():
                move(i // chunks, i % chunks)

        @pl.when(low)
        def _():
            at(i, relay_up)
            at(i - chunks, relay_down)

        @pl.when(jnp.logical_not(low))
        def _():
            at(i, relay_down)
            at(i - chunks, relay_up)

    each(steps + chunks, relay)

    @pl.when(low)
    def _():
        send_values(True)

    @pl.when(jnp.logical_not(low))
    def _():
        send_values(False)

    def drain_sums(i):
        k, q = i // chunks, i % chunks

        @pl.when(slots - 1 - k > me)
        def _():
            sum_copy(slots - 1 - k, q, True).wait_send()

            @pl.when(q == 0)
            def _():
                bound_copy(slots - 1 - k, True).wait_send()

        @pl.when(k < me)
        def _():
            sum_copy(k, q, False).wait_send()

            @pl.when(q == 0)
            def _():
                bound_copy(k, False).wait_send()

    def rotate_share(source):
        at_t = pl.multiple_of(source * share, share)
        tc, ts = tables[0, pl.ds(at_t, share), :], tables[1, pl.ds(at_t, share), :]

        def one(c):
            at_k = pl.multiple_of((source * NCH + c) * share, share)
            jitter = jnp.clip(offsets_ref[served_ref[me], c] - c * L, 0, GAP - 1)
            start = L + c * GAP + jitter
            oc, os = tables[0, pl.ds(start, 1), :], tables[1, pl.ds(start, 1), :]
            cos = tc * oc - ts * os
            sin = ts * oc + tc * os
            for g in range(kv_heads):
                at = g * 2 * HD
                x = blocks[source, c, :, at : at + HD].astype(jnp.float32)
                keys[g, pl.ds(at_k, share), :] = turn(x, cos, sin).astype(jnp.bfloat16)

        each(NCH, one)

    tables_copy.wait()
    rotate_share(me)

    def take(j):
        for g in range(kv_heads):
            block_copy(other_shift(j), g, 0).wait_recv()
        rotate_share(other(j))

    each(slots - 1, take)

    @pl.when(me > 0)
    def _():
        bound_copy(me, True).wait_recv()

    @pl.when(me < slots - 1)
    def _():
        bound_copy(me, False).wait_recv()

    def settle(q):
        @pl.when(me > 0)
        def _():
            sum_copy(me, q, True).wait_recv()
            add_codes(q, me, me + 1)

        @pl.when(me < slots - 1)
        def _():
            sum_copy(me, q, False).wait_recv()
            add_codes(q, me, me)

    each(chunks, settle)

    at_q = L + NCH * GAP
    qc, qs = tables[0, at_q : at_q + rows, :], tables[1, at_q : at_q + rows, :]
    for g in range(kv_heads):
        at = g * 2 * HD
        keys[g, past:, :] = turn(sums[chunks - 1, me, :, at : at + HD], qc, qs).astype(jnp.bfloat16)
        fresh[g] = sums[chunks - 1, me, :, at + HD : at + 2 * HD].astype(jnp.bfloat16)
    for h in range(heads):
        q, at = divmod(h * HD, width)
        queries[h * rows : (h + 1) * rows, :] = turn(
            sums[q, me, :, at : at + HD], qc, qs
        ).astype(jnp.bfloat16)

    block = 2 * rows
    factor = math.log2(math.e) / math.sqrt(HD)
    lower = lax.broadcasted_iota(jnp.int32, (block, rows), 0) % rows >= lax.broadcasted_iota(
        jnp.int32, (block, rows), 1
    )
    contract = (((1,), (1,)), ((), ()))

    def weigh(b):
        g = (b * 2) // sharing
        at = pl.ds(pl.multiple_of(b * block, block), block)
        q = queries[at, :]
        own = lax.dot_general(q, keys[g, past:, :], contract, preferred_element_type=jnp.float32)
        own = jnp.where(lower, own, -jnp.inf)
        top = own
        for j in range(past // span):
            s = lax.dot_general(
                q, keys[g, j * span : (j + 1) * span, :], contract,
                preferred_element_type=jnp.float32,
            )
            scores[:, j * span : (j + 1) * span] = s
            for k in range(span // HD):
                top = jnp.maximum(top, s[:, k * HD : (k + 1) * HD])
        top = jnp.max(top, axis=1, keepdims=True)
        w = jnp.exp2((own - top) * factor)
        total = w
        own_weights[at, :] = w.astype(jnp.bfloat16)
        for j in range(past // span):
            w = jnp.exp2((scores[:, j * span : (j + 1) * span] - top) * factor)
            for k in range(span // HD):
                total = total + w[:, k * HD : (k + 1) * HD]
            weights[b, j] = w.astype(jnp.bfloat16)
        totals[at, :] = total

    each(heads // 2, weigh)

    stack = sharing * rows

    def invert(h):
        at = pl.ds(pl.multiple_of(h * rows, rows), rows)
        totals[at, :] = jnp.broadcast_to(
            1.0 / jnp.sum(totals[at, :], axis=1, keepdims=True), (rows, HD)
        )

    each(heads, invert)

    pairs = sharing // 2

    pairs = sharing // 2
    keys_each = some * share
    size = min(keys_each, span)

    def product(source, g, piece):
        v = blocks[
            source, piece * some : (piece + 1) * some, :, (2 * g + 1) * HD : (2 * g + 2) * HD
        ].reshape(keys_each, HD)
        mine = slice(g * pairs, (g + 1) * pairs)
        total = None
        for i in range(keys_each // size):
            start = (source * parts + piece) * keys_each + i * size
            at = pl.ds(pl.multiple_of(lax.rem(start, span), size), size)
            w = weights[mine, start // span] if size == span else weights[mine, start // span, :, at]
            w = w.reshape(stack, size)
            term = jnp.dot(w, v[i * size : (i + 1) * size], preferred_element_type=jnp.float32)
            total = term if total is None else total + term
        return total

    for g in range(kv_heads):
        at = slice(g * stack, (g + 1) * stack)
        mixed[at, :] = jnp.dot(
            own_weights[at, :], fresh[g], preferred_element_type=jnp.float32
        )
        for piece in range(parts):
            mixed[at, :] = mixed[at, :] + product(me, g, piece)

    def take_value(j, g, piece):
        at = slice(g * stack, (g + 1) * stack)
        block_copy(other_shift(j), g, 1 + piece).wait_recv()
        return mixed[at, :] + product(other(j), g, piece)

    def take_values(j, g, count):
        at = slice(g * stack, (g + 1) * stack)
        for piece in range(count):
            mixed[at, :] = take_value(j, g, piece)

    def out_copy(g):
        cols = slice(g * stack, (g + 1) * stack)
        return pltpu.make_async_copy(out.at[:, cols], out_hbm.at[0, :, cols], out_sem.at[g])

    def drain(k):
        strip_copy(k).wait_send()
        for d in range(1, peers):
            spread_copy(k, d).wait_send()
        for g in range(kv_heads):
            block_copy(k, g, 0).wait_send()

    each(slots, drain, 1)
    each(steps, drain_sums)

    early = slots - 3
    for j in range(early):
        for g in range(kv_heads):
            take_values(j, g, parts)
    for g in range(kv_heads):
        for j in range(early, slots - 2):
            take_values(j, g, parts)
        take_values(slots - 2, g, parts - 1)
        at = slice(g * stack, (g + 1) * stack)
        done = take_value(slots - 2, g, parts - 1) * totals[at, :]
        for h in range(sharing):
            first = (g * sharing + h) * HD
            out[:, first : first + HD] = done[h * rows : (h + 1) * rows].astype(out.dtype)
        out_copy(g).start()

    def drain_values(k):
        for g in range(kv_heads):
            for piece in range(parts):
                block_copy(k, g, 1 + piece).wait_send()

    each(slots, drain_values, 1)
    for g in range(kv_heads):
        out_copy(g).wait()


def per_device(hidden, query_weight, keyvalue_weight, block_store, block_ids, offsets, served):
    slots = lax.axis_size("store")
    peers = lax.axis_size("mp")
    rows, model = hidden.shape[1:]
    share, kv_cols = block_store.shape[1:]
    q_cols = query_weight.shape[1]
    heads = q_cols // HD
    kv_heads = kv_cols // (2 * HD)
    chunks = q_cols // kv_cols + 1
    depth = model // slots
    past = NCH * L
    span = 512
    staged = (2 * rows, span) == (share, kv_cols) and block_store.shape[0] <= heads // 2 * past // span
    starts = (np.arange(NCH)[:, None] * L + np.arange(GAP)[None, :]).reshape(-1)
    tables = np.stack(
        signed_tables(np.concatenate([np.arange(L), starts, past + GAP + np.arange(rows)]))
    )
    hbm = pl.BlockSpec(memory_space=pl.ANY)
    dma = pltpu.SemaphoreType.DMA
    return pl.pallas_call(
        functools.partial(serve_body, slots, peers, heads, kv_heads),
        out_shape=jax.ShapeDtypeStruct((1, rows, q_cols), jnp.bfloat16),
        in_specs=[hbm] * 8,
        out_specs=hbm,
        scratch_shapes=[
            pltpu.SMEM(block_ids.shape, jnp.int32),
            pltpu.SMEM(served.shape, jnp.int32),
            pltpu.SMEM(offsets.shape, jnp.int32),
            pltpu.VMEM((slots, rows, depth), jnp.bfloat16),
            pltpu.VMEM(query_weight.shape, jnp.bfloat16),
            pltpu.VMEM(keyvalue_weight.shape, jnp.bfloat16),
            pltpu.VMEM((chunks, slots, rows, kv_cols), jnp.float32),
            pltpu.VMEM((slots + 1, chunks, rows + rows // BANDS * PACKED, kv_cols), jnp.int16),
            pltpu.VMEM((slots, 8, HD), jnp.float32),
            pltpu.VMEM((slots + 1, 8, HD), jnp.float32),
            pltpu.VMEM((slots + 1, 8, HD), jnp.float32),
            pltpu.VMEM((slots, NCH, share, kv_cols), jnp.bfloat16),
            pltpu.VMEM((kv_heads, past + rows, HD), jnp.bfloat16),
            pltpu.VMEM((kv_heads, rows, HD), jnp.bfloat16),
            pltpu.VMEM((heads * rows, HD), jnp.bfloat16),
            pltpu.VMEM((2 * rows, past), jnp.float32),
            pltpu.VMEM((heads // 2, past // span, 2 * rows, span), jnp.bfloat16),
            pltpu.VMEM((heads * rows, rows), jnp.bfloat16),
            None if staged else pltpu.VMEM(block_store.shape, jnp.bfloat16),
            pltpu.VMEM((slots, NCH, share, kv_cols), jnp.bfloat16),
            pltpu.VMEM((heads * rows, HD), jnp.float32),
            pltpu.VMEM((heads * rows, HD), jnp.float32),
            pltpu.VMEM(tables.shape, jnp.float32),
            pltpu.VMEM((rows, q_cols), jnp.bfloat16),
            dma((3,)),
            dma((3,)),
            dma((1,)),
            dma((heads // 2,)),
            dma((kv_heads,)),
            dma((slots,)),
            dma((slots,)),
            dma((slots, peers)),
            dma((slots, peers)),
            dma((slots, 3 * kv_heads)),
            dma((slots, 3 * kv_heads)),
            dma((slots + 1, chunks)),
            dma((slots + 1, chunks)),
            dma((slots + 1,)),
            dma((slots + 1,)),
        ],
        compiler_params=pltpu.CompilerParams(
            vmem_limit_bytes=63 << 20, collective_id=0, has_side_effects=True
        ),
        name="serve",
    )(block_ids, served, offsets, hidden, query_weight, keyvalue_weight, block_store, tables)


def solution(mesh):
    in_specs = (
        P(("groups", "store"), None, None),
        P("store", "mp"),
        P("store", "mp"),
        P("groups", "store", "mp"),
        P("groups", None),
        P("groups", None),
        P("groups"),
    )
    out_specs = P(("groups", "store"), None, "mp")
    return jax.shard_map(
        per_device, mesh=mesh, in_specs=in_specs, out_specs=out_specs, check_vma=False
    )
```
